32 devices in a mesh: gx: 4 (over z), gy: 8 (over y, x, core).
Axes of the slice: x: 2, y: 2, z: 4, core: 2. Of those that a mesh axis runs over, the one named last changes fastest.
Arguments:
- offsets: float32 [2, 16, 32, 256], P(None, 'gx', 'gy'), may hold values from 0 to 1
- probes: float32 [16, 16, 32, 256], P(None, 'gx', 'gy'), may hold values from -6 to 6
- counts: int32 [16, 32], P('gx', 'gy'), may hold values from 1 to 256, as said below
Outputs:
- kernel_product: float32 [16, 16, 32, 256], P(None, 'gx', 'gy')
The draws below stay inside these ranges and needn't reach their ends.
Inputs may be any that keep to these rules, and one draw needn't show every extreme that they name: `counts`: each draw has a leaf with all 256 slots used and a leaf with one slot used.
All inputs are finite; a program needn't handle non-finite values.
Results may differ from the reference program's by a relative error of at most 0.0001.
Values sent between devices are 32-bit elements; how exact they have to be, the bound alone decides.
A program may use at most 64 MiB of HBM per device.

```python
import jax
import jax.numpy as jnp
from jax import lax

ORDER = 8
LEAF = 256
PROBES = 16
DEPTH = 2
NXL = 16
NYL = 32


def draw_counts(key, part):
    key_level, key_full, key_single = jax.random.split(key, 3)
    spread = jax.random.randint(key_level, (NXL, NYL), 0, LEAF)
    counts = LEAF - spread * spread // LEAF
    cells = jnp.arange(NXL * NYL, dtype=jnp.int32).reshape(NXL, NYL)
    full_cell = jax.random.randint(key_full, (), 0, NXL * NYL)
    single_cell = (full_cell + 1 + jax.random.randint(key_single, (), 0, NXL * NYL - 1)) % (NXL * NYL)
    counts = jnp.where(cells == full_cell, LEAF, counts)
    counts = jnp.where(cells == single_cell, 1, counts)
    return counts.astype(jnp.int32)


def shard_levels(own_key, shape, cuts, smallest, largest):
    factor_of = 1.0
    for dim, shards_of in cuts:
        steps = jax.random.uniform(jax.random.fold_in(jax.random.fold_in(own_key, 6), dim), (shards_of,), jnp.float32, smallest / len(cuts), largest / len(cuts))
        factor_of = factor_of * jnp.repeat(jnp.exp(steps), shape[dim] // shards_of).reshape((-1,) + (1,) * (len(shape) - 1 - dim))
    return factor_of


def bell_draw(key, shape, scale, limit, shards=(), held_as=jnp.bfloat16):
    factor_of = shard_levels(key, shape, shards, -0.22, 0.18) if shards else 1.0
    entries = jax.random.normal(key, shape, jnp.float32) * scale * factor_of
    return jnp.minimum(jnp.maximum(entries, -limit), limit).astype(held_as)


def setup_inputs(seed: int = 0) -> dict:
    streams_of = jax.random.split(jax.random.key(seed), 4)
    offsets = jnp.clip(1.0 * jax.random.uniform(streams_of[0], (2, NXL, NYL, LEAF), jnp.float32) ** shard_levels(streams_of[0], (2, NXL, NYL, LEAF), ((1, 4), (2, 8)), -0.2, 0.2), 0.0, 1.0)
    probes = bell_draw(streams_of[1], (PROBES, NXL, NYL, LEAF), 1.0, 6.0, ((1, 4), (2, 8)), jnp.float32)
    counts = draw_counts(jax.random.fold_in(streams_of[3], 71), 0)
    return dict(offsets=offsets, probes=probes, counts=counts)


ROOT_THREE = 1.7320508075688772
LENGTH_SCALE = 6.0
AMPLITUDE = 1.0 / 96.0
SHORT_LENGTH = 0.5
SHORT_AMPLITUDE = 1.0 / 16.0
NUGGET = 0.5

def matern(dist_sq):
    distance = jnp.sqrt(dist_sq)
    scaled = ROOT_THREE * distance / LENGTH_SCALE
    short_scaled = ROOT_THREE * distance / SHORT_LENGTH
    long_part = AMPLITUDE * (1.0 + scaled) * jnp.exp(-scaled)
    return long_part + SHORT_AMPLITUDE * (1.0 + short_scaled) * jnp.exp(-short_scaled)

def cheb_nodes(degree):
    node_slots = jnp.arange(degree, dtype=jnp.float32)
    return jnp.cos((2.0 * node_slots + 1.0) * (jnp.pi / (2.0 * degree)))

def cheb_weights(coords, degree):
    powers = jnp.arange(1, degree, dtype=jnp.float32)
    node_slots = jnp.arange(degree, dtype=jnp.float32)
    angles = jnp.arccos(jnp.clip(coords, -1.0, 1.0))
    series = jnp.cos(angles[..., None] * powers)
    at_nodes = jnp.cos(powers[:, None] * (2.0 * node_slots[None, :] + 1.0) * (jnp.pi / (2.0 * degree)))
    return 1.0 / degree + 2.0 / degree * jnp.einsum('...k,km->...m', series, at_nodes, precision=lax.Precision.HIGHEST)

def leaf_weights(offsets, degree):
    along_x = cheb_weights(2.0 * offsets[0] - 1.0, degree)
    along_y = cheb_weights(2.0 * offsets[1] - 1.0, degree)
    product = along_x[..., :, None] * along_y[..., None, :]
    return product.reshape(offsets.shape[1:] + (degree * degree,))

def child_maps(degree):
    node_values = cheb_nodes(degree)
    result = []
    for child_x in range(2):
        for child_y in range(2):
            weight_x = cheb_weights((node_values - 1.0) / 2.0 + child_x, degree)
            weight_y = cheb_weights((node_values - 1.0) / 2.0 + child_y, degree)
            result.append((weight_x[:, None, :, None] * weight_y[None, :, None, :]).reshape(degree * degree, degree * degree))
    return jnp.stack(result).reshape(2, 2, degree * degree, degree * degree)

def upward(children, maps_table):
    half_x = children.shape[0] // 2
    half_y = children.shape[1] // 2
    grouped = children.reshape((half_x, 2, half_y, 2) + children.shape[2:])
    return jnp.einsum('xyrq,ixjypr->ijpq', maps_table, grouped, precision=lax.Precision.HIGHEST)

def downward(parents, maps_table):
    spread = jnp.einsum('xyrq,ijpq->ixjypr', maps_table, parents, precision=lax.Precision.HIGHEST)
    return spread.reshape((2 * parents.shape[0], 2 * parents.shape[1]) + parents.shape[2:])

def transfer_kernel(shift_x, shift_y, box_side, degree):
    node_values = cheb_nodes(degree) * (box_side / 2.0)
    node_x = jnp.repeat(node_values, degree)
    node_y = jnp.tile(node_values, degree)
    delta_x = node_x[:, None] - node_x[None, :] - jnp.asarray(shift_x)[..., None, None] * box_side
    delta_y = node_y[:, None] - node_y[None, :] - jnp.asarray(shift_y)[..., None, None] * box_side
    return matern(delta_x * delta_x + delta_y * delta_y)

def interact(window, count_x, count_y, base_x, base_y, box_side, degree):
    cells_x = base_x + jnp.arange(count_x, dtype=jnp.int32)
    cells_y = base_y + jnp.arange(count_y, dtype=jnp.int32)
    accumulated = jnp.zeros((count_x, count_y) + window.shape[2:], jnp.float32)
    for a in range(-3, 4):
        for b in range(-3, 4):
            if max(abs(a), abs(b)) < 2:
                continue
            within_x = jnp.abs((cells_x + a) // 2 - cells_x // 2) <= 1
            within_y = jnp.abs((cells_y + b) // 2 - cells_y // 2) <= 1
            allowed = (within_x[:, None] & within_y[None, :]).astype(jnp.float32)
            matrix = transfer_kernel(jnp.float32(a), jnp.float32(b), box_side, degree)
            source = window[3 + a:3 + a + count_x, 3 + b:3 + b + count_y]
            accumulated = accumulated + allowed[:, :, None, None] * jnp.einsum('qr,ijpr->ijpq', matrix, source, precision=lax.Precision.HIGHEST)
    return accumulated

def interact_top(box_grid, own_x, own_y, box_side, degree):
    shift_x = (jnp.arange(box_grid.shape[0], dtype=jnp.int32) - own_x).astype(jnp.float32)
    shift_y = (jnp.arange(box_grid.shape[1], dtype=jnp.int32) - own_y).astype(jnp.float32)
    spread_x = shift_x[:, None] + 0.0 * shift_y[None, :]
    spread_y = 0.0 * shift_x[:, None] + shift_y[None, :]
    matrices = transfer_kernel(spread_x, spread_y, box_side, degree)
    separated = (jnp.maximum(jnp.abs(spread_x), jnp.abs(spread_y)) >= 2.0).astype(jnp.float32)
    return jnp.einsum('abqr,abpr->pq', matrices * separated[:, :, None, None], box_grid, precision=lax.Precision.HIGHEST)

def near_row(window, targets):
    width = targets.shape[1]
    accumulated = jnp.zeros((window.shape[0] - 2, width, targets.shape[2]), jnp.float32)
    for a in range(3):
        for b in range(3):
            source = window[:, a, b:b + width]
            delta_x = targets[0][:, :, None] - source[0][:, None, :] - (a - 1.0)
            delta_y = targets[1][:, :, None] - source[1][:, None, :] - (b - 1.0)
            kernel_tile = matern(delta_x * delta_x + delta_y * delta_y)
            accumulated = accumulated + jnp.einsum('jst,pjt->pjs', kernel_tile, source[2:], precision=lax.Precision.HIGHEST)
    return accumulated

def near_field(padded, offsets):

    def one_row(row_index):
        window = lax.dynamic_slice_in_dim(padded, row_index, 3, 1)
        targets = lax.dynamic_index_in_dim(offsets, row_index, 1, keepdims=False)
        return near_row(window, targets)
    row_terms = lax.map(one_row, jnp.arange(offsets.shape[1], dtype=jnp.int32))
    return jnp.transpose(row_terms, (1, 0, 2, 3))

def reference(offsets, probes, counts):
    degree = ORDER
    in_use = (jnp.arange(LEAF, dtype=jnp.int32)[None, None, :] < counts[:, :, None]).astype(jnp.float32)
    masked = probes * in_use[None]
    stacked = jnp.concatenate([offsets, masked], axis=0)
    padded = jnp.pad(stacked, ((0, 0), (1, 1), (1, 1), (0, 0)))
    near_part = near_field(padded, offsets)
    weights = leaf_weights(offsets, degree)
    maps_table = child_maps(degree)
    levels = [jnp.einsum('ijsq,pijs->ijpq', weights, masked, precision=lax.Precision.HIGHEST)]
    top_level = DEPTH + 2
    for repeat in range(top_level):
        levels.append(upward(levels[-1], maps_table))
    box_grid = levels[top_level]
    grid_rows = []
    for box_x in range(box_grid.shape[0]):
        grid_cols = [interact_top(box_grid, box_x, box_y, 2.0 ** top_level, degree) for box_y in range(box_grid.shape[1])]
        grid_rows.append(jnp.stack(grid_cols))
    local_exp = jnp.stack(grid_rows)
    for level_index in range(top_level - 1, -1, -1):
        source = jnp.pad(levels[level_index], ((3, 3), (3, 3), (0, 0), (0, 0)))
        local_exp = downward(local_exp, maps_table) + interact(source, levels[level_index].shape[0], levels[level_index].shape[1], 0, 0, 2.0 ** level_index, degree)
    far_part = jnp.einsum('ijsq,ijpq->pijs', weights, local_exp, precision=lax.Precision.HIGHEST)
    return in_use[None] * (near_part + far_part + NUGGET * masked)
```

```python
import functools
import math

import jax
import jax.numpy as jnp
import numpy as np
from jax import lax
from jax.experimental import pallas as pl
from jax.experimental.pallas import tpu as pltpu
from jax.sharding import PartitionSpec as P

ORDER = 8
NODES = ORDER * ORDER
ROOT_THREE = 1.7320508075688772
LENGTH_SCALE = 6.0
AMPLITUDE = 1.0 / 96.0
SHORT_AMPLITUDE = 1.0 / 16.0
NUGGET = 0.5
RATIO = 12
UNIT = ROOT_THREE * RATIO / LENGTH_SCALE
FACTOR = AMPLITUDE / RATIO
LOG2_E = 1.4426950408889634
SHORT_SHIFT = math.log2(SHORT_AMPLITUDE / FACTOR)
HIGH = lax.Precision.HIGH
HIGHEST = lax.Precision.HIGHEST
ROWS = 24
UNIT_ROWS = 64
GROUP = 4
GROUP_HALF = 4
SCALE = UNIT * LOG2_E
AUG = 32


def node_table():
    slots = np.arange(ORDER)
    return np.cos((2.0 * slots + 1.0) * (np.pi / (2.0 * ORDER)))


def series_at_nodes():
    powers = np.arange(ORDER)
    slots = np.arange(ORDER)
    table = np.cos(powers[:, None] * (2.0 * slots[None, :] + 1.0) * (np.pi / (2.0 * ORDER)))
    table = table * (2.0 / ORDER)
    table[0] = 1.0 / ORDER
    return table


SERIES = series_at_nodes()


def interpolation(coords):
    angles = np.arccos(np.clip(coords, -1.0, 1.0))
    series = np.cos(angles[:, None] * np.arange(ORDER))
    return series @ series_at_nodes()


def child_maps():
    nodes = node_table()
    result = []
    for child_x in range(2):
        for child_y in range(2):
            weight_x = interpolation((nodes - 1.0) / 2.0 + child_x)
            weight_y = interpolation((nodes - 1.0) / 2.0 + child_y)
            result.append(
                (weight_x[:, None, :, None] * weight_y[None, :, None, :]).reshape(NODES, NODES)
            )
    return np.stack(result).astype(np.float32)


def matern(dist_sq):
    safe = jnp.maximum(dist_sq, 1e-30)
    scaled = safe * lax.rsqrt(safe)
    decay = jnp.exp2(scaled * (-LOG2_E / RATIO))
    short = jnp.exp2(scaled * -LOG2_E + SHORT_SHIFT)
    return decay * (scaled + RATIO) + short * (scaled + 1.0)


def split(value):
    high = value.astype(jnp.bfloat16)
    return high, (value - high.astype(jnp.float32)).astype(jnp.bfloat16)


def dot(a, b):
    return jnp.dot(a, b, preferred_element_type=jnp.float32)


def split_dot(a, b):
    a_high, a_low = split(a)
    b_high, b_low = split(b)
    return dot(a_high, b_high) + dot(a_high, b_low) + dot(a_low, b_high)


def leaf_weights(coords, table_ref):
    axes = []
    for axis in range(2):
        t = 2.0 * coords[axis : axis + 1] - 1.0
        terms = [jnp.ones_like(t), t]
        while len(terms) < ORDER:
            terms.append(2.0 * t * terms[-1] - terms[-2])
        total = table_ref[:, 0:1] * terms[0]
        for n in range(1, ORDER):
            total = total + table_ref[:, n : n + 1] * terms[n]
        axes.append(total)
    return jnp.concatenate([axes[0][m : m + 1] * axes[1] for m in range(ORDER)], axis=0)


def up_kernel(side, count_ref, table_ref, maps_ref, offsets_ref, probes_ref, record_ref, *level_refs):
    slots = offsets_ref.shape[3]
    probes = probes_ref.shape[0]
    lane = lax.broadcasted_iota(jnp.int32, (1, slots), 1)
    for i in range(side):
        for j in range(side):
            count = count_ref[i, j]
            masked = jnp.where(lane < count, probes_ref[:, i, j, :], 0.0)
            coords = offsets_ref[:, i, j, :]
            record_ref[i, j, 0:probes, :] = masked
            record_ref[i, j, probes : probes + 2, :] = coords
            record_ref[i, j, probes + 2 : ROWS, :] = jnp.full(
                (ROWS - probes - 2, slots), count.astype(jnp.float32)
            )
            level_refs[0][i, j] = dot_rows(masked, leaf_weights(coords, table_ref))
    for level in range(1, len(level_refs)):
        boxes = side >> level
        for x in range(boxes):
            for y in range(boxes):
                level_refs[level][x, y] = merged(level_refs[level - 1], x, y, maps_ref)


def dot_rows(a, b):
    return lax.dot_general(
        a, b, (((1,), (1,)), ((), ())), precision=HIGHEST, preferred_element_type=jnp.float32
    )


def merged(children_ref, x, y, maps_ref, pad=0):
    total = None
    for child in range(4):
        term = jnp.dot(
            children_ref[pad + 2 * x + child // 2, pad + 2 * y + child % 2],
            maps_ref[child],
            precision=HIGHEST,
            preferred_element_type=jnp.float32,
        )
        total = term if total is None else total + term
    return total


def exchange_kernel(sizes, *refs):
    size_x, size_y = sizes
    sources, own_ref = refs[0:3], refs[3]
    windows, grid_ref = refs[4:7], refs[7]
    send_sem, recv_sem, line_send, line_recv, own_sem = refs[8:]
    ix = lax.axis_index("gx")
    iy = lax.axis_index("gy")
    steps = [(dx, dy) for dx in (-1, 0, 1) for dy in (-1, 0, 1) if (dx, dy) != (0, 0)]

    def inside(dx, dy):
        x = ix + dx
        y = iy + dy
        return (x >= 0) & (x < size_x) & (y >= 0) & (y < size_y)

    own_copy = pltpu.make_async_copy(own_ref.at[0, 0], grid_ref.at[ix, iy], own_sem)
    own_copy.start()
    for source, window in zip(sources, windows):
        side = source.shape[0]
        width = (window.shape[0] - side) // 2
        window[...] = jnp.zeros_like(window)
        window[width : width + side, width : width + side] = source[...]

    barrier = pltpu.get_barrier_semaphore()

    def greet(x, y):
        pl.semaphore_signal(
            barrier, inc=1, device_id=(x, y), device_id_type=pl.DeviceIdType.MESH
        )

    for k in range(1, size_x):
        greet(lax.rem(ix + k, size_x), iy)
    for k in range(1, size_y):
        greet(ix, lax.rem(iy + k, size_y))
    for dx, dy in steps:
        if dx and dy:
            pl.when(inside(dx, dy))(lambda dx=dx, dy=dy: greet(ix + dx, iy + dy))
    sides_x = jnp.minimum(ix, 1) + jnp.minimum(size_x - 1 - ix, 1)
    sides_y = jnp.minimum(iy, 1) + jnp.minimum(size_y - 1 - iy, 1)
    pl.semaphore_wait(barrier, size_x + size_y - 2 + sides_x * sides_y)

    def line_copy(slot, source, target, x, y):
        return pltpu.make_async_remote_copy(
            src_ref=source,
            dst_ref=target,
            send_sem=line_send.at[slot],
            recv_sem=line_recv.at[slot],
            device_id=(x, y),
            device_id_type=pl.DeviceIdType.MESH,
        )

    along_x = [
        line_copy(k - 1, own_ref.at[0, 0], grid_ref.at[ix, iy], lax.rem(ix + k, size_x), iy)
        for k in range(1, size_x)
    ]
    for copy in along_x:
        copy.start()

    def pieces(step, side, width):
        if step > 0:
            return pl.ds(side - width, width), pl.ds(0, width)
        if step < 0:
            return pl.ds(0, width), pl.ds(side + width, width)
        return pl.ds(0, side), pl.ds(width, side)

    def halo_copy(n, which):
        dx, dy = steps[n]
        source, window = sources[which], windows[which]
        side = source.shape[0]
        width = (window.shape[0] - side) // 2
        from_x, to_x = pieces(dx, side, width)
        from_y, to_y = pieces(dy, side, width)
        return pltpu.make_async_remote_copy(
            src_ref=source.at[from_x, from_y],
            dst_ref=window.at[to_x, to_y],
            send_sem=send_sem.at[which, n],
            recv_sem=recv_sem.at[which, n],
            device_id=(ix + dx, iy + dy),
            device_id_type=pl.DeviceIdType.MESH,
        )

    order = [(which, n) for which in range(3) for n in range(len(steps))]
    for which, n in order:
        pl.when(inside(*steps[n]))(lambda which=which, n=n: halo_copy(n, which).start())
    for copy in along_x:
        copy.wait_recv()
    own_copy.wait()
    along_y = [
        line_copy(
            size_x - 1 + k - 1, grid_ref.at[:, iy], grid_ref.at[:, iy],
            ix, lax.rem(iy + k, size_y),
        )
        for k in range(1, size_y)
    ]
    for copy in along_y:
        copy.start()
    for which, n in order:
        dx, dy = steps[n]
        pl.when(inside(-dx, -dy))(lambda which=which, n=n: halo_copy(n, which).wait_recv())
    for copy in along_y:
        copy.wait_recv()
    for which, n in order:
        pl.when(inside(*steps[n]))(lambda which=which, n=n: halo_copy(n, which).wait_send())
    for copy in along_x + along_y:
        copy.wait_send()


def kernel_of(dist_sq):
    safe = jnp.maximum(dist_sq, 1e-30)
    scaled = safe * lax.rsqrt(safe)
    decay = jnp.exp2(scaled * (-1.0 / RATIO))
    short = jnp.exp2(SHORT_SHIFT - scaled)
    return decay * (scaled + RATIO * LOG2_E) + short * (scaled + LOG2_E)


def three(value):
    first = value.astype(jnp.bfloat16)
    rest = value - first.astype(jnp.float32)
    second = rest.astype(jnp.bfloat16)
    third = (rest - second.astype(jnp.float32)).astype(jnp.bfloat16)
    return [part.astype(jnp.float32) for part in (first, second, third)]


def near_kernel(side, window_ref, local_ref, out_ref, aug_ref, rows_ref, target_ref, first_ref, second_ref,
                 g_ref, high_ref, low_ref, basis_ref, result_ref, count_ref, unit_ref, leaf_ref):
    wide = side + 2
    slots = window_ref.shape[3]
    probes = out_ref.shape[0]
    half = slots // 2
    per_cell = slots // UNIT_ROWS
    per_tile = 128 // UNIT_ROWS
    dummy = wide * wide * per_cell
    lane = lax.broadcasted_iota(jnp.int32, (1, slots), 1)
    lane_tile = lax.broadcasted_iota(jnp.int32, (1, 128), 1)
    middle = wide / 2.0

    for x in range(wide):
        for y in range(wide):
            value = window_ref[x, y, probes + 2 : probes + 3, 0:1].astype(jnp.int32)
            count_ref[x * wide + y] = value[0, 0]

    def chunk_list(leaf, starts):
        i = lax.div(leaf, side)
        j = lax.rem(leaf, side)
        keep = count_ref[(i + 1) * wide + j + 1] > half
        chunk = jnp.where(keep, starts[0], starts[1])
        begin = chunk * per_cell
        n = begin
        for a in range(3):
            for b in range(3):
                cell = (i + a) * wide + j + b
                for u in range(per_cell):
                    unit_ref[n + u] = cell * per_cell + u
                n = n + lax.div(count_ref[cell] + (UNIT_ROWS - 1), UNIT_ROWS)
        for u in range(per_cell):
            unit_ref[n + u] = dummy
        chunks = lax.div(n - begin + per_cell - 1, per_cell)
        for k in range(9):
            leaf_ref[chunk + k] = leaf
        return starts[0] + jnp.where(keep, chunks, 0), starts[1] + jnp.where(keep, 0, chunks)

    def padding(chunk, size):
        for k in range(size):
            for u in range(per_cell):
                unit_ref[(chunk + k) * per_cell + u] = dummy
            leaf_ref[chunk + k] = 0
        return chunk + size

    begin_wide = padding(jnp.int32(0), GROUP)
    begin_half = padding(jnp.int32(9 * side * side + 3 * GROUP + 8), GROUP_HALF)

    def prepare(x, carry):
        px = (window_ref[x, :, probes, :] + (x.astype(jnp.float32) - middle)) * SCALE
        row = lax.broadcasted_iota(jnp.int32, (wide, 1), 0).astype(jnp.float32)
        py = (window_ref[x, :, probes + 1, :] + (row - middle)) * SCALE
        parts = three(px), three(py), three(px * px + py * py)
        order = [(0, 0), (0, 0), (0, 0), (0, 1), (0, 1), (0, 2), (1, 0), (1, 0), (1, 0), (1, 1), (1, 1), (1, 2), (2, 0), (2, 1), (2, 2)]
        for k, (which, part) in enumerate(order):
            aug_ref[:, k, :] = parts[which][part]
        for k in range(15, 18):
            aug_ref[:, k, :] = jnp.ones_like(px)
        for k in range(18, AUG):
            aug_ref[:, k, :] = jnp.zeros_like(px)
        for y in range(wide):
            cell = x * wide + y
            rows_ref[pl.ds(pl.multiple_of(cell * slots, slots), slots), :] = jnp.transpose(aug_ref[y]).astype(jnp.bfloat16)
            p = window_ref[x, y, 0:probes, :] * (FACTOR / LOG2_E)
            high = p.astype(jnp.bfloat16).astype(jnp.float32)
            both = jnp.concatenate([high, p - high], axis=0)
            for tile in range(slots // 128):
                piece = both[:, tile * 128 : (tile + 1) * 128]
                turned = pltpu.roll(piece, UNIT_ROWS, 1)
                unit = cell * per_cell + tile * per_tile
                low_lanes = lane_tile < UNIT_ROWS
                first_ref[unit] = jnp.where(low_lanes, piece, 0.0).astype(jnp.bfloat16)
                first_ref[unit + 1] = jnp.where(low_lanes, turned, 0.0).astype(jnp.bfloat16)
                second_ref[unit] = jnp.where(low_lanes, 0.0, turned).astype(jnp.bfloat16)
                second_ref[unit + 1] = jnp.where(low_lanes, 0.0, piece).astype(jnp.bfloat16)
        return carry
    lax.fori_loop(0, wide, prepare, 0)

    rows_ref[dummy * UNIT_ROWS :, :] = jnp.zeros((UNIT_ROWS, AUG), jnp.bfloat16)
    first_ref[dummy] = jnp.zeros((2 * probes, 128), jnp.bfloat16)
    second_ref[dummy] = jnp.zeros((2 * probes, 128), jnp.bfloat16)
    high_ref[...] = jnp.zeros_like(high_ref)
    low_ref[...] = jnp.zeros_like(low_ref)

    row = lax.broadcasted_iota(jnp.int32, (side, 1), 0).astype(jnp.float32)
    for i in range(side):
        offsets = [window_ref[i + 1, 1 : side + 1, probes + axis, :] for axis in range(2)]
        px = (offsets[0] + (i + 1.0 - middle)) * SCALE
        py = (offsets[1] + (row + 1.0 - middle)) * SCALE
        parts = three(-2.0 * px), three(-2.0 * py), three(px * px + py * py)
        order = [(0, 0), (0, 1), (0, 2), (0, 0), (0, 1), (0, 0), (1, 0), (1, 1), (1, 2), (1, 0), (1, 1), (1, 0)]
        for k, (which, part) in enumerate(order):
            aug_ref[0:side, k, :] = parts[which][part]
        for k in range(12, 15):
            aug_ref[0:side, k, :] = jnp.ones_like(px)
        for k in range(3):
            aug_ref[0:side, 15 + k, :] = parts[2][k]
        for j in range(side):
            target_ref[i * side + j] = aug_ref[j].astype(jnp.bfloat16)
        for axis in range(2):
            t = 2.0 * offsets[axis] - 1.0
            terms = [None, t, 2.0 * t * t - 1.0]
            while len(terms) < ORDER:
                terms.append(2.0 * t * terms[-1] - terms[-2])
            for m in range(ORDER):
                value = float(SERIES[0, m]) + float(SERIES[1, m]) * t
                for n in range(2, ORDER):
                    value = value + float(SERIES[n, m]) * terms[n]
                basis_ref[axis, i * side : (i + 1) * side, m, :] = value

    def far_leaf(leaf, starts):
        i = lax.div(leaf, side)
        j = lax.rem(leaf, side)
        x = basis_ref[0, leaf]
        y = basis_ref[1, leaf]
        weights = jnp.concatenate([x[m : m + 1] * y for m in range(ORDER)], axis=0)
        result_ref[leaf] = split_dot(local_ref[i, j], weights) + NUGGET * window_ref[i + 1, j + 1, 0:probes, :]
        return chunk_list(leaf, starts)
    end_wide, end_half = lax.fori_loop(0, side * side, far_leaf, (begin_wide, begin_half), unroll=4)
    padding(end_wide, 2 * GROUP)
    padding(end_half, 2 * GROUP_HALF)

    def sweep(begin, end, width, group):
        def units(chunk):
            return [unit_ref[chunk * per_cell + u] for u in range(per_cell)]

        def distances(chunk):
            rows = jnp.concatenate([rows_ref[pl.ds(pl.multiple_of(unit * UNIT_ROWS, UNIT_ROWS), UNIT_ROWS), :] for unit in units(chunk)], axis=0)
            return dot(rows, target_ref[leaf_ref[chunk], :, 0:width])

        def product(chunk, n):
            u = units(chunk)
            p = jnp.concatenate([first_ref[u[0]] + second_ref[u[1]], first_ref[u[2]] + second_ref[u[3]]], axis=1)
            both = dot(p, high_ref[n, :, :width])
            return both[:probes] + both[probes:] + dot(p[:probes], low_ref[n, :, :width])

        def add(chunk, value):
            result_ref[leaf_ref[chunk], :, 0:width] += value

        for n in range(group):
            g_ref[n, :, :width] = distances(begin + n)

        def step(number, carry):
            chunk = begin + number * group
            sums = []
            for n in range(group):
                sums.append((chunk + n - 1, product(chunk + n - 1, (n - 1) % group)))
                high, low = split(kernel_of(g_ref[n, :, :width]))
                high_ref[n, :, :width] = high
                low_ref[n, :, :width] = low
                g_ref[n, :, :width] = distances(chunk + group + n)
            for item in sums:
                add(*item)
            return carry
        steps = lax.div(end - begin + group - 1, group)
        lax.fori_loop(0, steps, step, 0)
        last = begin + steps * group - 1
        add(last, product(last, group - 1))

    sweep(begin_wide, end_wide, slots, GROUP)
    sweep(begin_half, end_half, half, GROUP_HALF)
    for leaf in range(side * side):
        x = leaf // side
        y = leaf % side
        out_ref[:, x, y, :] = jnp.where(lane < count_ref[(x + 1) * wide + y + 1], result_ref[leaf], 0.0)


def near_scratch(side, slots, probes):
    wide = side + 2
    units = wide * wide * slots // UNIT_ROWS + 1
    chunks = 18 * side * side + 5 * GROUP + 3 * GROUP_HALF + 24
    return [pltpu.VMEM((wide, AUG, slots), jnp.float32),
            pltpu.VMEM((units * UNIT_ROWS, AUG), jnp.bfloat16),
            pltpu.VMEM((side * side, AUG, slots), jnp.bfloat16),
            pltpu.VMEM((units, 2 * probes, 128), jnp.bfloat16),
            pltpu.VMEM((units, 2 * probes, 128), jnp.bfloat16),
            pltpu.VMEM((max(GROUP, GROUP_HALF), slots, slots), jnp.float32),
            pltpu.VMEM((max(GROUP, GROUP_HALF), slots, slots), jnp.bfloat16),
            pltpu.VMEM((max(GROUP, GROUP_HALF), slots, slots), jnp.bfloat16),
            pltpu.VMEM((2, side * side, ORDER, slots), jnp.float32),
            pltpu.VMEM((side * side, probes, slots), jnp.float32),
            pltpu.SMEM((wide * wide,), jnp.int32),
            pltpu.SMEM((chunks * slots // UNIT_ROWS,), jnp.int32),
            pltpu.SMEM((chunks,), jnp.int32)]


def list_tables():
    nodes = node_table() / 2.0
    node_x = np.repeat(nodes, ORDER)
    node_y = np.tile(nodes, ORDER)
    source = np.zeros((6, 6, NODES, 8))
    for x in range(6):
        for y in range(6):
            source[x, y, :, 0] = x + node_x
            source[x, y, :, 1] = y + node_y
            source[x, y, :, 2] = x
            source[x, y, :, 3] = y
    target = np.zeros((8, 2, 2, NODES))
    for x in range(2):
        for y in range(2):
            target[0, x, y] = 2 + x + node_x
            target[1, x, y] = 2 + y + node_y
            target[2, x, y] = 2 + x
            target[3, x, y] = 2 + y
    return (
        source.reshape(36 * NODES, 8).astype(np.float32),
        target.reshape(8, 4 * NODES).astype(np.float32),
    )


def matrices(target_ref, source_ref, rows, lanes, scale):
    delta_x = (target_ref[0:1, lanes] - source_ref[rows, 0:1]) * scale
    delta_y = (target_ref[1:2, lanes] - source_ref[rows, 1:2]) * scale
    apart = jnp.maximum(
        jnp.abs(target_ref[2:3, lanes] - source_ref[rows, 2:3]),
        jnp.abs(target_ref[3:4, lanes] - source_ref[rows, 3:4]),
    )
    return jnp.where(apart > 1.5, matern(delta_x * delta_x + delta_y * delta_y), 0.0)


def list_kernel(
    depth, extra, has_top, source_ref, target_ref, child_ref, maps_ref, *refs
):
    if has_top:
        top_ref, refs = refs[0], refs[1:]
    rims, grid_ref, out_ref = refs[:depth], refs[depth], refs[depth + 1]
    padded = refs[depth + 2 : depth + 2 + extra]
    locals_ref = refs[depth + 2 + extra :]
    probes = grid_ref.shape[2]
    width = target_ref.shape[1]
    groups = source_ref.shape[0] // width
    per_group = width // NODES

    for level in range(extra):
        padded[level][...] = jnp.zeros_like(padded[level])
        count_x = padded[level].shape[0] - 4
        count_y = padded[level].shape[1] - 4
        if level == 0:
            padded[0][2 : 2 + count_x, 2 : 2 + count_y] = grid_ref[...]
        else:
            for x in range(count_x):
                for y in range(count_y):
                    padded[level][2 + x, 2 + y] = merged(padded[level - 1], x, y, maps_ref, 2)

    def gathered(load, group):
        boxes = [group * per_group + n for n in range(per_group)]
        return jnp.concatenate([load(box // 6, box % 6) for box in boxes], axis=1)

    ix = lax.axis_index("gx")
    iy = lax.axis_index("gy")
    own_child = []
    for level in range(extra):
        own_child.append((ix >> level) % 2 * 2 + (iy >> level) % 2)
    lanes = slice(0, extra * NODES)
    far_target = jnp.concatenate([child_ref[child] for child in own_child], axis=1)
    lane = lax.broadcasted_iota(jnp.int32, (1, extra * NODES), 1)
    scales = jnp.zeros((1, extra * NODES), jnp.float32)
    for level in range(extra):
        scales = jnp.where(lane // NODES == level, UNIT * 2.0 ** (depth + level), scales)
    total = jnp.zeros((extra * probes, extra * NODES), jnp.float32)
    for group in range(groups):
        parts = []
        for level in range(extra):
            first_x = (ix >> (level + 1)) * 2
            first_y = (iy >> (level + 1)) * 2
            parts.append(
                gathered(lambda x, y: padded[level][first_x + x, first_y + y], group)
            )
        rows = slice(group * width, (group + 1) * width)
        matrix = matrices(far_target, source_ref, rows, lanes, scales)
        total = total + split_dot(jnp.concatenate(parts, axis=0), matrix)
    local = top_ref[...] if has_top else None
    for level in range(extra - 1, -1, -1):
        own = total[level * probes : (level + 1) * probes, level * NODES : (level + 1) * NODES]
        own = own * FACTOR
        if local is not None:
            own = own + dot_rows(local, maps_ref[own_child[level]])
        local = own
    locals_ref[depth][0, 0] = local

    for level in range(depth - 1, -1, -1):
        rim_ref = rims[level]
        half = (rim_ref.shape[0] - 4) // 2
        total = jnp.zeros((half * half * probes, width), jnp.float32)
        for group in range(groups):
            parts = [
                gathered(lambda x, y: rim_ref[2 * px + x, 2 * py + y], group)
                for px in range(half)
                for py in range(half)
            ]
            rows = slice(group * width, (group + 1) * width)
            matrix = matrices(
                target_ref, source_ref, rows, slice(0, width), UNIT * 2.0**level
            )
            total = total + split_dot(jnp.concatenate(parts, axis=0), matrix)
        target = out_ref if level == 0 else locals_ref[level]
        above = jnp.concatenate(
            [locals_ref[level + 1][px, py] for px in range(half) for py in range(half)], axis=0
        )
        for child in range(4):
            value = FACTOR * total[:, child * NODES : (child + 1) * NODES] + dot_rows(
                above, maps_ref[child]
            )
            for box in range(half * half):
                target[2 * (box // half) + child // 2, 2 * (box % half) + child % 2] = value[
                    box * probes : (box + 1) * probes
                ]


def upward(children, maps):
    half_x = children.shape[0] // 2
    half_y = children.shape[1] // 2
    grouped = children.reshape((half_x, 2, half_y, 2) + children.shape[2:])
    return jnp.einsum(
        "xyrq,ixjypr->ijpq", maps.reshape(2, 2, NODES, NODES), grouped, precision=HIGHEST
    )


def interact_top(box_grid, own_x, own_y, box_side):
    nodes = jnp.asarray(node_table() * (box_side / 2.0), jnp.float32)
    node_x = jnp.repeat(nodes, ORDER)
    node_y = jnp.tile(nodes, ORDER)
    shift_x = (jnp.arange(box_grid.shape[0], dtype=jnp.int32) - own_x).astype(jnp.float32)
    shift_y = (jnp.arange(box_grid.shape[1], dtype=jnp.int32) - own_y).astype(jnp.float32)
    delta_x = (node_x[:, None] - node_x[None, :] - shift_x[:, None, None] * box_side) * UNIT
    delta_y = (node_y[:, None] - node_y[None, :] - shift_y[:, None, None] * box_side) * UNIT
    matrices = matern((delta_x * delta_x)[:, None] + (delta_y * delta_y)[None])
    separated = jnp.maximum(jnp.abs(shift_x)[:, None], jnp.abs(shift_y)[None]) >= 2.0
    return jnp.einsum(
        "abqr,abpr->pq",
        jnp.where(separated[:, :, None, None], FACTOR * matrices, 0.0),
        box_grid,
        precision=HIGHEST,
    )


def per_device(offsets, probes, counts):
    count_p, side, _, slots = probes.shape
    depth = side.bit_length() - 1
    extra = 2
    top = depth + extra
    index_x = lax.axis_index("gx")
    index_y = lax.axis_index("gy")
    size_x = lax.axis_size("gx")
    size_y = lax.axis_size("gy")
    wide = side + 2
    table = jnp.asarray(series_at_nodes().T, jnp.float32)
    maps = jnp.asarray(child_maps())
    smem = pl.BlockSpec(memory_space=pltpu.SMEM)
    vmem = pl.BlockSpec(memory_space=pltpu.VMEM)

    def shape(*dims):
        return jax.ShapeDtypeStruct(dims, jnp.float32)

    record, *levels = pl.pallas_call(
        functools.partial(up_kernel, side),
        out_shape=[shape(side, side, ROWS, slots)]
        + [shape(side >> k, side >> k, count_p, NODES) for k in range(depth + 1)],
        in_specs=[smem, vmem, vmem, vmem, vmem],
        out_specs=[vmem] * (depth + 2),
        name="up",
    )(counts, table, maps, offsets, probes)
    window, *rims, grid = pl.pallas_call(
        functools.partial(exchange_kernel, (size_x, size_y)),
        out_shape=[shape(wide, wide, ROWS, slots)]
        + [shape((side >> k) + 4, (side >> k) + 4, count_p, NODES) for k in range(depth)]
        + [shape(size_x, size_y, count_p, NODES)],
        in_specs=[vmem] * (depth + 2),
        out_specs=[vmem] * (depth + 2),
        scratch_shapes=[
            pltpu.SemaphoreType.DMA((depth + 1, 8)),
            pltpu.SemaphoreType.DMA((depth + 1, 8)),
            pltpu.SemaphoreType.DMA((size_x + size_y - 2,)),
            pltpu.SemaphoreType.DMA((size_x + size_y - 2,)),
            pltpu.SemaphoreType.DMA,
        ],
        compiler_params=pltpu.CompilerParams(collective_id=0, has_side_effects=True),
        name="exchange",
    )(record, *levels)

    tops = []
    if max(size_x, size_y) > 2 * 2**extra:
        grids = [grid]
        for _ in range(extra):
            grids.append(upward(grids[-1], maps))
        tops = [interact_top(grids[-1], index_x // 2**extra, index_y // 2**extra, 2.0**top)]
    source_table, target_table = list_tables()
    child_table = np.ascontiguousarray(
        np.transpose(target_table.reshape(8, 4, NODES), (1, 0, 2))
    )
    local = pl.pallas_call(
        functools.partial(list_kernel, depth, extra, bool(tops)),
        out_shape=shape(side, side, count_p, NODES),
        in_specs=[vmem] * (4 + len(tops) + depth + 1),
        out_specs=vmem,
        scratch_shapes=[
            pltpu.VMEM(((size_x >> k) + 4, (size_y >> k) + 4, count_p, NODES), jnp.float32)
            for k in range(extra)
        ]
        + [
            pltpu.VMEM((side >> k, side >> k, count_p, NODES), jnp.float32)
            for k in range(depth + 1)
        ],
        name="lists",
    )(
        jnp.asarray(source_table),
        jnp.asarray(target_table),
        jnp.asarray(child_table),
        maps,
        *tops,
        *rims,
        grid,
    )
    return pl.pallas_call(
        functools.partial(near_kernel, side),
        out_shape=shape(count_p, side, side, slots),
        in_specs=[vmem, vmem],
        out_specs=vmem,
        scratch_shapes=near_scratch(side, slots, count_p),
        name="near",
    )(window, local)


def solution(mesh):
    placed = (P(None, "gx", "gy", None), P(None, "gx", "gy", None), P("gx", "gy"))
    return jax.shard_map(
        per_device, mesh=mesh, in_specs=placed, out_specs=P(None, "gx", "gy", None), check_vma=False
    )
```

```python
import functools
import math

import jax
import jax.numpy as jnp
import numpy as np
from jax import lax
from jax.experimental import pallas as pl
from jax.experimental.pallas import tpu as pltpu
from jax.sharding import PartitionSpec as P

ORDER = 8
NODES = ORDER * ORDER
ROOT_THREE = 1.7320508075688772
LENGTH_SCALE = 6.0
AMPLITUDE = 1.0 / 96.0
SHORT_AMPLITUDE = 1.0 / 16.0
NUGGET = 0.5
RATIO = 12
UNIT = ROOT_THREE * RATIO / LENGTH_SCALE
FACTOR = AMPLITUDE / RATIO
LOG2_E = 1.4426950408889634
SHORT_SHIFT = math.log2(SHORT_AMPLITUDE / FACTOR)
HIGH = lax.Precision.HIGH
HIGHEST = lax.Precision.HIGHEST
ROWS = 24
UNIT_ROWS = 64
GROUP = 4
GROUP_HALF = 4
SCALE = UNIT * LOG2_E
AUG = 32


def node_table():
    slots = np.arange(ORDER)
    return np.cos((2.0 * slots + 1.0) * (np.pi / (2.0 * ORDER)))


def series_at_nodes():
    powers = np.arange(ORDER)
    slots = np.arange(ORDER)
    table = np.cos(powers[:, None] * (2.0 * slots[None, :] + 1.0) * (np.pi / (2.0 * ORDER)))
    table = table * (2.0 / ORDER)
    table[0] = 1.0 / ORDER
    return table


SERIES = series_at_nodes()


def interpolation(coords):
    angles = np.arccos(np.clip(coords, -1.0, 1.0))
    series = np.cos(angles[:, None] * np.arange(ORDER))
    return series @ series_at_nodes()


def child_maps():
    nodes = node_table()
    result = []
    for child_x in range(2):
        for child_y in range(2):
            weight_x = interpolation((nodes - 1.0) / 2.0 + child_x)
            weight_y = interpolation((nodes - 1.0) / 2.0 + child_y)
            result.append(
                (weight_x[:, None, :, None] * weight_y[None, :, None, :]).reshape(NODES, NODES)
            )
    return np.stack(result).astype(np.float32)


def matern(dist_sq):
    safe = jnp.maximum(dist_sq, 1e-30)
    scaled = safe * lax.rsqrt(safe)
    decay = jnp.exp2(scaled * (-LOG2_E / RATIO))
    short = jnp.exp2(scaled * -LOG2_E + SHORT_SHIFT)
    return decay * (scaled + RATIO) + short * (scaled + 1.0)


def split(value):
    high = value.astype(jnp.bfloat16)
    return high, (value - high.astype(jnp.float32)).astype(jnp.bfloat16)


def dot(a, b):
    return jnp.dot(a, b, preferred_element_type=jnp.float32)


def split_dot(a, b):
    a_high, a_low = split(a)
    b_high, b_low = split(b)
    return dot(a_high, b_high) + dot(a_high, b_low) + dot(a_low, b_high)


def kernel_of(dist_sq):
    safe = jnp.maximum(dist_sq, 1e-30)
    scaled = safe * lax.rsqrt(safe)
    decay = jnp.exp2(scaled * (-1.0 / RATIO))
    short = jnp.exp2(SHORT_SHIFT - scaled)
    return decay * (scaled + RATIO * LOG2_E) + short * (scaled + LOG2_E)


def three(value):
    first = value.astype(jnp.bfloat16)
    rest = value - first.astype(jnp.float32)
    second = rest.astype(jnp.bfloat16)
    third = (rest - second.astype(jnp.float32)).astype(jnp.bfloat16)
    return [part.astype(jnp.float32) for part in (first, second, third)]


def near_kernel(side, window_ref, local_ref, basis_ref, out_ref, aug_ref, rows_ref, target_ref, first_ref, second_ref,
                 g_ref, high_ref, low_ref, result_ref, count_ref, unit_ref, leaf_ref):
    wide = side + 2
    slots = window_ref.shape[3]
    probes = out_ref.shape[0]
    half = slots // 2
    per_cell = slots // UNIT_ROWS
    per_tile = 128 // UNIT_ROWS
    dummy = wide * wide * per_cell
    lane = lax.broadcasted_iota(jnp.int32, (1, slots), 1)
    lane_tile = lax.broadcasted_iota(jnp.int32, (1, 128), 1)
    middle = wide / 2.0

    for x in range(wide):
        for y in range(wide):
            value = window_ref[x, y, probes + 2 : probes + 3, 0:1].astype(jnp.int32)
            count_ref[x * wide + y] = value[0, 0]

    def chunk_list(leaf, starts):
        i = lax.div(leaf, side)
        j = lax.rem(leaf, side)
        keep = count_ref[(i + 1) * wide + j + 1] > half
        chunk = jnp.where(keep, starts[0], starts[1])
        begin = chunk * per_cell
        n = begin
        for a in range(3):
            for b in range(3):
                cell = (i + a) * wide + j + b
                for u in range(per_cell):
                    unit_ref[n + u] = cell * per_cell + u
                n = n + lax.div(count_ref[cell] + (UNIT_ROWS - 1), UNIT_ROWS)
        for u in range(per_cell):
            unit_ref[n + u] = dummy
        chunks = lax.div(n - begin + per_cell - 1, per_cell)
        for k in range(9):
            leaf_ref[chunk + k] = leaf
        return starts[0] + jnp.where(keep, chunks, 0), starts[1] + jnp.where(keep, 0, chunks)

    def padding(chunk, size):
        for k in range(size):
            for u in range(per_cell):
                unit_ref[(chunk + k) * per_cell + u] = dummy
            leaf_ref[chunk + k] = 0
        return chunk + size

    begin_wide = padding(jnp.int32(0), GROUP)
    begin_half = padding(jnp.int32(9 * side * side + 3 * GROUP + 8), GROUP_HALF)

    def prepare(x, carry):
        px = (window_ref[x, :, probes, :] + (x.astype(jnp.float32) - middle)) * SCALE
        row = lax.broadcasted_iota(jnp.int32, (wide, 1), 0).astype(jnp.float32)
        py = (window_ref[x, :, probes + 1, :] + (row - middle)) * SCALE
        parts = three(px), three(py), three(px * px + py * py)
        order = [(0, 0), (0, 0), (0, 0), (0, 1), (0, 1), (0, 2), (1, 0), (1, 0), (1, 0), (1, 1), (1, 1), (1, 2), (2, 0), (2, 1), (2, 2)]
        for k, (which, part) in enumerate(order):
            aug_ref[:, k, :] = parts[which][part]
        for k in range(15, 18):
            aug_ref[:, k, :] = jnp.ones_like(px)
        for k in range(18, AUG):
            aug_ref[:, k, :] = jnp.zeros_like(px)
        for y in range(wide):
            cell = x * wide + y
            rows_ref[pl.ds(pl.multiple_of(cell * slots, slots), slots), :] = jnp.transpose(aug_ref[y]).astype(jnp.bfloat16)
            p = window_ref[x, y, 0:probes, :] * (FACTOR / LOG2_E)
            high = p.astype(jnp.bfloat16).astype(jnp.float32)
            both = jnp.concatenate([high, p - high], axis=0)
            for tile in range(slots // 128):
                piece = both[:, tile * 128 : (tile + 1) * 128]
                turned = pltpu.roll(piece, UNIT_ROWS, 1)
                unit = cell * per_cell + tile * per_tile
                low_lanes = lane_tile < UNIT_ROWS
                first_ref[unit] = jnp.where(low_lanes, piece, 0.0).astype(jnp.bfloat16)
                first_ref[unit + 1] = jnp.where(low_lanes, turned, 0.0).astype(jnp.bfloat16)
                second_ref[unit] = jnp.where(low_lanes, 0.0, turned).astype(jnp.bfloat16)
                second_ref[unit + 1] = jnp.where(low_lanes, 0.0, piece).astype(jnp.bfloat16)
        return carry
    lax.fori_loop(0, wide, prepare, 0)

    rows_ref[dummy * UNIT_ROWS :, :] = jnp.zeros((UNIT_ROWS, AUG), jnp.bfloat16)
    first_ref[dummy] = jnp.zeros((2 * probes, 128), jnp.bfloat16)
    second_ref[dummy] = jnp.zeros((2 * probes, 128), jnp.bfloat16)
    high_ref[...] = jnp.zeros_like(high_ref)
    low_ref[...] = jnp.zeros_like(low_ref)

    row = lax.broadcasted_iota(jnp.int32, (side, 1), 0).astype(jnp.float32)
    for i in range(side):
        offsets = [window_ref[i + 1, 1 : side + 1, probes + axis, :] for axis in range(2)]
        px = (offsets[0] + (i + 1.0 - middle)) * SCALE
        py = (offsets[1] + (row + 1.0 - middle)) * SCALE
        parts = three(-2.0 * px), three(-2.0 * py), three(px * px + py * py)
        order = [(0, 0), (0, 1), (0, 2), (0, 0), (0, 1), (0, 0), (1, 0), (1, 1), (1, 2), (1, 0), (1, 1), (1, 0)]
        for k, (which, part) in enumerate(order):
            aug_ref[0:side, k, :] = parts[which][part]
        for k in range(12, 15):
            aug_ref[0:side, k, :] = jnp.ones_like(px)
        for k in range(3):
            aug_ref[0:side, 15 + k, :] = parts[2][k]
        for j in range(side):
            target_ref[i * side + j] = aug_ref[j].astype(jnp.bfloat16)

    def far_leaf(leaf, starts):
        i = lax.div(leaf, side)
        j = lax.rem(leaf, side)
        x = basis_ref[0, leaf]
        y = basis_ref[1, leaf]
        weights = jnp.concatenate([x[m : m + 1] * y for m in range(ORDER)], axis=0)
        result_ref[leaf] = split_dot(local_ref[i, j], weights) + NUGGET * window_ref[i + 1, j + 1, 0:probes, :]
        return chunk_list(leaf, starts)
    end_wide, end_half = lax.fori_loop(0, side * side, far_leaf, (begin_wide, begin_half), unroll=4)
    padding(end_wide, 2 * GROUP)
    padding(end_half, 2 * GROUP_HALF)

    def sweep(begin, end, width, group):
        def units(chunk):
            return [unit_ref[chunk * per_cell + u] for u in range(per_cell)]

        def distances(chunk):
            rows = jnp.concatenate([rows_ref[pl.ds(pl.multiple_of(unit * UNIT_ROWS, UNIT_ROWS), UNIT_ROWS), :] for unit in units(chunk)], axis=0)
            return dot(rows, target_ref[leaf_ref[chunk], :, 0:width])

        def product(chunk, n):
            u = units(chunk)
            p = jnp.concatenate([first_ref[u[0]] + second_ref[u[1]], first_ref[u[2]] + second_ref[u[3]]], axis=1)
            both = dot(p, high_ref[n, :, :width])
            return both[:probes] + both[probes:] + dot(p[:probes], low_ref[n, :, :width])

        def add(chunk, value):
            result_ref[leaf_ref[chunk], :, 0:width] += value

        for n in range(group):
            g_ref[n, :, :width] = distances(begin + n)

        def step(number, carry):
            chunk = begin + number * group
            sums = []
            for n in range(group):
                sums.append((chunk + n - 1, product(chunk + n - 1, (n - 1) % group)))
                high, low = split(kernel_of(g_ref[n, :, :width]))
                high_ref[n, :, :width] = high
                low_ref[n, :, :width] = low
                g_ref[n, :, :width] = distances(chunk + group + n)
            for item in sums:
                add(*item)
            return carry
        steps = lax.div(end - begin + group - 1, group)
        lax.fori_loop(0, steps, step, 0)
        last = begin + steps * group - 1
        add(last, product(last, group - 1))

    sweep(begin_wide, end_wide, slots, GROUP)
    sweep(begin_half, end_half, half, GROUP_HALF)
    for leaf in range(side * side):
        x = leaf // side
        y = leaf % side
        out_ref[:, x, y, :] = jnp.where(lane < count_ref[(x + 1) * wide + y + 1], result_ref[leaf], 0.0)


def near_scratch(side, slots, probes):
    wide = side + 2
    units = wide * wide * slots // UNIT_ROWS + 1
    chunks = 18 * side * side + 5 * GROUP + 3 * GROUP_HALF + 24
    return [pltpu.VMEM((wide, AUG, slots), jnp.float32),
            pltpu.VMEM((units * UNIT_ROWS, AUG), jnp.bfloat16),
            pltpu.VMEM((side * side, AUG, slots), jnp.bfloat16),
            pltpu.VMEM((units, 2 * probes, 128), jnp.bfloat16),
            pltpu.VMEM((units, 2 * probes, 128), jnp.bfloat16),
            pltpu.VMEM((max(GROUP, GROUP_HALF), slots, slots), jnp.float32),
            pltpu.VMEM((max(GROUP, GROUP_HALF), slots, slots), jnp.bfloat16),
            pltpu.VMEM((max(GROUP, GROUP_HALF), slots, slots), jnp.bfloat16),
            pltpu.VMEM((side * side, probes, slots), jnp.float32),
            pltpu.SMEM((wide * wide,), jnp.int32),
            pltpu.SMEM((chunks * slots // UNIT_ROWS,), jnp.int32),
            pltpu.SMEM((chunks,), jnp.int32)]


def pair_tables(levels):
    nodes = node_table() / 2.0
    node_x = np.repeat(nodes, ORDER)
    node_y = np.tile(nodes, ORDER)
    shift_x = np.arange(7.0) - 3.0
    shift_y = np.arange(6.0)[:, None] - 2.0 - np.arange(2.0)[None, :]
    delta_x = node_x[None, :] - node_x[:, None] - shift_x[:, None, None]
    delta_y = node_y[None, None, None, :] - node_y[None, :, None, None] - shift_y[:, None, :, None]
    apart = np.maximum(np.abs(shift_x)[:, None, None], np.abs(shift_y)[None])
    result = []
    for level in range(levels):
        dist = 2.0**level * np.sqrt(delta_x[:, None, :, None] ** 2 + delta_y[None] ** 2)
        scaled = ROOT_THREE * dist / LENGTH_SCALE
        short = scaled * RATIO
        value = AMPLITUDE * (1.0 + scaled) * np.exp(-scaled)
        value = value + SHORT_AMPLITUDE * (1.0 + short) * np.exp(-short)
        value = np.where(apart[:, :, None, :, None] > 1.5, value, 0.0)
        result.append(value.reshape(42 * NODES, 2 * NODES))
    return two_parts(np.stack(result))


def two_parts(value):
    high = value.astype(np.float32).astype(jnp.bfloat16)
    low = (value - high.astype(np.float64)).astype(np.float32).astype(jnp.bfloat16)
    return np.stack([high, low])


def split_dot_const(a, high, low):
    a_high, a_low = split(a)
    rows = a.shape[0]
    both = dot(jnp.concatenate([a_high, a_low], axis=0), high)
    return both[:rows] + both[rows:] + dot(a_high, low)


def dot_rows(a, b):
    return lax.dot_general(a, b, (((1,), (1,)), ((), ())), preferred_element_type=jnp.float32)


def chebyshev(t):
    terms = [None, t, 2.0 * t * t - 1.0]
    while len(terms) < ORDER:
        terms.append(2.0 * t * terms[-1] - terms[-2])
    values = []
    for m in range(ORDER):
        value = float(SERIES[0, m]) + float(SERIES[1, m]) * t
        for n in range(2, ORDER):
            value = value + float(SERIES[n, m]) * terms[n]
        values.append(value)
    return values


def tree_kernel(sizes, depth, extra, count_ref, table_ref, down_ref, up_ref, node_ref, offsets_ref, probes_ref,
                window_ref, local_ref, basis_ref, *refs):
    size_x, size_y = sizes
    rims, refs = refs[:depth], refs[depth:]
    locals_ref, refs = refs[:depth], refs[depth:]
    padded, refs = refs[:extra], refs[extra:]
    own_ref, grid_ref, pair_ref, refs = refs[0], refs[1], refs[2], refs[3:]
    send_sem, recv_sem, line_send, line_recv, own_sem, pair_sem = refs
    windows = (window_ref, *rims)
    side = probes_ref.shape[1]
    probes = probes_ref.shape[0]
    slots = probes_ref.shape[3]
    ix = lax.axis_index("gx")
    iy = lax.axis_index("gy")
    steps = [(dx, dy) for dx in (-1, 0, 1) for dy in (-1, 0, 1) if (dx, dy) != (0, 0)]

    pair_copies = [
        pltpu.make_async_copy(table_ref.at[:, level], pair_ref.at[:, level], pair_sem.at[level])
        for level in range(depth + extra)
    ]
    for copy in pair_copies:
        copy.start()

    def inside(dx, dy):
        x = ix + dx
        y = iy + dy
        return (x >= 0) & (x < size_x) & (y >= 0) & (y < size_y)

    for window in windows:
        window[...] = jnp.zeros_like(window)

    barrier = pltpu.get_barrier_semaphore()

    def greet(x, y):
        pl.semaphore_signal(barrier, inc=1, device_id=(x, y), device_id_type=pl.DeviceIdType.MESH)

    for k in range(1, size_x):
        greet(lax.rem(ix + k, size_x), iy)
    for k in range(1, size_y):
        greet(ix, lax.rem(iy + k, size_y))
    for dx, dy in steps:
        if dx and dy:
            pl.when(inside(dx, dy))(lambda dx=dx, dy=dy: greet(ix + dx, iy + dy))

    lane = lax.broadcasted_iota(jnp.int32, (1, slots), 1)
    for i in range(side):
        for j in range(side):
            count = count_ref[i, j]
            window_ref[i + 1, j + 1, 0:probes, :] = jnp.where(lane < count, probes_ref[:, i, j, :], 0.0)
            window_ref[i + 1, j + 1, probes : probes + 2, :] = offsets_ref[:, i, j, :]
            window_ref[i + 1, j + 1, probes + 2 : ROWS, :] = jnp.full(
                (ROWS - probes - 2, slots), count.astype(jnp.float32)
            )

    sides_x = jnp.minimum(ix, 1) + jnp.minimum(size_x - 1 - ix, 1)
    sides_y = jnp.minimum(iy, 1) + jnp.minimum(size_y - 1 - iy, 1)
    pl.semaphore_wait(barrier, size_x + size_y - 2 + sides_x * sides_y)

    def pieces(step, inner, width):
        if step > 0:
            return pl.ds(inner, width), pl.ds(0, width)
        if step < 0:
            return pl.ds(width, width), pl.ds(width + inner, width)
        return pl.ds(width, inner), pl.ds(width, inner)

    def halo_copy(n, which):
        dx, dy = steps[n]
        window = windows[which]
        wide_x, wide_y = (1, 1) if which == 0 else (2, 1)
        from_x, to_x = pieces(dx, window.shape[0] - 2 * wide_x, wide_x)
        from_y, to_y = pieces(dy, window.shape[1] - 2 * wide_y, wide_y)
        return pltpu.make_async_remote_copy(
            src_ref=window.at[from_x, from_y],
            dst_ref=window.at[to_x, to_y],
            send_sem=send_sem.at[which, n],
            recv_sem=recv_sem.at[which, n],
            device_id=(ix + dx, iy + dy),
            device_id_type=pl.DeviceIdType.MESH,
        )

    def send_halo(which):
        for n in range(len(steps)):
            pl.when(inside(*steps[n]))(lambda n=n: halo_copy(n, which).start())

    def receive_halo(which):
        for n in range(len(steps)):
            dx, dy = steps[n]
            pl.when(inside(-dx, -dy))(lambda n=n: halo_copy(n, which).wait_recv())

    send_halo(0)

    for i in range(side):
        for axis in range(2):
            values = chebyshev(2.0 * offsets_ref[axis, i] - 1.0)
            for m in range(ORDER):
                basis_ref[axis, i * side : (i + 1) * side, m, :] = values[m]
    for i in range(side):
        for j in range(0, side, 2):
            pair = []
            for y in (j, j + 1):
                base_x = basis_ref[0, i * side + y]
                base_y = basis_ref[1, i * side + y]
                weights = jnp.concatenate([base_x[m : m + 1] * base_y for m in range(ORDER)], axis=0)
                w_high, w_low = split(weights)
                m_high, m_low = split(window_ref[i + 1, y + 1, 0:probes, :])
                both = dot_rows(jnp.concatenate([m_high, m_low], axis=0), w_high)
                pair.append(both[:probes] + both[probes:] + dot_rows(m_high, w_low))
            rims[0][2 + i, 1 + j // 2] = jnp.concatenate(pair, axis=1)

    for level in range(1, depth + 1):
        boxes = side >> level
        rim_ref = rims[level - 1]
        children = jnp.concatenate(
            [
                jnp.concatenate([rim_ref[2 + 2 * x, 1 + y], rim_ref[3 + 2 * x, 1 + y]], axis=1)
                for x in range(boxes)
                for y in range(boxes)
            ],
            axis=0,
        )
        merged = split_dot_const(children, up_ref[0], up_ref[1])
        send_halo(level)
        if level == depth:
            own_ref[...] = merged[:, 0:NODES]
        else:
            low_lanes = lax.broadcasted_iota(jnp.int32, (1, 2 * NODES), 1) < NODES
            for x in range(boxes):
                for y in range(0, boxes, 2):
                    first = (x * boxes + y) * probes
                    rims[level][2 + x, 1 + y // 2] = jnp.where(
                        low_lanes, merged[first : first + probes], merged[first + probes : first + 2 * probes]
                    )

    own_copy = pltpu.make_async_copy(own_ref, grid_ref.at[ix, iy], own_sem)
    own_copy.start()

    def line_copy(slot, source, target, x, y):
        return pltpu.make_async_remote_copy(
            src_ref=source,
            dst_ref=target,
            send_sem=line_send.at[slot],
            recv_sem=line_recv.at[slot],
            device_id=(x, y),
            device_id_type=pl.DeviceIdType.MESH,
        )

    along_x = [
        line_copy(k - 1, own_ref, grid_ref.at[ix, iy], lax.rem(ix + k, size_x), iy)
        for k in range(1, size_x)
    ]
    for copy in along_x:
        copy.start()
    for copy in along_x:
        copy.wait_recv()
    own_copy.wait()
    along_y = [
        line_copy(size_x - 1 + k - 1, grid_ref.at[:, iy], grid_ref.at[:, iy], ix, lax.rem(iy + k, size_y))
        for k in range(1, size_y)
    ]
    for copy in along_y:
        copy.start()

    for copy in pair_copies:
        copy.wait()
    block = 6 * NODES
    length = 6 * block
    sums = {}
    for level in range(depth):
        receive_halo(level + 1)
        rim_ref = rims[level]
        half = (rim_ref.shape[0] - 4) // 2
        sources = jnp.concatenate(
            [
                jnp.concatenate([rim_ref[2 * px + x, py + y] for x in range(6) for y in range(3)], axis=1)
                for px in range(half)
                for py in range(half)
            ],
            axis=0,
        )
        matrix = [
            jnp.concatenate(
                [pair_ref[part, level, block : block + length], pair_ref[part, level, 0:length]], axis=1
            )
            for part in range(2)
        ]
        sums[level] = split_dot_const(sources, *matrix)

    for copy in along_y:
        copy.wait_recv()
    for level in range(extra):
        padded[level][...] = jnp.zeros_like(padded[level])
    padded[0][2 : 2 + size_x, 2 : 2 + size_y] = grid_ref[...]

    def merged_boxes(grid, count_x, count_y):
        children = jnp.concatenate(
            [
                jnp.concatenate(
                    [grid[2 + 2 * x + c // 2, 2 + 2 * y + c % 2] for c in range(4)], axis=1
                )
                for x in range(count_x)
                for y in range(count_y)
            ],
            axis=0,
        )
        return split_dot_const(children, up_ref[0], up_ref[1])[:, 0:NODES]

    for level in range(1, extra):
        count_x = size_x >> level
        count_y = size_y >> level
        boxes = merged_boxes(padded[level - 1], count_x, count_y)
        for n in range(count_x * count_y):
            padded[level][2 + n // count_y, 2 + n % count_y] = boxes[n * probes : (n + 1) * probes]

    local = None
    if max(size_x, size_y) > 2 * 2**extra:
        count_x = size_x >> extra
        count_y = size_y >> extra
        boxes = merged_boxes(padded[extra - 1], count_x, count_y)
        box_side = 2.0 ** (depth + extra)
        local = jnp.zeros((probes, NODES), jnp.float32)
        for n in range(count_x * count_y):
            shift_x = (n // count_y - (ix >> extra)).astype(jnp.float32)
            shift_y = (n % count_y - (iy >> extra)).astype(jnp.float32)
            delta_x = (node_ref[0] - node_ref[1] - shift_x) * (box_side * UNIT)
            delta_y = (node_ref[2] - node_ref[3] - shift_y) * (box_side * UNIT)
            matrix = FACTOR * matern(delta_x * delta_x + delta_y * delta_y)
            apart = jnp.maximum(jnp.abs(shift_x), jnp.abs(shift_y)) >= 2.0
            local = local + split_dot(boxes[n * probes : (n + 1) * probes], jnp.where(apart, matrix, 0.0))

    for level in range(extra - 1, -1, -1):
        first_x = (ix >> (level + 1)) * 2
        first_y = (iy >> (level + 1)) * 2
        child_x = (ix >> level) % 2
        child_y = (iy >> level) % 2
        sources = jnp.concatenate(
            [padded[level][first_x + x, first_y + y] for x in range(6) for y in range(6)], axis=1
        )
        rows = pl.ds(pl.multiple_of((1 - child_x) * block, block), length)
        value = split_dot_const(
            sources, pair_ref[0, depth + level, rows], pair_ref[1, depth + level, rows]
        )
        own = jnp.where(child_y > 0, value[:, NODES:], value[:, :NODES])
        if local is not None:
            spread = split_dot_const(local, down_ref[0], down_ref[1])
            near_y = [
                jnp.where(child_y > 0, spread[:, (2 * c + 1) * NODES : (2 * c + 2) * NODES],
                          spread[:, 2 * c * NODES : (2 * c + 1) * NODES])
                for c in range(2)
            ]
            own = own + jnp.where(child_x > 0, near_y[1], near_y[0])
        local = own

    above = local
    for level in range(depth - 1, -1, -1):
        half = side >> (level + 1)
        value = sums[level] + split_dot_const(above, down_ref[0], down_ref[1])
        target = local_ref if level == 0 else locals_ref[level]
        for box in range(half * half):
            for child in range(4):
                target[2 * (box // half) + child // 2, 2 * (box % half) + child % 2] = value[
                    box * probes : (box + 1) * probes, child * NODES : (child + 1) * NODES
                ]
        if level > 0:
            above = jnp.concatenate(
                [target[x, y] for x in range(2 * half) for y in range(2 * half)], axis=0
            )

    receive_halo(0)
    for which in range(depth + 1):
        for n in range(len(steps)):
            pl.when(inside(*steps[n]))(lambda which=which, n=n: halo_copy(n, which).wait_send())
    for copy in along_x + along_y:
        copy.wait_send()


def per_device(offsets, probes, counts):
    count_p, side, _, slots = probes.shape
    depth = side.bit_length() - 1
    extra = 2
    size_x = lax.axis_size("gx")
    size_y = lax.axis_size("gy")
    wide = side + 2
    maps = child_maps().astype(np.float64)
    up = maps.reshape(4 * NODES, NODES)
    down = np.transpose(maps, (2, 0, 1)).reshape(NODES, 4 * NODES)
    nodes = node_table() / 2.0
    node_x = np.broadcast_to(np.repeat(nodes, ORDER), (NODES, NODES))
    node_y = np.broadcast_to(np.tile(nodes, ORDER), (NODES, NODES))
    smem = pl.BlockSpec(memory_space=pltpu.SMEM)
    vmem = pl.BlockSpec(memory_space=pltpu.VMEM)

    def shape(*dims):
        return jax.ShapeDtypeStruct(dims, jnp.float32)

    def scratch(*dims):
        return pltpu.VMEM(dims, jnp.float32)

    window, local, basis = pl.pallas_call(
        functools.partial(tree_kernel, (size_x, size_y), depth, extra),
        out_shape=[
            shape(wide, wide, ROWS, slots),
            shape(side, side, count_p, NODES),
            shape(2, side * side, ORDER, slots),
        ],
        in_specs=[smem, pl.BlockSpec(memory_space=pl.ANY)] + [vmem] * 5,
        out_specs=[vmem] * 3,
        scratch_shapes=[
            scratch((side >> k) + 4, ((side >> k) + 4) // 2, count_p, 2 * NODES) for k in range(depth)
        ]
        + [scratch(side >> k, side >> k, count_p, NODES) for k in range(depth)]
        + [scratch((size_x >> k) + 4, (size_y >> k) + 4, count_p, NODES) for k in range(extra)]
        + [
            scratch(count_p, NODES),
            scratch(size_x, size_y, count_p, NODES),
            pltpu.VMEM((2, depth + extra, 42 * NODES, 2 * NODES), jnp.bfloat16),
            pltpu.SemaphoreType.DMA((depth + 1, 8)),
            pltpu.SemaphoreType.DMA((depth + 1, 8)),
            pltpu.SemaphoreType.DMA((size_x + size_y - 2,)),
            pltpu.SemaphoreType.DMA((size_x + size_y - 2,)),
            pltpu.SemaphoreType.DMA,
            pltpu.SemaphoreType.DMA((depth + extra,)),
        ],
        compiler_params=pltpu.CompilerParams(collective_id=0, has_side_effects=True),
        name="tree",
    )(
        counts,
        jnp.asarray(pair_tables(depth + extra)),
        jnp.asarray(two_parts(down)),
        jnp.asarray(two_parts(np.concatenate([up, up], axis=1))),
        jnp.asarray(np.stack([node_x, node_x.T, node_y, node_y.T]), jnp.float32),
        offsets,
        probes,
    )
    return pl.pallas_call(
        functools.partial(near_kernel, side),
        out_shape=shape(count_p, side, side, slots),
        in_specs=[vmem] * 3,
        out_specs=vmem,
        scratch_shapes=near_scratch(side, slots, count_p),
        name="near",
    )(window, local, basis)


def solution(mesh):
    placed = (P(None, "gx", "gy", None), P(None, "gx", "gy", None), P("gx", "gy"))
    return jax.shard_map(
        per_device, mesh=mesh, in_specs=placed, out_specs=P(None, "gx", "gy", None), check_vma=False
    )
```

```python
import functools
import math

import jax
import jax.numpy as jnp
import numpy as np
from jax import lax
from jax.experimental import pallas as pl
from jax.experimental.pallas import tpu as pltpu
from jax.sharding import PartitionSpec as P

ORDER = 8
NODES = ORDER * ORDER
ROOT_THREE = 1.7320508075688772
LENGTH_SCALE = 6.0
AMPLITUDE = 1.0 / 96.0
SHORT_AMPLITUDE = 1.0 / 16.0
NUGGET = 0.5
RATIO = 12
UNIT = ROOT_THREE * RATIO / LENGTH_SCALE
FACTOR = AMPLITUDE / RATIO
LOG2_E = 1.4426950408889634
SHORT_SHIFT = math.log2(SHORT_AMPLITUDE / FACTOR)
HIGH = lax.Precision.HIGH
HIGHEST = lax.Precision.HIGHEST
ROWS = 24
UNIT_ROWS = 64
DONE = ((0, -1), (0, 1), (-1, 0), (1, 0))
FIRST_STEPS = 4
GROUP = 4
GROUP_HALF = 4
SCALE = UNIT * LOG2_E
AUG = 32


def node_table():
    slots = np.arange(ORDER)
    return np.cos((2.0 * slots + 1.0) * (np.pi / (2.0 * ORDER)))


def series_at_nodes():
    powers = np.arange(ORDER)
    slots = np.arange(ORDER)
    table = np.cos(powers[:, None] * (2.0 * slots[None, :] + 1.0) * (np.pi / (2.0 * ORDER)))
    table = table * (2.0 / ORDER)
    table[0] = 1.0 / ORDER
    return table


SERIES = series_at_nodes()


def interpolation(coords):
    angles = np.arccos(np.clip(coords, -1.0, 1.0))
    series = np.cos(angles[:, None] * np.arange(ORDER))
    return series @ series_at_nodes()


def child_maps():
    nodes = node_table()
    result = []
    for child_x in range(2):
        for child_y in range(2):
            weight_x = interpolation((nodes - 1.0) / 2.0 + child_x)
            weight_y = interpolation((nodes - 1.0) / 2.0 + child_y)
            result.append(
                (weight_x[:, None, :, None] * weight_y[None, :, None, :]).reshape(NODES, NODES)
            )
    return np.stack(result).astype(np.float32)


def matern(dist_sq):
    safe = jnp.maximum(dist_sq, 1e-30)
    scaled = safe * lax.rsqrt(safe)
    decay = jnp.exp2(scaled * (-LOG2_E / RATIO))
    short = jnp.exp2(scaled * -LOG2_E + SHORT_SHIFT)
    return decay * (scaled + RATIO) + short * (scaled + 1.0)


def split(value):
    high = value.astype(jnp.bfloat16)
    return high, (value - high.astype(jnp.float32)).astype(jnp.bfloat16)


def dot(a, b):
    return jnp.dot(a, b, preferred_element_type=jnp.float32)


def split_dot(a, b):
    a_high, a_low = split(a)
    b_high, b_low = split(b)
    return dot(a_high, b_high) + dot(a_high, b_low) + dot(a_low, b_high)


def kernel_of(dist_sq):
    safe = jnp.maximum(dist_sq, 1e-30)
    scaled = safe * lax.rsqrt(safe)
    decay = jnp.exp2(scaled * (-1.0 / RATIO))
    short = jnp.exp2(SHORT_SHIFT - scaled)
    return decay * (scaled + RATIO * LOG2_E) + short * (scaled + LOG2_E)


def three(value):
    first = value.astype(jnp.bfloat16)
    rest = value - first.astype(jnp.float32)
    second = rest.astype(jnp.bfloat16)
    third = (rest - second.astype(jnp.float32)).astype(jnp.bfloat16)
    return [part.astype(jnp.float32) for part in (first, second, third)]


def store_sources(aug_ref, px, py):
    boxes = px.shape[0]
    parts = three(px), three(py), three(px * px + py * py)
    order = [(0, 0), (0, 0), (0, 0), (0, 1), (0, 1), (0, 2)]
    order += [(1, 0), (1, 0), (1, 0), (1, 1), (1, 1), (1, 2), (2, 0), (2, 1), (2, 2)]
    for k, (which, part) in enumerate(order):
        aug_ref[0:boxes, k, :] = parts[which][part]
    for k in range(15, 18):
        aug_ref[0:boxes, k, :] = jnp.ones_like(px)
    for k in range(18, AUG):
        aug_ref[0:boxes, k, :] = jnp.zeros_like(px)


def store_targets(aug_ref, px, py):
    boxes = px.shape[0]
    parts = three(-2.0 * px), three(-2.0 * py), three(px * px + py * py)
    order = [(0, 0), (0, 1), (0, 2), (0, 0), (0, 1), (0, 0)]
    order += [(1, 0), (1, 1), (1, 2), (1, 0), (1, 1), (1, 0)]
    for k, (which, part) in enumerate(order):
        aug_ref[0:boxes, k, :] = parts[which][part]
    for k in range(12, 15):
        aug_ref[0:boxes, k, :] = jnp.ones_like(px)
    for k in range(3):
        aug_ref[0:boxes, 15 + k, :] = parts[2][k]


def sweep(sources, buffers, begin, steps, width, group):
    rows_of, probes_of, leaf_of = sources
    target_ref, g_ref, high_ref, low_ref, result_ref = buffers
    probes = result_ref.shape[1]
    slots = g_ref.shape[1]

    def distances(chunk):
        return dot(rows_of(chunk), target_ref[leaf_of(chunk), :, 0:width])

    def product(chunk, n):
        p = probes_of(chunk)
        both = dot(p, high_ref[n, :, :width])
        return both[:probes] + both[probes:] + dot(p[:probes], low_ref[n, :, :width])

    def add(chunk, value):
        result_ref[leaf_of(chunk), :, 0:width] += value

    high_ref[group - 1, :, :width] = jnp.zeros((slots, width), jnp.bfloat16)
    low_ref[group - 1, :, :width] = jnp.zeros((slots, width), jnp.bfloat16)
    for n in range(group):
        g_ref[n, :, :width] = distances(begin + n)

    def step(number, carry):
        chunk = begin + number * group
        sums = []
        for n in range(group):
            sums.append((chunk + n - 1, product(chunk + n - 1, (n - 1) % group)))
            high, low = split(kernel_of(g_ref[n, :, :width]))
            high_ref[n, :, :width] = high
            low_ref[n, :, :width] = low
            g_ref[n, :, :width] = distances(chunk + group + n)
        for item in sums:
            add(*item)
        return carry

    lax.fori_loop(0, steps, step, 0)
    last = begin + steps * group - 1
    add(last, product(last, group - 1))


def near_kernel(side, window_ref, local_ref, basis_ref, partial_ref, out_ref, aug_ref, rows_ref, target_ref, first_ref, second_ref,
                 g_ref, high_ref, low_ref, result_ref, count_ref, unit_ref, leaf_ref):
    wide = side + 2
    slots = window_ref.shape[3]
    probes = out_ref.shape[0]
    half = slots // 2
    per_cell = slots // UNIT_ROWS
    per_tile = 128 // UNIT_ROWS
    dummy = wide * wide * per_cell
    lane = lax.broadcasted_iota(jnp.int32, (1, slots), 1)
    lane_tile = lax.broadcasted_iota(jnp.int32, (1, 128), 1)
    middle = wide / 2.0

    for x in range(wide):
        for y in range(wide):
            value = window_ref[x, y, probes + 2 : probes + 3, 0:1].astype(jnp.int32)
            count_ref[x * wide + y] = value[0, 0]

    def chunk_list(leaf, starts):
        i = lax.div(leaf, side)
        j = lax.rem(leaf, side)
        keep = count_ref[(i + 1) * wide + j + 1] > half
        chunk = jnp.where(keep, starts[0], starts[1])
        begin = chunk * per_cell
        n = begin
        for a in range(3):
            for b in range(3):
                cell = (i + a) * wide + j + b
                if (a, b) != (1, 1):
                    for u in range(per_cell):
                        unit_ref[n + u] = cell * per_cell + u
                used = lax.div(count_ref[cell] + (UNIT_ROWS - 1), UNIT_ROWS)
                if (a - 1, b - 1) == (0, 0):
                    continue
                if (a - 1, b - 1) in DONE:
                    x = i + (a - 1)
                    y = j + (b - 1)
                    used = jnp.where((x >= 0) & (x < side) & (y >= 0) & (y < side), 0, used)
                n = n + used
        for u in range(per_cell):
            unit_ref[n + u] = dummy
        chunks = lax.div(n - begin + per_cell - 1, per_cell)
        for k in range(9):
            leaf_ref[chunk + k] = leaf
        return starts[0] + jnp.where(keep, chunks, 0), starts[1] + jnp.where(keep, 0, chunks)

    def padding(chunk, size):
        for k in range(size):
            for u in range(per_cell):
                unit_ref[(chunk + k) * per_cell + u] = dummy
            leaf_ref[chunk + k] = 0
        return chunk + size

    begin_wide = padding(jnp.int32(0), GROUP)
    begin_half = padding(jnp.int32(9 * side * side + 3 * GROUP + 8), GROUP_HALF)

    def prepare(x, carry):
        px = (window_ref[x, :, probes, :] + (x.astype(jnp.float32) - middle)) * SCALE
        row = lax.broadcasted_iota(jnp.int32, (wide, 1), 0).astype(jnp.float32)
        py = (window_ref[x, :, probes + 1, :] + (row - middle)) * SCALE
        store_sources(aug_ref, px, py)
        for y in range(wide):
            cell = x * wide + y
            rows_ref[pl.ds(pl.multiple_of(cell * slots, slots), slots), :] = jnp.transpose(aug_ref[y]).astype(jnp.bfloat16)
            p = window_ref[x, y, 0:probes, :] * (FACTOR / LOG2_E)
            high = p.astype(jnp.bfloat16).astype(jnp.float32)
            both = jnp.concatenate([high, p - high], axis=0)
            for tile in range(slots // 128):
                piece = both[:, tile * 128 : (tile + 1) * 128]
                turned = pltpu.roll(piece, UNIT_ROWS, 1)
                unit = cell * per_cell + tile * per_tile
                low_lanes = lane_tile < UNIT_ROWS
                first_ref[unit] = jnp.where(low_lanes, piece, 0.0).astype(jnp.bfloat16)
                first_ref[unit + 1] = jnp.where(low_lanes, turned, 0.0).astype(jnp.bfloat16)
                second_ref[unit] = jnp.where(low_lanes, 0.0, turned).astype(jnp.bfloat16)
                second_ref[unit + 1] = jnp.where(low_lanes, 0.0, piece).astype(jnp.bfloat16)
        return carry
    lax.fori_loop(0, wide, prepare, 0)

    rows_ref[dummy * UNIT_ROWS :, :] = jnp.zeros((UNIT_ROWS, AUG), jnp.bfloat16)
    first_ref[dummy] = jnp.zeros((2 * probes, 128), jnp.bfloat16)
    second_ref[dummy] = jnp.zeros((2 * probes, 128), jnp.bfloat16)

    row = lax.broadcasted_iota(jnp.int32, (side, 1), 0).astype(jnp.float32)
    for i in range(side):
        offsets = [window_ref[i + 1, 1 : side + 1, probes + axis, :] for axis in range(2)]
        px = (offsets[0] + (i + 1.0 - middle)) * SCALE
        py = (offsets[1] + (row + 1.0 - middle)) * SCALE
        store_targets(aug_ref, px, py)
        for j in range(side):
            target_ref[i * side + j] = aug_ref[j].astype(jnp.bfloat16)

    def far_leaf(leaf, starts):
        i = lax.div(leaf, side)
        j = lax.rem(leaf, side)
        x = basis_ref[0, leaf]
        y = basis_ref[1, leaf]
        weights = jnp.concatenate([x[m : m + 1] * y for m in range(ORDER)], axis=0)
        result_ref[leaf] = split_dot(local_ref[i, j], weights) + NUGGET * window_ref[i + 1, j + 1, 0:probes, :] + partial_ref[leaf]
        return chunk_list(leaf, starts)
    end_wide, end_half = lax.fori_loop(0, side * side, far_leaf, (begin_wide, begin_half), unroll=4)
    padding(end_wide, 2 * GROUP)
    padding(end_half, 2 * GROUP_HALF)

    def units(chunk):
        return [unit_ref[chunk * per_cell + u] for u in range(per_cell)]

    def rows_of(chunk):
        return jnp.concatenate(
            [
                rows_ref[pl.ds(pl.multiple_of(unit * UNIT_ROWS, UNIT_ROWS), UNIT_ROWS), :]
                for unit in units(chunk)
            ],
            axis=0,
        )

    def probes_of(chunk):
        u = units(chunk)
        return jnp.concatenate(
            [first_ref[u[0]] + second_ref[u[1]], first_ref[u[2]] + second_ref[u[3]]], axis=1
        )

    def leaf_of(chunk):
        return leaf_ref[chunk]

    sources = rows_of, probes_of, leaf_of
    buffers = target_ref, g_ref, high_ref, low_ref, result_ref
    wide_steps = lax.div(end_wide - begin_wide + GROUP - 1, GROUP)
    half_steps = lax.div(end_half - begin_half + GROUP_HALF - 1, GROUP_HALF)
    sweep(sources, buffers, begin_wide, wide_steps, slots, GROUP)
    sweep(sources, buffers, begin_half, half_steps, half, GROUP_HALF)
    for leaf in range(side * side):
        x = leaf // side
        y = leaf % side
        out_ref[:, x, y, :] = jnp.where(lane < count_ref[(x + 1) * wide + y + 1], result_ref[leaf], 0.0)


def near_scratch(side, slots, probes):
    wide = side + 2
    units = wide * wide * slots // UNIT_ROWS + 1
    chunks = 18 * side * side + 5 * GROUP + 3 * GROUP_HALF + 24
    return [pltpu.VMEM((wide, AUG, slots), jnp.float32),
            pltpu.VMEM((units * UNIT_ROWS, AUG), jnp.bfloat16),
            pltpu.VMEM((side * side, AUG, slots), jnp.bfloat16),
            pltpu.VMEM((units, 2 * probes, 128), jnp.bfloat16),
            pltpu.VMEM((units, 2 * probes, 128), jnp.bfloat16),
            pltpu.VMEM((max(GROUP, GROUP_HALF), slots, slots), jnp.float32),
            pltpu.VMEM((max(GROUP, GROUP_HALF), slots, slots), jnp.bfloat16),
            pltpu.VMEM((max(GROUP, GROUP_HALF), slots, slots), jnp.bfloat16),
            pltpu.VMEM((side * side, probes, slots), jnp.float32),
            pltpu.SMEM((wide * wide,), jnp.int32),
            pltpu.SMEM((chunks * slots // UNIT_ROWS,), jnp.int32),
            pltpu.SMEM((chunks,), jnp.int32)]


def pair_tables(levels):
    nodes = node_table() / 2.0
    node_x = np.repeat(nodes, ORDER)
    node_y = np.tile(nodes, ORDER)
    shift_x = np.arange(7.0) - 3.0
    shift_y = np.arange(6.0)[:, None] - 2.0 - np.arange(2.0)[None, :]
    delta_x = node_x[None, :] - node_x[:, None] - shift_x[:, None, None]
    delta_y = node_y[None, None, None, :] - node_y[None, :, None, None] - shift_y[:, None, :, None]
    apart = np.maximum(np.abs(shift_x)[:, None, None], np.abs(shift_y)[None])
    result = []
    for level in range(levels):
        dist = 2.0**level * np.sqrt(delta_x[:, None, :, None] ** 2 + delta_y[None] ** 2)
        scaled = ROOT_THREE * dist / LENGTH_SCALE
        short = scaled * RATIO
        value = AMPLITUDE * (1.0 + scaled) * np.exp(-scaled)
        value = value + SHORT_AMPLITUDE * (1.0 + short) * np.exp(-short)
        value = np.where(apart[:, :, None, :, None] > 1.5, value, 0.0)
        result.append(value.reshape(42 * NODES, 2 * NODES))
    return two_parts(np.stack(result))


def two_parts(value):
    high = value.astype(np.float32).astype(jnp.bfloat16)
    low = (value - high.astype(np.float64)).astype(np.float32).astype(jnp.bfloat16)
    return np.stack([high, low])


def split_dot_const(a, high, low):
    a_high, a_low = split(a)
    rows = a.shape[0]
    both = dot(jnp.concatenate([a_high, a_low], axis=0), high)
    return both[:rows] + both[rows:] + dot(a_high, low)


def dot_rows(a, b):
    return lax.dot_general(a, b, (((1,), (1,)), ((), ())), preferred_element_type=jnp.float32)


def chebyshev(t):
    terms = [None, t, 2.0 * t * t - 1.0]
    while len(terms) < ORDER:
        terms.append(2.0 * t * terms[-1] - terms[-2])
    values = []
    for m in range(ORDER):
        value = float(SERIES[0, m]) + float(SERIES[1, m]) * t
        for n in range(2, ORDER):
            value = value + float(SERIES[n, m]) * terms[n]
        values.append(value)
    return values


def tree_kernel(sizes, depth, extra, count_ref, table_ref, down_ref, up_ref, node_ref, offsets_ref, probes_ref,
                window_ref, local_ref, basis_ref, partial_ref, *refs):
    size_x, size_y = sizes
    rims, refs = refs[:depth], refs[depth:]
    locals_ref, refs = refs[:depth], refs[depth:]
    padded, refs = refs[:extra], refs[extra:]
    own_ref, grid_ref, pair_ref, refs = refs[0], refs[1], refs[2], refs[3:]
    aug_ref, rows_ref, target_ref, probe_ref, g_ref, high_ref, low_ref, refs = *refs[:7], refs[7:]
    send_sem, recv_sem, line_send, line_recv, own_sem, pair_sem = refs
    windows = (window_ref, *rims)
    side = probes_ref.shape[1]
    probes = probes_ref.shape[0]
    slots = probes_ref.shape[3]
    ix = lax.axis_index("gx")
    iy = lax.axis_index("gy")
    steps = [(dx, dy) for dx in (-1, 0, 1) for dy in (-1, 0, 1) if (dx, dy) != (0, 0)]

    pair_copies = [
        pltpu.make_async_copy(table_ref.at[:, level], pair_ref.at[:, level], pair_sem.at[level])
        for level in range(depth + extra)
    ]
    for copy in pair_copies:
        copy.start()

    def inside(dx, dy):
        x = ix + dx
        y = iy + dy
        return (x >= 0) & (x < size_x) & (y >= 0) & (y < size_y)

    for window in windows:
        window[...] = jnp.zeros_like(window)

    barrier = pltpu.get_barrier_semaphore()

    def greet(x, y):
        pl.semaphore_signal(barrier, inc=1, device_id=(x, y), device_id_type=pl.DeviceIdType.MESH)

    for k in range(1, size_x):
        greet(lax.rem(ix + k, size_x), iy)
    for k in range(1, size_y):
        greet(ix, lax.rem(iy + k, size_y))
    for dx, dy in steps:
        if dx and dy:
            pl.when(inside(dx, dy))(lambda dx=dx, dy=dy: greet(ix + dx, iy + dy))

    lane = lax.broadcasted_iota(jnp.int32, (1, slots), 1)
    for i in range(side):
        for j in range(side):
            count = count_ref[i, j]
            window_ref[i + 1, j + 1, 0:probes, :] = jnp.where(lane < count, probes_ref[:, i, j, :], 0.0)
            window_ref[i + 1, j + 1, probes : probes + 2, :] = offsets_ref[:, i, j, :]
            window_ref[i + 1, j + 1, probes + 2 : ROWS, :] = jnp.full(
                (ROWS - probes - 2, slots), count.astype(jnp.float32)
            )

    sides_x = jnp.minimum(ix, 1) + jnp.minimum(size_x - 1 - ix, 1)
    sides_y = jnp.minimum(iy, 1) + jnp.minimum(size_y - 1 - iy, 1)
    pl.semaphore_wait(barrier, size_x + size_y - 2 + sides_x * sides_y)

    def pieces(step, inner, width):
        if step > 0:
            return pl.ds(inner, width), pl.ds(0, width)
        if step < 0:
            return pl.ds(width, width), pl.ds(width + inner, width)
        return pl.ds(width, inner), pl.ds(width, inner)

    def halo_copy(n, which):
        dx, dy = steps[n]
        window = windows[which]
        wide_x, wide_y = (1, 1) if which == 0 else (2, 1)
        from_x, to_x = pieces(dx, window.shape[0] - 2 * wide_x, wide_x)
        from_y, to_y = pieces(dy, window.shape[1] - 2 * wide_y, wide_y)
        return pltpu.make_async_remote_copy(
            src_ref=window.at[from_x, from_y],
            dst_ref=window.at[to_x, to_y],
            send_sem=send_sem.at[which, n],
            recv_sem=recv_sem.at[which, n],
            device_id=(ix + dx, iy + dy),
            device_id_type=pl.DeviceIdType.MESH,
        )

    def send_halo(which):
        for n in range(len(steps)):
            pl.when(inside(*steps[n]))(lambda n=n: halo_copy(n, which).start())

    def receive_halo(which):
        for n in range(len(steps)):
            dx, dy = steps[n]
            pl.when(inside(-dx, -dy))(lambda n=n: halo_copy(n, which).wait_recv())


    for i in range(side):
        for axis in range(2):
            values = chebyshev(2.0 * offsets_ref[axis, i] - 1.0)
            for m in range(ORDER):
                basis_ref[axis, i * side : (i + 1) * side, m, :] = values[m]
    for i in range(side):
        for j in range(0, side, 2):
            pair = []
            for y in (j, j + 1):
                base_x = basis_ref[0, i * side + y]
                base_y = basis_ref[1, i * side + y]
                weights = jnp.concatenate([base_x[m : m + 1] * base_y for m in range(ORDER)], axis=0)
                w_high, w_low = split(weights)
                m_high, m_low = split(window_ref[i + 1, y + 1, 0:probes, :])
                both = dot_rows(jnp.concatenate([m_high, m_low], axis=0), w_high)
                pair.append(both[:probes] + both[probes:] + dot_rows(m_high, w_low))
            rims[0][2 + i, 1 + j // 2] = jnp.concatenate(pair, axis=1)

    for level in range(1, depth + 1):
        boxes = side >> level
        rim_ref = rims[level - 1]
        children = jnp.concatenate(
            [
                jnp.concatenate([rim_ref[2 + 2 * x, 1 + y], rim_ref[3 + 2 * x, 1 + y]], axis=1)
                for x in range(boxes)
                for y in range(boxes)
            ],
            axis=0,
        )
        merged = split_dot_const(children, up_ref[0], up_ref[1])
        if level == depth:
            own_ref[...] = merged[:, 0:NODES]
        else:
            low_lanes = lax.broadcasted_iota(jnp.int32, (1, 2 * NODES), 1) < NODES
            for x in range(boxes):
                for y in range(0, boxes, 2):
                    first = (x * boxes + y) * probes
                    rims[level][2 + x, 1 + y // 2] = jnp.where(
                        low_lanes, merged[first : first + probes], merged[first + probes : first + 2 * probes]
                    )

    own_copy = pltpu.make_async_copy(own_ref, grid_ref.at[ix, iy], own_sem)
    own_copy.start()

    def line_copy(slot, source, target, x, y):
        return pltpu.make_async_remote_copy(
            src_ref=source,
            dst_ref=target,
            send_sem=line_send.at[slot],
            recv_sem=line_recv.at[slot],
            device_id=(x, y),
            device_id_type=pl.DeviceIdType.MESH,
        )

    along_x = [
        line_copy(k - 1, own_ref, grid_ref.at[ix, iy], lax.rem(ix + k, size_x), iy)
        for k in range(1, size_x)
    ]
    for copy in along_x:
        copy.start()
    for which in range(depth, 0, -1):
        send_halo(which)

    middle = (side + 2) / 2.0
    column = lax.broadcasted_iota(jnp.int32, (side, 1), 0).astype(jnp.float32)
    for i in range(side):
        px = (offsets_ref[0, i] + (i + 1.0 - middle)) * SCALE
        py = (offsets_ref[1, i] + (column + 1.0 - middle)) * SCALE
        store_sources(aug_ref, px, py)
        for j in range(side):
            cell = i * side + j
            rows_ref[cell] = jnp.transpose(aug_ref[j]).astype(jnp.bfloat16)
            p = window_ref[i + 1, j + 1, 0:probes, :] * (FACTOR / LOG2_E)
            p_high, p_low = split(p)
            probe_ref[cell] = jnp.concatenate([p_high, p_low], axis=0)
        store_targets(aug_ref, px, py)
        for j in range(side):
            target_ref[i * side + j] = aug_ref[j].astype(jnp.bfloat16)
    partial_ref[...] = jnp.zeros_like(partial_ref)
    pairs_done = side * side
    for da, db in DONE:
        pairs_done += (side - abs(da)) * (side - abs(db))

    def own_pair(number):
        number = jnp.clip(number, 0, pairs_done - 1)
        leaf = number
        cell = number
        start = side * side
        for da, db in DONE:
            columns = side - abs(db)
            k = jnp.maximum(number - start, 0)
            i = lax.div(k, columns) + max(-da, 0)
            j = lax.rem(k, columns) + max(-db, 0)
            leaf = jnp.where(number >= start, i * side + j, leaf)
            cell = jnp.where(number >= start, (i + da) * side + j + db, cell)
            start += (side - abs(da)) * columns
        return leaf, cell

    sources = (
        lambda number: rows_ref[own_pair(number)[1]],
        lambda number: probe_ref[own_pair(number)[1]],
        lambda number: own_pair(number)[0],
    )
    buffers = target_ref, g_ref, high_ref, low_ref, partial_ref
    all_steps = pairs_done // GROUP
    sweep(sources, buffers, 0, FIRST_STEPS, slots, GROUP)
    for copy in along_x:
        copy.wait_recv()
    own_copy.wait()
    along_y = [
        line_copy(size_x - 1 + k - 1, grid_ref.at[:, iy], grid_ref.at[:, iy], ix, lax.rem(iy + k, size_y))
        for k in range(1, size_y)
    ]
    for copy in along_y:
        copy.start()
    send_halo(0)
    sweep(sources, buffers, FIRST_STEPS * GROUP, all_steps - FIRST_STEPS, slots, GROUP)

    for copy in pair_copies:
        copy.wait()
    block = 6 * NODES
    length = 6 * block
    sums = {}
    for level in range(depth):
        receive_halo(level + 1)
        rim_ref = rims[level]
        half = (rim_ref.shape[0] - 4) // 2
        sources = jnp.concatenate(
            [
                jnp.concatenate([rim_ref[2 * px + x, py + y] for x in range(6) for y in range(3)], axis=1)
                for px in range(half)
                for py in range(half)
            ],
            axis=0,
        )
        matrix = [
            jnp.concatenate(
                [pair_ref[part, level, block : block + length], pair_ref[part, level, 0:length]], axis=1
            )
            for part in range(2)
        ]
        sums[level] = split_dot_const(sources, *matrix)

    for copy in along_y:
        copy.wait_recv()
    for level in range(extra):
        padded[level][...] = jnp.zeros_like(padded[level])
    padded[0][2 : 2 + size_x, 2 : 2 + size_y] = grid_ref[...]

    def merged_boxes(grid, count_x, count_y):
        children = jnp.concatenate(
            [
                jnp.concatenate(
                    [grid[2 + 2 * x + c // 2, 2 + 2 * y + c % 2] for c in range(4)], axis=1
                )
                for x in range(count_x)
                for y in range(count_y)
            ],
            axis=0,
        )
        return split_dot_const(children, up_ref[0], up_ref[1])[:, 0:NODES]

    for level in range(1, extra):
        count_x = size_x >> level
        count_y = size_y >> level
        boxes = merged_boxes(padded[level - 1], count_x, count_y)
        for n in range(count_x * count_y):
            padded[level][2 + n // count_y, 2 + n % count_y] = boxes[n * probes : (n + 1) * probes]

    local = None
    if max(size_x, size_y) > 2 * 2**extra:
        count_x = size_x >> extra
        count_y = size_y >> extra
        boxes = merged_boxes(padded[extra - 1], count_x, count_y)
        box_side = 2.0 ** (depth + extra)
        local = jnp.zeros((probes, NODES), jnp.float32)
        for n in range(count_x * count_y):
            shift_x = (n // count_y - (ix >> extra)).astype(jnp.float32)
            shift_y = (n % count_y - (iy >> extra)).astype(jnp.float32)
            delta_x = (node_ref[0] - node_ref[1] - shift_x) * (box_side * UNIT)
            delta_y = (node_ref[2] - node_ref[3] - shift_y) * (box_side * UNIT)
            matrix = FACTOR * matern(delta_x * delta_x + delta_y * delta_y)
            apart = jnp.maximum(jnp.abs(shift_x), jnp.abs(shift_y)) >= 2.0
            local = local + split_dot(boxes[n * probes : (n + 1) * probes], jnp.where(apart, matrix, 0.0))

    for level in range(extra - 1, -1, -1):
        first_x = (ix >> (level + 1)) * 2
        first_y = (iy >> (level + 1)) * 2
        child_x = (ix >> level) % 2
        child_y = (iy >> level) % 2
        sources = jnp.concatenate(
            [padded[level][first_x + x, first_y + y] for x in range(6) for y in range(6)], axis=1
        )
        rows = pl.ds(pl.multiple_of((1 - child_x) * block, block), length)
        value = split_dot_const(
            sources, pair_ref[0, depth + level, rows], pair_ref[1, depth + level, rows]
        )
        own = jnp.where(child_y > 0, value[:, NODES:], value[:, :NODES])
        if local is not None:
            spread = split_dot_const(local, down_ref[0], down_ref[1])
            near_y = [
                jnp.where(child_y > 0, spread[:, (2 * c + 1) * NODES : (2 * c + 2) * NODES],
                          spread[:, 2 * c * NODES : (2 * c + 1) * NODES])
                for c in range(2)
            ]
            own = own + jnp.where(child_x > 0, near_y[1], near_y[0])
        local = own

    above = local
    for level in range(depth - 1, -1, -1):
        half = side >> (level + 1)
        value = sums[level] + split_dot_const(above, down_ref[0], down_ref[1])
        target = local_ref if level == 0 else locals_ref[level]
        for box in range(half * half):
            for child in range(4):
                target[2 * (box // half) + child // 2, 2 * (box % half) + child % 2] = value[
                    box * probes : (box + 1) * probes, child * NODES : (child + 1) * NODES
                ]
        if level > 0:
            above = jnp.concatenate(
                [target[x, y] for x in range(2 * half) for y in range(2 * half)], axis=0
            )

    receive_halo(0)
    for which in range(depth + 1):
        for n in range(len(steps)):
            pl.when(inside(*steps[n]))(lambda which=which, n=n: halo_copy(n, which).wait_send())
    for copy in along_x + along_y:
        copy.wait_send()


def per_device(offsets, probes, counts):
    count_p, side, _, slots = probes.shape
    depth = side.bit_length() - 1
    extra = 2
    size_x = lax.axis_size("gx")
    size_y = lax.axis_size("gy")
    wide = side + 2
    maps = child_maps().astype(np.float64)
    up = maps.reshape(4 * NODES, NODES)
    down = np.transpose(maps, (2, 0, 1)).reshape(NODES, 4 * NODES)
    nodes = node_table() / 2.0
    node_x = np.broadcast_to(np.repeat(nodes, ORDER), (NODES, NODES))
    node_y = np.broadcast_to(np.tile(nodes, ORDER), (NODES, NODES))
    smem = pl.BlockSpec(memory_space=pltpu.SMEM)
    vmem = pl.BlockSpec(memory_space=pltpu.VMEM)

    def shape(*dims):
        return jax.ShapeDtypeStruct(dims, jnp.float32)

    def scratch(*dims):
        return pltpu.VMEM(dims, jnp.float32)

    window, local, basis, partial = pl.pallas_call(
        functools.partial(tree_kernel, (size_x, size_y), depth, extra),
        out_shape=[
            shape(wide, wide, ROWS, slots),
            shape(side, side, count_p, NODES),
            shape(2, side * side, ORDER, slots),
            shape(side * side, count_p, slots),
        ],
        in_specs=[smem, pl.BlockSpec(memory_space=pl.ANY)] + [vmem] * 5,
        out_specs=[vmem] * 4,
        scratch_shapes=[
            scratch((side >> k) + 4, ((side >> k) + 4) // 2, count_p, 2 * NODES) for k in range(depth)
        ]
        + [scratch(side >> k, side >> k, count_p, NODES) for k in range(depth)]
        + [scratch((size_x >> k) + 4, (size_y >> k) + 4, count_p, NODES) for k in range(extra)]
        + [
            scratch(count_p, NODES),
            scratch(size_x, size_y, count_p, NODES),
            pltpu.VMEM((2, depth + extra, 42 * NODES, 2 * NODES), jnp.bfloat16),
            scratch(side, AUG, slots),
            pltpu.VMEM((side * side, slots, AUG), jnp.bfloat16),
            pltpu.VMEM((side * side, AUG, slots), jnp.bfloat16),
            pltpu.VMEM((side * side, 2 * count_p, slots), jnp.bfloat16),
            scratch(GROUP, slots, slots),
            pltpu.VMEM((GROUP, slots, slots), jnp.bfloat16),
            pltpu.VMEM((GROUP, slots, slots), jnp.bfloat16),
            pltpu.SemaphoreType.DMA((depth + 1, 8)),
            pltpu.SemaphoreType.DMA((depth + 1, 8)),
            pltpu.SemaphoreType.DMA((size_x + size_y - 2,)),
            pltpu.SemaphoreType.DMA((size_x + size_y - 2,)),
            pltpu.SemaphoreType.DMA,
            pltpu.SemaphoreType.DMA((depth + extra,)),
        ],
        compiler_params=pltpu.CompilerParams(collective_id=0, has_side_effects=True),
        name="tree",
    )(
        counts,
        jnp.asarray(pair_tables(depth + extra)),
        jnp.asarray(two_parts(down)),
        jnp.asarray(two_parts(np.concatenate([up, up], axis=1))),
        jnp.asarray(np.stack([node_x, node_x.T, node_y, node_y.T]), jnp.float32),
        offsets,
        probes,
    )
    return pl.pallas_call(
        functools.partial(near_kernel, side),
        out_shape=shape(count_p, side, side, slots),
        in_specs=[vmem] * 4,
        out_specs=vmem,
        scratch_shapes=near_scratch(side, slots, count_p),
        name="near",
    )(window, local, basis, partial)


def solution(mesh):
    placed = (P(None, "gx", "gy", None), P(None, "gx", "gy", None), P("gx", "gy"))
    return jax.shard_map(
        per_device, mesh=mesh, in_specs=placed, out_specs=P(None, "gx", "gy", None), check_vma=False
    )
```

```python
import functools
import math

import jax
import jax.numpy as jnp
import numpy as np
from jax import lax
from jax.experimental import pallas as pl
from jax.experimental.pallas import tpu as pltpu
from jax.sharding import PartitionSpec as P

ORDER = 8
NODES = ORDER * ORDER
ROOT_THREE = 1.7320508075688772
LENGTH_SCALE = 6.0
AMPLITUDE = 1.0 / 96.0
SHORT_AMPLITUDE = 1.0 / 16.0
NUGGET = 0.5
RATIO = 12
UNIT = ROOT_THREE * RATIO / LENGTH_SCALE
FACTOR = AMPLITUDE / RATIO
LOG2_E = 1.4426950408889634
SHORT_SHIFT = math.log2(SHORT_AMPLITUDE / FACTOR)
HIGH = lax.Precision.HIGH
HIGHEST = lax.Precision.HIGHEST
ROWS = 24
AROUND = ((0, 1), (1, 0), (1, 1), (1, -1), (0, -1), (-1, 0), (-1, -1), (-1, 1))
FIRST_STEPS = 2
GROUP = 4
SCALE = UNIT * LOG2_E
AUG = 32


def node_table():
    slots = np.arange(ORDER)
    return np.cos((2.0 * slots + 1.0) * (np.pi / (2.0 * ORDER)))


def series_at_nodes():
    powers = np.arange(ORDER)
    slots = np.arange(ORDER)
    table = np.cos(powers[:, None] * (2.0 * slots[None, :] + 1.0) * (np.pi / (2.0 * ORDER)))
    table = table * (2.0 / ORDER)
    table[0] = 1.0 / ORDER
    return table


SERIES = series_at_nodes()


def interpolation(coords):
    angles = np.arccos(np.clip(coords, -1.0, 1.0))
    series = np.cos(angles[:, None] * np.arange(ORDER))
    return series @ series_at_nodes()


def child_maps():
    nodes = node_table()
    result = []
    for child_x in range(2):
        for child_y in range(2):
            weight_x = interpolation((nodes - 1.0) / 2.0 + child_x)
            weight_y = interpolation((nodes - 1.0) / 2.0 + child_y)
            result.append(
                (weight_x[:, None, :, None] * weight_y[None, :, None, :]).reshape(NODES, NODES)
            )
    return np.stack(result).astype(np.float32)


def matern(dist_sq):
    safe = jnp.maximum(dist_sq, 1e-30)
    scaled = safe * lax.rsqrt(safe)
    decay = jnp.exp2(scaled * (-LOG2_E / RATIO))
    short = jnp.exp2(scaled * -LOG2_E + SHORT_SHIFT)
    return decay * (scaled + RATIO) + short * (scaled + 1.0)


def split(value):
    high = value.astype(jnp.bfloat16)
    return high, (value - high.astype(jnp.float32)).astype(jnp.bfloat16)


def dot(a, b):
    return jnp.dot(a, b, preferred_element_type=jnp.float32)


def split_dot(a, b):
    a_high, a_low = split(a)
    b_high, b_low = split(b)
    return dot(a_high, b_high) + dot(a_high, b_low) + dot(a_low, b_high)


def kernel_of(dist_sq):
    safe = jnp.maximum(dist_sq, 1e-30)
    scaled = safe * lax.rsqrt(safe)
    decay = jnp.exp2(scaled * (-1.0 / RATIO))
    short = jnp.exp2(SHORT_SHIFT - scaled)
    return decay * (scaled + RATIO * LOG2_E) + short * (scaled + LOG2_E)


def three(value):
    first = value.astype(jnp.bfloat16)
    rest = value - first.astype(jnp.float32)
    second = rest.astype(jnp.bfloat16)
    third = (rest - second.astype(jnp.float32)).astype(jnp.bfloat16)
    return [part.astype(jnp.float32) for part in (first, second, third)]


def store_sources(aug_ref, px, py):
    boxes = px.shape[0]
    parts = three(px), three(py), three(px * px + py * py)
    order = [(0, 0), (0, 0), (0, 0), (0, 1), (0, 1), (0, 2)]
    order += [(1, 0), (1, 0), (1, 0), (1, 1), (1, 1), (1, 2), (2, 0), (2, 1), (2, 2)]
    for k, (which, part) in enumerate(order):
        aug_ref[0:boxes, k, :] = parts[which][part]
    for k in range(15, 18):
        aug_ref[0:boxes, k, :] = jnp.ones_like(px)
    for k in range(18, AUG):
        aug_ref[0:boxes, k, :] = jnp.zeros_like(px)


def store_targets(aug_ref, px, py):
    boxes = px.shape[0]
    parts = three(-2.0 * px), three(-2.0 * py), three(px * px + py * py)
    order = [(0, 0), (0, 1), (0, 2), (0, 0), (0, 1), (0, 0)]
    order += [(1, 0), (1, 1), (1, 2), (1, 0), (1, 1), (1, 0)]
    for k, (which, part) in enumerate(order):
        aug_ref[0:boxes, k, :] = parts[which][part]
    for k in range(12, 15):
        aug_ref[0:boxes, k, :] = jnp.ones_like(px)
    for k in range(3):
        aug_ref[0:boxes, 15 + k, :] = parts[2][k]


def sweep(entries, begin, end, cells, buffers):
    rows_ref, probe_ref = cells
    target_ref, g_ref, high_ref, low_ref, result_ref = buffers
    group = len(entries)
    probes = result_ref.shape[1]

    def distances(number, n):
        leaf, cell, _ = entries[n](number)
        return dot(rows_ref[cell], target_ref[leaf])

    def joined(p, multiply, n):
        both = multiply(p, high_ref[n])
        return both[:probes] + both[probes:] + multiply(p[:probes], low_ref[n])

    def products(number, n):
        leaf, cell, back = entries[n](number)
        result = [(leaf, joined(probe_ref[cell], dot, n))]
        if back is not None:
            result.append((back[0], joined(probe_ref[back[1]], dot_rows, n)))
        return result

    high_ref[group - 1] = jnp.zeros_like(high_ref[group - 1])
    low_ref[group - 1] = jnp.zeros_like(low_ref[group - 1])
    for n in range(group):
        g_ref[n] = distances(begin, n)

    def step(number, carry):
        sums = []
        for n in range(group):
            sums += products(number if n else number - 1, (n - 1) % group)
            high, low = split(kernel_of(g_ref[n]))
            high_ref[n] = high
            low_ref[n] = low
            g_ref[n] = distances(number + 1, n)
        for leaf, value in sums:
            result_ref[leaf] += value
        return carry

    lax.fori_loop(begin, end, step, 0)
    for leaf, value in products(end - 1, group - 1):
        result_ref[leaf] += value


def pair_tables(levels):
    nodes = node_table() / 2.0
    node_x = np.repeat(nodes, ORDER)
    node_y = np.tile(nodes, ORDER)
    shift_x = np.arange(7.0) - 3.0
    shift_y = np.arange(6.0)[:, None] - 2.0 - np.arange(2.0)[None, :]
    delta_x = node_x[None, :] - node_x[:, None] - shift_x[:, None, None]
    delta_y = node_y[None, None, None, :] - node_y[None, :, None, None] - shift_y[:, None, :, None]
    apart = np.maximum(np.abs(shift_x)[:, None, None], np.abs(shift_y)[None])
    result = []
    for level in range(levels):
        dist = 2.0**level * np.sqrt(delta_x[:, None, :, None] ** 2 + delta_y[None] ** 2)
        scaled = ROOT_THREE * dist / LENGTH_SCALE
        short = scaled * RATIO
        value = AMPLITUDE * (1.0 + scaled) * np.exp(-scaled)
        value = value + SHORT_AMPLITUDE * (1.0 + short) * np.exp(-short)
        value = np.where(apart[:, :, None, :, None] > 1.5, value, 0.0)
        result.append(value.reshape(42 * NODES, 2 * NODES))
    return two_parts(np.stack(result))


def two_parts(value):
    high = value.astype(np.float32).astype(jnp.bfloat16)
    low = (value - high.astype(np.float64)).astype(np.float32).astype(jnp.bfloat16)
    return np.stack([high, low])


def split_dot_const(a, high, low):
    a_high, a_low = split(a)
    rows = a.shape[0]
    both = dot(jnp.concatenate([a_high, a_low], axis=0), high)
    return both[:rows] + both[rows:] + dot(a_high, low)


def dot_rows(a, b):
    return lax.dot_general(a, b, (((1,), (1,)), ((), ())), preferred_element_type=jnp.float32)


def chebyshev(t):
    terms = [None, t, 2.0 * t * t - 1.0]
    while len(terms) < ORDER:
        terms.append(2.0 * t * terms[-1] - terms[-2])
    values = []
    for m in range(ORDER):
        value = float(SERIES[0, m]) + float(SERIES[1, m]) * t
        for n in range(2, ORDER):
            value = value + float(SERIES[n, m]) * terms[n]
        values.append(value)
    return values


def product_kernel(sizes, depth, extra, count_ref, table_ref, down_ref, up_ref, node_ref, offsets_ref, probes_ref,
                out_ref, *refs):
    size_x, size_y = sizes
    rims, refs = refs[:depth], refs[depth:]
    locals_ref, refs = refs[:depth], refs[depth:]
    padded, refs = refs[:extra], refs[extra:]
    window_ref, local_ref, basis_ref, partial_ref, refs = *refs[:4], refs[4:]
    own_ref, grid_ref, pair_ref, refs = refs[0], refs[1], refs[2], refs[3:]
    aug_ref, rows_ref, target_ref, probe_ref, g_ref, high_ref, low_ref, refs = *refs[:7], refs[7:]
    send_sem, recv_sem, line_send, line_recv, own_sem, pair_sem = refs
    windows = (window_ref, *rims)
    side = probes_ref.shape[1]
    probes = probes_ref.shape[0]
    slots = probes_ref.shape[3]
    ix = lax.axis_index("gx")
    iy = lax.axis_index("gy")
    steps = [(dx, dy) for dx in (-1, 0, 1) for dy in (-1, 0, 1) if (dx, dy) != (0, 0)]

    pair_copies = [
        pltpu.make_async_copy(table_ref.at[:, level], pair_ref.at[:, level], pair_sem.at[level])
        for level in range(depth + extra)
    ]
    for copy in pair_copies:
        copy.start()

    def inside(dx, dy):
        x = ix + dx
        y = iy + dy
        return (x >= 0) & (x < size_x) & (y >= 0) & (y < size_y)

    for window in windows:
        window[...] = jnp.zeros_like(window)

    barrier = pltpu.get_barrier_semaphore()

    def greet(x, y):
        pl.semaphore_signal(barrier, inc=1, device_id=(x, y), device_id_type=pl.DeviceIdType.MESH)

    for k in range(1, size_x):
        greet(lax.rem(ix + k, size_x), iy)
    for k in range(1, size_y):
        greet(ix, lax.rem(iy + k, size_y))
    for dx, dy in steps:
        if dx and dy:
            pl.when(inside(dx, dy))(lambda dx=dx, dy=dy: greet(ix + dx, iy + dy))

    lane = lax.broadcasted_iota(jnp.int32, (1, slots), 1)
    for i in range(side):
        for j in range(side):
            count = count_ref[i, j]
            window_ref[i + 1, j + 1, 0:probes, :] = jnp.where(lane < count, probes_ref[:, i, j, :], 0.0)
            window_ref[i + 1, j + 1, probes : probes + 2, :] = offsets_ref[:, i, j, :]
            window_ref[i + 1, j + 1, probes + 2 : ROWS, :] = jnp.full(
                (ROWS - probes - 2, slots), count.astype(jnp.float32)
            )

    sides_x = jnp.minimum(ix, 1) + jnp.minimum(size_x - 1 - ix, 1)
    sides_y = jnp.minimum(iy, 1) + jnp.minimum(size_y - 1 - iy, 1)
    pl.semaphore_wait(barrier, size_x + size_y - 2 + sides_x * sides_y)

    def pieces(step, inner, width):
        if step > 0:
            return pl.ds(inner, width), pl.ds(0, width)
        if step < 0:
            return pl.ds(width, width), pl.ds(width + inner, width)
        return pl.ds(width, inner), pl.ds(width, inner)

    def halo_copy(n, which):
        dx, dy = steps[n]
        window = windows[which]
        wide_x, wide_y = (1, 1) if which == 0 else (2, 1)
        from_x, to_x = pieces(dx, window.shape[0] - 2 * wide_x, wide_x)
        from_y, to_y = pieces(dy, window.shape[1] - 2 * wide_y, wide_y)
        return pltpu.make_async_remote_copy(
            src_ref=window.at[from_x, from_y],
            dst_ref=window.at[to_x, to_y],
            send_sem=send_sem.at[which, n],
            recv_sem=recv_sem.at[which, n],
            device_id=(ix + dx, iy + dy),
            device_id_type=pl.DeviceIdType.MESH,
        )

    def send_halo(which):
        for n in range(len(steps)):
            pl.when(inside(*steps[n]))(lambda n=n: halo_copy(n, which).start())

    def receive_halo(which):
        for n in range(len(steps)):
            dx, dy = steps[n]
            pl.when(inside(-dx, -dy))(lambda n=n: halo_copy(n, which).wait_recv())


    for i in range(side):
        for axis in range(2):
            values = chebyshev(2.0 * offsets_ref[axis, i] - 1.0)
            for m in range(ORDER):
                basis_ref[axis, i * side : (i + 1) * side, m, :] = values[m]
    for i in range(side):
        for j in range(0, side, 2):
            pair = []
            for y in (j, j + 1):
                base_x = basis_ref[0, i * side + y]
                base_y = basis_ref[1, i * side + y]
                weights = jnp.concatenate([base_x[m : m + 1] * base_y for m in range(ORDER)], axis=0)
                w_high, w_low = split(weights)
                m_high, m_low = split(window_ref[i + 1, y + 1, 0:probes, :])
                both = dot_rows(jnp.concatenate([m_high, m_low], axis=0), w_high)
                pair.append(both[:probes] + both[probes:] + dot_rows(m_high, w_low))
            rims[0][2 + i, 1 + j // 2] = jnp.concatenate(pair, axis=1)

    for level in range(1, depth + 1):
        boxes = side >> level
        rim_ref = rims[level - 1]
        children = jnp.concatenate(
            [
                jnp.concatenate([rim_ref[2 + 2 * x, 1 + y], rim_ref[3 + 2 * x, 1 + y]], axis=1)
                for x in range(boxes)
                for y in range(boxes)
            ],
            axis=0,
        )
        merged = split_dot_const(children, up_ref[0], up_ref[1])
        if level == depth:
            own_ref[...] = merged[:, 0:NODES]
        else:
            low_lanes = lax.broadcasted_iota(jnp.int32, (1, 2 * NODES), 1) < NODES
            for x in range(boxes):
                for y in range(0, boxes, 2):
                    first = (x * boxes + y) * probes
                    rims[level][2 + x, 1 + y // 2] = jnp.where(
                        low_lanes, merged[first : first + probes], merged[first + probes : first + 2 * probes]
                    )

    own_copy = pltpu.make_async_copy(own_ref, grid_ref.at[ix, iy], own_sem)
    own_copy.start()

    def line_copy(slot, source, target, x, y):
        return pltpu.make_async_remote_copy(
            src_ref=source,
            dst_ref=target,
            send_sem=line_send.at[slot],
            recv_sem=line_recv.at[slot],
            device_id=(x, y),
            device_id_type=pl.DeviceIdType.MESH,
        )

    along_x = [
        line_copy(k - 1, own_ref, grid_ref.at[ix, iy], lax.rem(ix + k, size_x), iy)
        for k in range(1, size_x)
    ]
    for copy in along_x:
        copy.start()
    for which in range(depth, 0, -1):
        send_halo(which)

    wide = side + 2
    middle = wide / 2.0

    def place(cells, base, step):
        row = lax.broadcasted_iota(jnp.int32, (cells, 1), 0).astype(jnp.float32)
        return base + step * row - middle

    def prepare(cells):
        for n, (x, y) in enumerate(cells):
            cell = x * wide + y
            rows_ref[cell] = jnp.transpose(aug_ref[n]).astype(jnp.bfloat16)
            p_high, p_low = split(window_ref[x, y, 0:probes, :] * (FACTOR / LOG2_E))
            probe_ref[cell] = jnp.concatenate([p_high, p_low], axis=0)

    for i in range(side):
        px = (offsets_ref[0, i] + (i + 1.0 - middle)) * SCALE
        py = (offsets_ref[1, i] + place(side, 1.0, 1.0)) * SCALE
        store_sources(aug_ref, px, py)
        prepare([(i + 1, j + 1) for j in range(side)])
        store_targets(aug_ref, px, py)
        for j in range(side):
            target_ref[i * side + j] = aug_ref[j].astype(jnp.bfloat16)
    partial_ref[...] = jnp.zeros_like(partial_ref)

    dummy = wide * wide
    rows_ref[dummy] = jnp.zeros_like(rows_ref[dummy])
    probe_ref[dummy] = jnp.zeros_like(probe_ref[dummy])

    def entry(segments, both_ways, stride, first):
        total = sum(length for length, _, _ in segments)

        def at(step):
            number = step * stride + first
            valid = (step >= 0) & (number < total)
            i = j = x = y = jnp.int32(0)
            start = 0
            for length, spot, (da, db) in segments:
                spot_i, spot_j = spot(jnp.maximum(number - start, 0))
                here = number >= start
                i = jnp.where(here, spot_i, i)
                j = jnp.where(here, spot_j, j)
                x = jnp.where(here, spot_i + da, x)
                y = jnp.where(here, spot_j + db, y)
                start += length
            leaf = jnp.where(valid, i * side + j, 0)
            cell = jnp.where(valid, (x + 1) * wide + y + 1, dummy)
            if not both_ways:
                return leaf, cell, None
            other = jnp.where(valid, x * side + y, 0)
            own = jnp.where(valid, (i + 1) * wide + j + 1, dummy)
            return leaf, cell, (other, own)

        return at, total

    def inner_spot(da, db):
        columns = side - abs(db)
        return lambda k: (lax.div(k, columns) + max(-da, 0), lax.rem(k, columns) + max(-db, 0))

    def outer_spot(da, db):
        edge_i = side - 1 if da > 0 else 0
        edge_j = side - 1 if db > 0 else 0
        if da == 0:
            return lambda k: (k, edge_j)
        if db == 0:
            return lambda k: (edge_i, k)
        rest = lambda k: k - side + (0 if edge_i else 1)
        return lambda k: (jnp.where(k < side, edge_i, rest(k)), jnp.where(k < side, k, edge_j))

    def length(da, db):
        return (side - abs(da)) * (side - abs(db))

    alone = [(length(0, 0), inner_spot(0, 0), (0, 0))]
    mutual = [(length(*step), inner_spot(*step), step) for step in AROUND[:4]]
    outer = [(side * side - length(*step), outer_spot(*step), step) for step in AROUND]
    entries = [entry(mutual, True, 3, n)[0] for n in range(3)] + [entry(alone, False, 1, 0)[0]]
    mutual_steps = -(-entry(mutual, True, 1, 0)[1] // 3)
    cells = rows_ref, probe_ref
    buffers = target_ref, g_ref, high_ref, low_ref, partial_ref
    sweep(entries, 0, FIRST_STEPS, cells, buffers)
    for copy in along_x:
        copy.wait_recv()
    own_copy.wait()
    along_y = [
        line_copy(size_x - 1 + k - 1, grid_ref.at[:, iy], grid_ref.at[:, iy], ix, lax.rem(iy + k, size_y))
        for k in range(1, size_y)
    ]
    for copy in along_y:
        copy.start()
    send_halo(0)
    sweep(entries, FIRST_STEPS, mutual_steps, cells, buffers)

    for copy in pair_copies:
        copy.wait()
    block = 6 * NODES
    length = 6 * block
    sums = {}
    for level in range(depth):
        receive_halo(level + 1)
        rim_ref = rims[level]
        half = (rim_ref.shape[0] - 4) // 2
        sources = jnp.concatenate(
            [
                jnp.concatenate([rim_ref[2 * px + x, py + y] for x in range(6) for y in range(3)], axis=1)
                for px in range(half)
                for py in range(half)
            ],
            axis=0,
        )
        matrix = [
            jnp.concatenate(
                [pair_ref[part, level, block : block + length], pair_ref[part, level, 0:length]], axis=1
            )
            for part in range(2)
        ]
        sums[level] = split_dot_const(sources, *matrix)

    for copy in along_y:
        copy.wait_recv()
    for level in range(extra):
        padded[level][...] = jnp.zeros_like(padded[level])
    padded[0][2 : 2 + size_x, 2 : 2 + size_y] = grid_ref[...]

    def merged_boxes(grid, count_x, count_y):
        children = jnp.concatenate(
            [
                jnp.concatenate(
                    [grid[2 + 2 * x + c // 2, 2 + 2 * y + c % 2] for c in range(4)], axis=1
                )
                for x in range(count_x)
                for y in range(count_y)
            ],
            axis=0,
        )
        return split_dot_const(children, up_ref[0], up_ref[1])[:, 0:NODES]

    for level in range(1, extra):
        count_x = size_x >> level
        count_y = size_y >> level
        boxes = merged_boxes(padded[level - 1], count_x, count_y)
        for n in range(count_x * count_y):
            padded[level][2 + n // count_y, 2 + n % count_y] = boxes[n * probes : (n + 1) * probes]

    local = None
    if max(size_x, size_y) > 2 * 2**extra:
        count_x = size_x >> extra
        count_y = size_y >> extra
        boxes = merged_boxes(padded[extra - 1], count_x, count_y)
        box_side = 2.0 ** (depth + extra)
        local = jnp.zeros((probes, NODES), jnp.float32)
        for n in range(count_x * count_y):
            shift_x = (n // count_y - (ix >> extra)).astype(jnp.float32)
            shift_y = (n % count_y - (iy >> extra)).astype(jnp.float32)
            delta_x = (node_ref[0] - node_ref[1] - shift_x) * (box_side * UNIT)
            delta_y = (node_ref[2] - node_ref[3] - shift_y) * (box_side * UNIT)
            matrix = FACTOR * matern(delta_x * delta_x + delta_y * delta_y)
            apart = jnp.maximum(jnp.abs(shift_x), jnp.abs(shift_y)) >= 2.0
            local = local + split_dot(boxes[n * probes : (n + 1) * probes], jnp.where(apart, matrix, 0.0))

    for level in range(extra - 1, -1, -1):
        first_x = (ix >> (level + 1)) * 2
        first_y = (iy >> (level + 1)) * 2
        child_x = (ix >> level) % 2
        child_y = (iy >> level) % 2
        sources = jnp.concatenate(
            [padded[level][first_x + x, first_y + y] for x in range(6) for y in range(6)], axis=1
        )
        rows = pl.ds(pl.multiple_of((1 - child_x) * block, block), length)
        value = split_dot_const(
            sources, pair_ref[0, depth + level, rows], pair_ref[1, depth + level, rows]
        )
        own = jnp.where(child_y > 0, value[:, NODES:], value[:, :NODES])
        if local is not None:
            spread = split_dot_const(local, down_ref[0], down_ref[1])
            near_y = [
                jnp.where(child_y > 0, spread[:, (2 * c + 1) * NODES : (2 * c + 2) * NODES],
                          spread[:, 2 * c * NODES : (2 * c + 1) * NODES])
                for c in range(2)
            ]
            own = own + jnp.where(child_x > 0, near_y[1], near_y[0])
        local = own

    above = local
    for level in range(depth - 1, -1, -1):
        half = side >> (level + 1)
        value = sums[level] + split_dot_const(above, down_ref[0], down_ref[1])
        target = local_ref if level == 0 else locals_ref[level]
        for box in range(half * half):
            for child in range(4):
                target[2 * (box // half) + child // 2, 2 * (box % half) + child % 2] = value[
                    box * probes : (box + 1) * probes, child * NODES : (child + 1) * NODES
                ]
        if level > 0:
            above = jnp.concatenate(
                [target[x, y] for x in range(2 * half) for y in range(2 * half)], axis=0
            )

    receive_halo(0)
    for x in (0, wide - 1):
        px = (window_ref[x, :, probes, :] + (x - middle)) * SCALE
        py = (window_ref[x, :, probes + 1, :] + place(wide, 0.0, 1.0)) * SCALE
        store_sources(aug_ref, px, py)
        prepare([(x, y) for y in range(wide)])
    for y in (0, wide - 1):
        px = (window_ref[1 : side + 1, y, probes, :] + place(side, 1.0, 1.0)) * SCALE
        py = (window_ref[1 : side + 1, y, probes + 1, :] + (y - middle)) * SCALE
        store_sources(aug_ref, px, py)
        prepare([(x, y) for x in range(1, side + 1)])
    rest = [(side * side - mutual_steps, lambda k: inner_spot(0, 0)(k + mutual_steps), (0, 0))]
    rest = outer + (rest if mutual_steps < side * side else [])
    entries = [entry(rest, False, GROUP, n) for n in range(GROUP)]
    sweep([at for at, _ in entries], 0, -(-entries[0][1] // GROUP), cells, buffers)
    for leaf in range(side * side):
        i = leaf // side
        j = leaf % side
        base_x = basis_ref[0, leaf]
        base_y = basis_ref[1, leaf]
        weights = jnp.concatenate([base_x[m : m + 1] * base_y for m in range(ORDER)], axis=0)
        value = split_dot(local_ref[i, j], weights) + partial_ref[leaf]
        value = value + NUGGET * window_ref[i + 1, j + 1, 0:probes, :]
        out_ref[:, i, j, :] = jnp.where(lane < count_ref[i, j], value, 0.0)
    for which in range(depth + 1):
        for n in range(len(steps)):
            pl.when(inside(*steps[n]))(lambda which=which, n=n: halo_copy(n, which).wait_send())
    for copy in along_x + along_y:
        copy.wait_send()


def per_device(offsets, probes, counts):
    count_p, side, _, slots = probes.shape
    depth = side.bit_length() - 1
    extra = 2
    size_x = lax.axis_size("gx")
    size_y = lax.axis_size("gy")
    wide = side + 2
    maps = child_maps().astype(np.float64)
    up = maps.reshape(4 * NODES, NODES)
    down = np.transpose(maps, (2, 0, 1)).reshape(NODES, 4 * NODES)
    nodes = node_table() / 2.0
    node_x = np.broadcast_to(np.repeat(nodes, ORDER), (NODES, NODES))
    node_y = np.broadcast_to(np.tile(nodes, ORDER), (NODES, NODES))
    smem = pl.BlockSpec(memory_space=pltpu.SMEM)
    vmem = pl.BlockSpec(memory_space=pltpu.VMEM)

    def shape(*dims):
        return jax.ShapeDtypeStruct(dims, jnp.float32)

    def scratch(*dims):
        return pltpu.VMEM(dims, jnp.float32)

    return pl.pallas_call(
        functools.partial(product_kernel, (size_x, size_y), depth, extra),
        out_shape=shape(count_p, side, side, slots),
        in_specs=[smem, pl.BlockSpec(memory_space=pl.ANY)] + [vmem] * 5,
        out_specs=vmem,
        scratch_shapes=[
            scratch((side >> k) + 4, ((side >> k) + 4) // 2, count_p, 2 * NODES) for k in range(depth)
        ]
        + [scratch(side >> k, side >> k, count_p, NODES) for k in range(depth)]
        + [scratch((size_x >> k) + 4, (size_y >> k) + 4, count_p, NODES) for k in range(extra)]
        + [
            scratch(wide, wide, ROWS, slots),
            scratch(side, side, count_p, NODES),
            scratch(2, side * side, ORDER, slots),
            scratch(side * side, count_p, slots),
            scratch(count_p, NODES),
            scratch(size_x, size_y, count_p, NODES),
            pltpu.VMEM((2, depth + extra, 42 * NODES, 2 * NODES), jnp.bfloat16),
            scratch(wide, AUG, slots),
            pltpu.VMEM((wide * wide + 1, slots, AUG), jnp.bfloat16),
            pltpu.VMEM((side * side, AUG, slots), jnp.bfloat16),
            pltpu.VMEM((wide * wide + 1, 2 * count_p, slots), jnp.bfloat16),
            scratch(4, slots, slots),
            pltpu.VMEM((4, slots, slots), jnp.bfloat16),
            pltpu.VMEM((4, slots, slots), jnp.bfloat16),
            pltpu.SemaphoreType.DMA((depth + 1, 8)),
            pltpu.SemaphoreType.DMA((depth + 1, 8)),
            pltpu.SemaphoreType.DMA((size_x + size_y - 2,)),
            pltpu.SemaphoreType.DMA((size_x + size_y - 2,)),
            pltpu.SemaphoreType.DMA,
            pltpu.SemaphoreType.DMA((depth + extra,)),
        ],
        compiler_params=pltpu.CompilerParams(collective_id=0, has_side_effects=True),
        name="product",
    )(
        counts,
        jnp.asarray(pair_tables(depth + extra)),
        jnp.asarray(two_parts(down)),
        jnp.asarray(two_parts(np.concatenate([up, up], axis=1))),
        jnp.asarray(np.stack([node_x, node_x.T, node_y, node_y.T]), jnp.float32),
        offsets,
        probes,
    )


def solution(mesh):
    placed = (P(None, "gx", "gy", None), P(None, "gx", "gy", None), P("gx", "gy"))
    return jax.shard_map(
        per_device, mesh=mesh, in_specs=placed, out_specs=P(None, "gx", "gy", None), check_vma=False
    )
```

```python
import functools
import math

import jax
import jax.numpy as jnp
import numpy as np
from jax import lax
from jax.experimental import pallas as pl
from jax.experimental.pallas import tpu as pltpu
from jax.sharding import PartitionSpec as P

ORDER = 8
NODES = ORDER * ORDER
ROOT_THREE = 1.7320508075688772
LENGTH_SCALE = 6.0
AMPLITUDE = 1.0 / 96.0
SHORT_AMPLITUDE = 1.0 / 16.0
NUGGET = 0.5
RATIO = 12
UNIT = ROOT_THREE * RATIO / LENGTH_SCALE
FACTOR = AMPLITUDE / RATIO
LOG2_E = 1.4426950408889634
SHORT_SHIFT = math.log2(SHORT_AMPLITUDE / FACTOR)
HIGH = lax.Precision.HIGH
HIGHEST = lax.Precision.HIGHEST
ROWS = 24
AROUND = ((0, 1), (1, 0), (1, 1), (1, -1), (0, -1), (-1, 0), (-1, -1), (-1, 1))
FIRST_STEPS = 4
SECOND_STEPS = 12
GROUP = 4
SCALE = UNIT * LOG2_E
AUG = 32


def node_table():
    slots = np.arange(ORDER)
    return np.cos((2.0 * slots + 1.0) * (np.pi / (2.0 * ORDER)))


def series_at_nodes():
    powers = np.arange(ORDER)
    slots = np.arange(ORDER)
    table = np.cos(powers[:, None] * (2.0 * slots[None, :] + 1.0) * (np.pi / (2.0 * ORDER)))
    table = table * (2.0 / ORDER)
    table[0] = 1.0 / ORDER
    return table


SERIES = series_at_nodes()


def interpolation(coords):
    angles = np.arccos(np.clip(coords, -1.0, 1.0))
    series = np.cos(angles[:, None] * np.arange(ORDER))
    return series @ series_at_nodes()


def child_maps():
    nodes = node_table()
    result = []
    for child_x in range(2):
        for child_y in range(2):
            weight_x = interpolation((nodes - 1.0) / 2.0 + child_x)
            weight_y = interpolation((nodes - 1.0) / 2.0 + child_y)
            result.append(
                (weight_x[:, None, :, None] * weight_y[None, :, None, :]).reshape(NODES, NODES)
            )
    return np.stack(result).astype(np.float32)


def matern(dist_sq):
    safe = jnp.maximum(dist_sq, 1e-30)
    scaled = safe * lax.rsqrt(safe)
    decay = jnp.exp2(scaled * (-LOG2_E / RATIO))
    short = jnp.exp2(scaled * -LOG2_E + SHORT_SHIFT)
    return decay * (scaled + RATIO) + short * (scaled + 1.0)


def split(value):
    high = value.astype(jnp.bfloat16)
    return high, (value - high.astype(jnp.float32)).astype(jnp.bfloat16)


def dot(a, b):
    return jnp.dot(a, b, preferred_element_type=jnp.float32)


def split_dot(a, b):
    a_high, a_low = split(a)
    b_high, b_low = split(b)
    return dot(a_high, b_high) + dot(a_high, b_low) + dot(a_low, b_high)


def kernel_of(dist_sq):
    safe = jnp.maximum(dist_sq, 1e-30)
    scaled = safe * lax.rsqrt(safe)
    decay = jnp.exp2(scaled * (-1.0 / RATIO))
    short = jnp.exp2(SHORT_SHIFT - scaled)
    return decay * (scaled + RATIO * LOG2_E) + short * (scaled + LOG2_E)


def three(value):
    first = value.astype(jnp.bfloat16)
    rest = value - first.astype(jnp.float32)
    second = rest.astype(jnp.bfloat16)
    third = (rest - second.astype(jnp.float32)).astype(jnp.bfloat16)
    return [part.astype(jnp.float32) for part in (first, second, third)]


def store_sources(aug_ref, px, py):
    boxes = px.shape[0]
    parts = three(px), three(py), three(px * px + py * py)
    order = [(0, 0), (0, 0), (0, 0), (0, 1), (0, 1), (0, 2)]
    order += [(1, 0), (1, 0), (1, 0), (1, 1), (1, 1), (1, 2), (2, 0), (2, 1), (2, 2)]
    for k, (which, part) in enumerate(order):
        aug_ref[0:boxes, k, :] = parts[which][part]
    for k in range(15, 18):
        aug_ref[0:boxes, k, :] = jnp.ones_like(px)
    for k in range(18, AUG):
        aug_ref[0:boxes, k, :] = jnp.zeros_like(px)


def store_targets(aug_ref, px, py):
    boxes = px.shape[0]
    parts = three(-2.0 * px), three(-2.0 * py), three(px * px + py * py)
    order = [(0, 0), (0, 1), (0, 2), (0, 0), (0, 1), (0, 0)]
    order += [(1, 0), (1, 1), (1, 2), (1, 0), (1, 1), (1, 0)]
    for k, (which, part) in enumerate(order):
        aug_ref[0:boxes, k, :] = parts[which][part]
    for k in range(12, 15):
        aug_ref[0:boxes, k, :] = jnp.ones_like(px)
    for k in range(3):
        aug_ref[0:boxes, 15 + k, :] = parts[2][k]


def sweep(entries, begin, end, cells, buffers):
    rows_ref, probe_ref = cells
    target_ref, g_ref, high_ref, low_ref, result_ref = buffers
    group = len(entries)
    probes = result_ref.shape[1]

    def distances(number, n):
        leaf, cell, _ = entries[n](number)
        return dot(rows_ref[cell], target_ref[leaf])

    def joined(p, multiply, n):
        both = multiply(p, high_ref[n])
        return both[:probes] + both[probes:] + multiply(p[:probes], low_ref[n])

    def products(number, n):
        leaf, cell, back = entries[n](number)
        result = [(leaf, joined(probe_ref[cell], dot, n))]
        if back is not None:
            result.append((back[0], joined(probe_ref[back[1]], dot_rows, n)))
        return result

    high_ref[group - 1] = jnp.zeros_like(high_ref[group - 1])
    low_ref[group - 1] = jnp.zeros_like(low_ref[group - 1])
    for n in range(group):
        g_ref[n] = distances(begin, n)

    def step(number, carry):
        sums = []
        for n in range(group):
            sums += products(number if n else number - 1, (n - 1) % group)
            high, low = split(kernel_of(g_ref[n]))
            high_ref[n] = high
            low_ref[n] = low
            g_ref[n] = distances(number + 1, n)
        for leaf, value in sums:
            result_ref[leaf] += value
        return carry

    lax.fori_loop(begin, end, step, 0)
    for leaf, value in products(end - 1, group - 1):
        result_ref[leaf] += value


def pair_tables(levels):
    nodes = node_table() / 2.0
    node_x = np.repeat(nodes, ORDER)
    node_y = np.tile(nodes, ORDER)
    shift_x = np.arange(7.0) - 3.0
    shift_y = np.arange(6.0)[:, None] - 2.0 - np.arange(2.0)[None, :]
    delta_x = node_x[None, :] - node_x[:, None] - shift_x[:, None, None]
    delta_y = node_y[None, None, None, :] - node_y[None, :, None, None] - shift_y[:, None, :, None]
    apart = np.maximum(np.abs(shift_x)[:, None, None], np.abs(shift_y)[None])
    result = []
    for level in range(levels):
        dist = 2.0**level * np.sqrt(delta_x[:, None, :, None] ** 2 + delta_y[None] ** 2)
        scaled = ROOT_THREE * dist / LENGTH_SCALE
        short = scaled * RATIO
        value = AMPLITUDE * (1.0 + scaled) * np.exp(-scaled)
        value = value + SHORT_AMPLITUDE * (1.0 + short) * np.exp(-short)
        value = np.where(apart[:, :, None, :, None] > 1.5, value, 0.0)
        result.append(value.reshape(42 * NODES, 2 * NODES))
    return two_parts(np.stack(result))


def two_parts(value):
    high = value.astype(np.float32).astype(jnp.bfloat16)
    low = (value - high.astype(np.float64)).astype(np.float32).astype(jnp.bfloat16)
    return np.stack([high, low])


def split_dot_const(a, high, low):
    a_high, a_low = split(a)
    rows = a.shape[0]
    both = dot(jnp.concatenate([a_high, a_low], axis=0), high)
    return both[:rows] + both[rows:] + dot(a_high, low)


def dot_rows(a, b):
    return lax.dot_general(a, b, (((1,), (1,)), ((), ())), preferred_element_type=jnp.float32)


def chebyshev(t):
    terms = [None, t, 2.0 * t * t - 1.0]
    while len(terms) < ORDER:
        terms.append(2.0 * t * terms[-1] - terms[-2])
    values = []
    for m in range(ORDER):
        value = float(SERIES[0, m]) + float(SERIES[1, m]) * t
        for n in range(2, ORDER):
            value = value + float(SERIES[n, m]) * terms[n]
        values.append(value)
    return values


def product_kernel(sizes, depth, extra, count_ref, table_ref, down_ref, up_ref, node_ref, offsets_ref, probes_ref,
                out_ref, *refs):
    size_x, size_y = sizes
    rims, refs = refs[:depth], refs[depth:]
    locals_ref, refs = refs[:depth], refs[depth:]
    padded, refs = refs[:extra], refs[extra:]
    window_ref, local_ref, basis_ref, partial_ref, refs = *refs[:4], refs[4:]
    own_ref, grid_ref, pair_ref, refs = refs[0], refs[1], refs[2], refs[3:]
    aug_ref, rows_ref, target_ref, probe_ref, g_ref, high_ref, low_ref, refs = *refs[:7], refs[7:]
    send_sem, recv_sem, line_send, line_recv, own_sem, pair_sem = refs
    windows = (window_ref, *rims)
    side = probes_ref.shape[1]
    probes = probes_ref.shape[0]
    slots = probes_ref.shape[3]
    ix = lax.axis_index("gx")
    iy = lax.axis_index("gy")
    steps = [(dx, dy) for dx in (-1, 0, 1) for dy in (-1, 0, 1) if (dx, dy) != (0, 0)]

    pair_copies = [
        pltpu.make_async_copy(table_ref.at[:, level], pair_ref.at[:, level], pair_sem.at[level])
        for level in range(depth + extra)
    ]
    for copy in pair_copies:
        copy.start()

    def inside(dx, dy):
        x = ix + dx
        y = iy + dy
        return (x >= 0) & (x < size_x) & (y >= 0) & (y < size_y)

    for window in windows:
        window[...] = jnp.zeros_like(window)

    barrier = pltpu.get_barrier_semaphore()

    def greet(x, y):
        pl.semaphore_signal(barrier, inc=1, device_id=(x, y), device_id_type=pl.DeviceIdType.MESH)

    for k in range(1, size_x):
        greet(lax.rem(ix + k, size_x), iy)
    for k in range(1, size_y):
        greet(ix, lax.rem(iy + k, size_y))
    for dx, dy in steps:
        if dx and dy:
            pl.when(inside(dx, dy))(lambda dx=dx, dy=dy: greet(ix + dx, iy + dy))

    lane = lax.broadcasted_iota(jnp.int32, (1, slots), 1)
    for i in range(side):
        for j in range(side):
            count = count_ref[i, j]
            window_ref[i + 1, j + 1, 0:probes, :] = jnp.where(lane < count, probes_ref[:, i, j, :], 0.0)
            window_ref[i + 1, j + 1, probes : probes + 2, :] = offsets_ref[:, i, j, :]
            window_ref[i + 1, j + 1, probes + 2 : ROWS, :] = jnp.full(
                (ROWS - probes - 2, slots), count.astype(jnp.float32)
            )

    def pieces(step, inner, width):
        if step > 0:
            return pl.ds(inner, width), pl.ds(0, width)
        if step < 0:
            return pl.ds(width, width), pl.ds(width + inner, width)
        return pl.ds(width, inner), pl.ds(width, inner)

    def halo_copy(n, which):
        dx, dy = steps[n]
        window = windows[which]
        wide_x, wide_y = (1, 1) if which == 0 else (2, 1)
        from_x, to_x = pieces(dx, window.shape[0] - 2 * wide_x, wide_x)
        from_y, to_y = pieces(dy, window.shape[1] - 2 * wide_y, wide_y)
        return pltpu.make_async_remote_copy(
            src_ref=window.at[from_x, from_y],
            dst_ref=window.at[to_x, to_y],
            send_sem=send_sem.at[which, n],
            recv_sem=recv_sem.at[which, n],
            device_id=(ix + dx, iy + dy),
            device_id_type=pl.DeviceIdType.MESH,
        )

    def send_halo(which):
        for n in range(len(steps)):
            pl.when(inside(*steps[n]))(lambda n=n: halo_copy(n, which).start())

    def receive_halo(which):
        for n in range(len(steps)):
            dx, dy = steps[n]
            pl.when(inside(-dx, -dy))(lambda n=n: halo_copy(n, which).wait_recv())


    for i in range(side):
        for axis in range(2):
            values = chebyshev(2.0 * offsets_ref[axis, i] - 1.0)
            for m in range(ORDER):
                basis_ref[axis, i * side : (i + 1) * side, m, :] = values[m]
    for i in range(side):
        for j in range(0, side, 2):
            pair = []
            for y in (j, j + 1):
                base_x = basis_ref[0, i * side + y]
                base_y = basis_ref[1, i * side + y]
                weights = jnp.concatenate([base_x[m : m + 1] * base_y for m in range(ORDER)], axis=0)
                w_high, w_low = split(weights)
                m_high, m_low = split(window_ref[i + 1, y + 1, 0:probes, :])
                both = dot_rows(jnp.concatenate([m_high, m_low], axis=0), w_high)
                pair.append(both[:probes] + both[probes:] + dot_rows(m_high, w_low))
            rims[0][2 + i, 1 + j // 2] = jnp.concatenate(pair, axis=1)

    for level in range(1, depth + 1):
        boxes = side >> level
        rim_ref = rims[level - 1]
        children = jnp.concatenate(
            [
                jnp.concatenate([rim_ref[2 + 2 * x, 1 + y], rim_ref[3 + 2 * x, 1 + y]], axis=1)
                for x in range(boxes)
                for y in range(boxes)
            ],
            axis=0,
        )
        merged = split_dot_const(children, up_ref[0], up_ref[1])
        if level == depth:
            own_ref[...] = merged[:, 0:NODES]
        else:
            low_lanes = lax.broadcasted_iota(jnp.int32, (1, 2 * NODES), 1) < NODES
            for x in range(boxes):
                for y in range(0, boxes, 2):
                    first = (x * boxes + y) * probes
                    rims[level][2 + x, 1 + y // 2] = jnp.where(
                        low_lanes, merged[first : first + probes], merged[first + probes : first + 2 * probes]
                    )

    wide = side + 2
    middle = wide / 2.0

    def place(cells, base, step):
        row = lax.broadcasted_iota(jnp.int32, (cells, 1), 0).astype(jnp.float32)
        return base + step * row - middle

    def prepare(cells):
        for n, (x, y) in enumerate(cells):
            cell = x * wide + y
            rows_ref[cell] = jnp.transpose(aug_ref[n]).astype(jnp.bfloat16)
            p_high, p_low = split(window_ref[x, y, 0:probes, :] * (FACTOR / LOG2_E))
            probe_ref[cell] = jnp.concatenate([p_high, p_low], axis=0)

    for i in range(side):
        px = (offsets_ref[0, i] + (i + 1.0 - middle)) * SCALE
        py = (offsets_ref[1, i] + place(side, 1.0, 1.0)) * SCALE
        store_sources(aug_ref, px, py)
        prepare([(i + 1, j + 1) for j in range(side)])
        store_targets(aug_ref, px, py)
        for j in range(side):
            target_ref[i * side + j] = aug_ref[j].astype(jnp.bfloat16)
    partial_ref[...] = jnp.zeros_like(partial_ref)

    dummy = wide * wide
    rows_ref[dummy] = jnp.zeros_like(rows_ref[dummy])
    probe_ref[dummy] = jnp.zeros_like(probe_ref[dummy])

    def entry(segments, both_ways, stride, first):
        total = sum(length for length, _, _ in segments)

        def at(step):
            number = step * stride + first
            valid = (step >= 0) & (number < total)
            i = j = x = y = jnp.int32(0)
            start = 0
            for length, spot, (da, db) in segments:
                spot_i, spot_j = spot(jnp.maximum(number - start, 0))
                here = number >= start
                i = jnp.where(here, spot_i, i)
                j = jnp.where(here, spot_j, j)
                x = jnp.where(here, spot_i + da, x)
                y = jnp.where(here, spot_j + db, y)
                start += length
            leaf = jnp.where(valid, i * side + j, 0)
            cell = jnp.where(valid, (x + 1) * wide + y + 1, dummy)
            if not both_ways:
                return leaf, cell, None
            other = jnp.where(valid, x * side + y, 0)
            own = jnp.where(valid, (i + 1) * wide + j + 1, dummy)
            return leaf, cell, (other, own)

        return at, total

    def inner_spot(da, db):
        columns = side - abs(db)
        return lambda k: (lax.div(k, columns) + max(-da, 0), lax.rem(k, columns) + max(-db, 0))

    def outer_spot(da, db):
        edge_i = side - 1 if da > 0 else 0
        edge_j = side - 1 if db > 0 else 0
        if da == 0:
            return lambda k: (k, edge_j)
        if db == 0:
            return lambda k: (edge_i, k)
        rest = lambda k: k - side + (0 if edge_i else 1)
        return lambda k: (jnp.where(k < side, edge_i, rest(k)), jnp.where(k < side, k, edge_j))

    def length(da, db):
        return (side - abs(da)) * (side - abs(db))

    alone = [(length(0, 0), inner_spot(0, 0), (0, 0))]
    mutual = [(length(*step), inner_spot(*step), step) for step in AROUND[:4]]
    outer = [(side * side - length(*step), outer_spot(*step), step) for step in AROUND]
    entries = [entry(mutual, True, 3, n)[0] for n in range(3)] + [entry(alone, False, 1, 0)[0]]
    mutual_steps = -(-entry(mutual, True, 1, 0)[1] // 3)
    cells = rows_ref, probe_ref
    buffers = target_ref, g_ref, high_ref, low_ref, partial_ref
    sweep(entries, 0, FIRST_STEPS, cells, buffers)

    sides_x = jnp.minimum(ix, 1) + jnp.minimum(size_x - 1 - ix, 1)
    sides_y = jnp.minimum(iy, 1) + jnp.minimum(size_y - 1 - iy, 1)
    pl.semaphore_wait(barrier, size_x + size_y - 2 + sides_x * sides_y)

    own_copy = pltpu.make_async_copy(own_ref, grid_ref.at[ix, iy], own_sem)
    own_copy.start()

    def line_copy(slot, source, target, x, y):
        return pltpu.make_async_remote_copy(
            src_ref=source,
            dst_ref=target,
            send_sem=line_send.at[slot],
            recv_sem=line_recv.at[slot],
            device_id=(x, y),
            device_id_type=pl.DeviceIdType.MESH,
        )

    along_x = [
        line_copy(k - 1, own_ref, grid_ref.at[ix, iy], lax.rem(ix + k, size_x), iy)
        for k in range(1, size_x)
    ]
    for copy in along_x:
        copy.start()
    send_halo(0)
    for which in range(depth, 0, -1):
        send_halo(which)

    sweep(entries, FIRST_STEPS, SECOND_STEPS, cells, buffers)
    for copy in along_x:
        copy.wait_recv()
    own_copy.wait()
    along_y = [
        line_copy(size_x - 1 + k - 1, grid_ref.at[:, iy], grid_ref.at[:, iy], ix, lax.rem(iy + k, size_y))
        for k in range(1, size_y)
    ]
    for copy in along_y:
        copy.start()
    sweep(entries, SECOND_STEPS, mutual_steps, cells, buffers)

    receive_halo(0)
    for x in (0, wide - 1):
        px = (window_ref[x, :, probes, :] + (x - middle)) * SCALE
        py = (window_ref[x, :, probes + 1, :] + place(wide, 0.0, 1.0)) * SCALE
        store_sources(aug_ref, px, py)
        prepare([(x, y) for y in range(wide)])
    for y in (0, wide - 1):
        px = (window_ref[1 : side + 1, y, probes, :] + place(side, 1.0, 1.0)) * SCALE
        py = (window_ref[1 : side + 1, y, probes + 1, :] + (y - middle)) * SCALE
        store_sources(aug_ref, px, py)
        prepare([(x, y) for x in range(1, side + 1)])
    rest = [(side * side - mutual_steps, lambda k: inner_spot(0, 0)(k + mutual_steps), (0, 0))]
    rest = outer + (rest if mutual_steps < side * side else [])
    entries = [entry(rest, False, GROUP, n) for n in range(GROUP)]
    sweep([at for at, _ in entries], 0, -(-entries[0][1] // GROUP), cells, buffers)

    for copy in pair_copies:
        copy.wait()
    block = 6 * NODES
    length = 6 * block
    sums = {}
    for level in range(depth):
        receive_halo(level + 1)
        rim_ref = rims[level]
        half = (rim_ref.shape[0] - 4) // 2
        sources = jnp.concatenate(
            [
                jnp.concatenate([rim_ref[2 * px + x, py + y] for x in range(6) for y in range(3)], axis=1)
                for px in range(half)
                for py in range(half)
            ],
            axis=0,
        )
        matrix = [
            jnp.concatenate(
                [pair_ref[part, level, block : block + length], pair_ref[part, level, 0:length]], axis=1
            )
            for part in range(2)
        ]
        sums[level] = split_dot_const(sources, *matrix)

    for copy in along_y:
        copy.wait_recv()
    for level in range(extra):
        padded[level][...] = jnp.zeros_like(padded[level])
    padded[0][2 : 2 + size_x, 2 : 2 + size_y] = grid_ref[...]

    def merged_boxes(grid, count_x, count_y):
        children = jnp.concatenate(
            [
                jnp.concatenate(
                    [grid[2 + 2 * x + c // 2, 2 + 2 * y + c % 2] for c in range(4)], axis=1
                )
                for x in range(count_x)
                for y in range(count_y)
            ],
            axis=0,
        )
        return split_dot_const(children, up_ref[0], up_ref[1])[:, 0:NODES]

    for level in range(1, extra):
        count_x = size_x >> level
        count_y = size_y >> level
        boxes = merged_boxes(padded[level - 1], count_x, count_y)
        for n in range(count_x * count_y):
            padded[level][2 + n // count_y, 2 + n % count_y] = boxes[n * probes : (n + 1) * probes]

    local = None
    if max(size_x, size_y) > 2 * 2**extra:
        count_x = size_x >> extra
        count_y = size_y >> extra
        boxes = merged_boxes(padded[extra - 1], count_x, count_y)
        box_side = 2.0 ** (depth + extra)
        local = jnp.zeros((probes, NODES), jnp.float32)
        for n in range(count_x * count_y):
            shift_x = (n // count_y - (ix >> extra)).astype(jnp.float32)
            shift_y = (n % count_y - (iy >> extra)).astype(jnp.float32)
            delta_x = (node_ref[0] - node_ref[1] - shift_x) * (box_side * UNIT)
            delta_y = (node_ref[2] - node_ref[3] - shift_y) * (box_side * UNIT)
            matrix = FACTOR * matern(delta_x * delta_x + delta_y * delta_y)
            apart = jnp.maximum(jnp.abs(shift_x), jnp.abs(shift_y)) >= 2.0
            local = local + split_dot(boxes[n * probes : (n + 1) * probes], jnp.where(apart, matrix, 0.0))

    for level in range(extra - 1, -1, -1):
        first_x = (ix >> (level + 1)) * 2
        first_y = (iy >> (level + 1)) * 2
        child_x = (ix >> level) % 2
        child_y = (iy >> level) % 2
        sources = jnp.concatenate(
            [padded[level][first_x + x, first_y + y] for x in range(6) for y in range(6)], axis=1
        )
        rows = pl.ds(pl.multiple_of((1 - child_x) * block, block), length)
        value = split_dot_const(
            sources, pair_ref[0, depth + level, rows], pair_ref[1, depth + level, rows]
        )
        own = jnp.where(child_y > 0, value[:, NODES:], value[:, :NODES])
        if local is not None:
            spread = split_dot_const(local, down_ref[0], down_ref[1])
            near_y = [
                jnp.where(child_y > 0, spread[:, (2 * c + 1) * NODES : (2 * c + 2) * NODES],
                          spread[:, 2 * c * NODES : (2 * c + 1) * NODES])
                for c in range(2)
            ]
            own = own + jnp.where(child_x > 0, near_y[1], near_y[0])
        local = own

    above = local
    for level in range(depth - 1, -1, -1):
        half = side >> (level + 1)
        value = sums[level] + split_dot_const(above, down_ref[0], down_ref[1])
        target = local_ref if level == 0 else locals_ref[level]
        for box in range(half * half):
            for child in range(4):
                target[2 * (box // half) + child // 2, 2 * (box % half) + child % 2] = value[
                    box * probes : (box + 1) * probes, child * NODES : (child + 1) * NODES
                ]
        if level > 0:
            above = jnp.concatenate(
                [target[x, y] for x in range(2 * half) for y in range(2 * half)], axis=0
            )

    for leaf in range(side * side):
        i = leaf // side
        j = leaf % side
        base_x = basis_ref[0, leaf]
        base_y = basis_ref[1, leaf]
        weights = jnp.concatenate([base_x[m : m + 1] * base_y for m in range(ORDER)], axis=0)
        value = split_dot(local_ref[i, j], weights) + partial_ref[leaf]
        value = value + NUGGET * window_ref[i + 1, j + 1, 0:probes, :]
        out_ref[:, i, j, :] = jnp.where(lane < count_ref[i, j], value, 0.0)
    for which in range(depth + 1):
        for n in range(len(steps)):
            pl.when(inside(*steps[n]))(lambda which=which, n=n: halo_copy(n, which).wait_send())
    for copy in along_x + along_y:
        copy.wait_send()


def per_device(offsets, probes, counts):
    count_p, side, _, slots = probes.shape
    depth = side.bit_length() - 1
    extra = 2
    size_x = lax.axis_size("gx")
    size_y = lax.axis_size("gy")
    wide = side + 2
    maps = child_maps().astype(np.float64)
    up = maps.reshape(4 * NODES, NODES)
    down = np.transpose(maps, (2, 0, 1)).reshape(NODES, 4 * NODES)
    nodes = node_table() / 2.0
    node_x = np.broadcast_to(np.repeat(nodes, ORDER), (NODES, NODES))
    node_y = np.broadcast_to(np.tile(nodes, ORDER), (NODES, NODES))
    smem = pl.BlockSpec(memory_space=pltpu.SMEM)
    vmem = pl.BlockSpec(memory_space=pltpu.VMEM)

    def shape(*dims):
        return jax.ShapeDtypeStruct(dims, jnp.float32)

    def scratch(*dims):
        return pltpu.VMEM(dims, jnp.float32)

    return pl.pallas_call(
        functools.partial(product_kernel, (size_x, size_y), depth, extra),
        out_shape=shape(count_p, side, side, slots),
        in_specs=[smem, pl.BlockSpec(memory_space=pl.ANY)] + [vmem] * 5,
        out_specs=vmem,
        scratch_shapes=[
            scratch((side >> k) + 4, ((side >> k) + 4) // 2, count_p, 2 * NODES) for k in range(depth)
        ]
        + [scratch(side >> k, side >> k, count_p, NODES) for k in range(depth)]
        + [scratch((size_x >> k) + 4, (size_y >> k) + 4, count_p, NODES) for k in range(extra)]
        + [
            scratch(wide, wide, ROWS, slots),
            scratch(side, side, count_p, NODES),
            scratch(2, side * side, ORDER, slots),
            scratch(side * side, count_p, slots),
            scratch(count_p, NODES),
            scratch(size_x, size_y, count_p, NODES),
            pltpu.VMEM((2, depth + extra, 42 * NODES, 2 * NODES), jnp.bfloat16),
            scratch(wide, AUG, slots),
            pltpu.VMEM((wide * wide + 1, slots, AUG), jnp.bfloat16),
            pltpu.VMEM((side * side, AUG, slots), jnp.bfloat16),
            pltpu.VMEM((wide * wide + 1, 2 * count_p, slots), jnp.bfloat16),
            scratch(4, slots, slots),
            pltpu.VMEM((4, slots, slots), jnp.bfloat16),
            pltpu.VMEM((4, slots, slots), jnp.bfloat16),
            pltpu.SemaphoreType.DMA((depth + 1, 8)),
            pltpu.SemaphoreType.DMA((depth + 1, 8)),
            pltpu.SemaphoreType.DMA((size_x + size_y - 2,)),
            pltpu.SemaphoreType.DMA((size_x + size_y - 2,)),
            pltpu.SemaphoreType.DMA,
            pltpu.SemaphoreType.DMA((depth + extra,)),
        ],
        compiler_params=pltpu.CompilerParams(collective_id=0, has_side_effects=True),
        name="product",
    )(
        counts,
        jnp.asarray(pair_tables(depth + extra)),
        jnp.asarray(two_parts(down)),
        jnp.asarray(two_parts(np.concatenate([up, up], axis=1))),
        jnp.asarray(np.stack([node_x, node_x.T, node_y, node_y.T]), jnp.float32),
        offsets,
        probes,
    )


def solution(mesh):
    placed = (P(None, "gx", "gy", None), P(None, "gx", "gy", None), P("gx", "gy"))
    return jax.shard_map(
        per_device, mesh=mesh, in_specs=placed, out_specs=P(None, "gx", "gy", None), check_vma=False
    )
```

```python
import functools
import math

import jax
import jax.numpy as jnp
import numpy as np
from jax import lax
from jax.experimental import pallas as pl
from jax.experimental.pallas import tpu as pltpu
from jax.sharding import PartitionSpec as P

ORDER = 8
NODES = ORDER * ORDER
ROOT_THREE = 1.7320508075688772
LENGTH_SCALE = 6.0
AMPLITUDE = 1.0 / 96.0
SHORT_AMPLITUDE = 1.0 / 16.0
NUGGET = 0.5
RATIO = 12
UNIT = ROOT_THREE * RATIO / LENGTH_SCALE
FACTOR = AMPLITUDE / RATIO
LOG2_E = 1.4426950408889634
SHORT_SHIFT = math.log2(SHORT_AMPLITUDE / FACTOR)
HIGH = lax.Precision.HIGH
HIGHEST = lax.Precision.HIGHEST
ROWS = 24
AROUND = ((0, 1), (1, 0), (1, 1), (1, -1), (0, -1), (-1, 0), (-1, -1), (-1, 1))
FIRST_STEPS = 4
SECOND_STEPS = 12
GROUP = 4
INLINE_STEPS = 4
SCALE = UNIT * LOG2_E
AUG = 32


def node_table():
    slots = np.arange(ORDER)
    return np.cos((2.0 * slots + 1.0) * (np.pi / (2.0 * ORDER)))


def series_at_nodes():
    powers = np.arange(ORDER)
    slots = np.arange(ORDER)
    table = np.cos(powers[:, None] * (2.0 * slots[None, :] + 1.0) * (np.pi / (2.0 * ORDER)))
    table = table * (2.0 / ORDER)
    table[0] = 1.0 / ORDER
    return table


SERIES = series_at_nodes()


def interpolation(coords):
    angles = np.arccos(np.clip(coords, -1.0, 1.0))
    series = np.cos(angles[:, None] * np.arange(ORDER))
    return series @ series_at_nodes()


def child_maps():
    nodes = node_table()
    result = []
    for child_x in range(2):
        for child_y in range(2):
            weight_x = interpolation((nodes - 1.0) / 2.0 + child_x)
            weight_y = interpolation((nodes - 1.0) / 2.0 + child_y)
            result.append(
                (weight_x[:, None, :, None] * weight_y[None, :, None, :]).reshape(NODES, NODES)
            )
    return np.stack(result).astype(np.float32)


def matern(dist_sq):
    safe = jnp.maximum(dist_sq, 1e-30)
    scaled = safe * lax.rsqrt(safe)
    decay = jnp.exp2(scaled * (-LOG2_E / RATIO))
    short = jnp.exp2(scaled * -LOG2_E + SHORT_SHIFT)
    return decay * (scaled + RATIO) + short * (scaled + 1.0)


def split(value):
    high = value.astype(jnp.bfloat16)
    return high, (value - high.astype(jnp.float32)).astype(jnp.bfloat16)


def dot(a, b):
    return jnp.dot(a, b, preferred_element_type=jnp.float32)


def split_dot(a, b):
    a_high, a_low = split(a)
    b_high, b_low = split(b)
    return dot(a_high, b_high) + dot(a_high, b_low) + dot(a_low, b_high)


def kernel_of(dist_sq):
    safe = jnp.maximum(dist_sq, 1e-30)
    scaled = safe * lax.rsqrt(safe)
    decay = jnp.exp2(scaled * (-1.0 / RATIO))
    short = jnp.exp2(SHORT_SHIFT - scaled)
    return decay * (scaled + RATIO * LOG2_E) + short * (scaled + LOG2_E)


def three(value):
    first = value.astype(jnp.bfloat16)
    rest = value - first.astype(jnp.float32)
    second = rest.astype(jnp.bfloat16)
    third = (rest - second.astype(jnp.float32)).astype(jnp.bfloat16)
    return [part.astype(jnp.float32) for part in (first, second, third)]


def store_sources(aug_ref, px, py):
    boxes = px.shape[0]
    parts = three(px), three(py), three(px * px + py * py)
    order = [(0, 0), (0, 0), (0, 0), (0, 1), (0, 1), (0, 2)]
    order += [(1, 0), (1, 0), (1, 0), (1, 1), (1, 1), (1, 2), (2, 0), (2, 1), (2, 2)]
    for k, (which, part) in enumerate(order):
        aug_ref[0:boxes, k, :] = parts[which][part]
    for k in range(15, 18):
        aug_ref[0:boxes, k, :] = jnp.ones_like(px)
    for k in range(18, AUG):
        aug_ref[0:boxes, k, :] = jnp.zeros_like(px)


def store_targets(aug_ref, px, py):
    boxes = px.shape[0]
    parts = three(-2.0 * px), three(-2.0 * py), three(px * px + py * py)
    order = [(0, 0), (0, 1), (0, 2), (0, 0), (0, 1), (0, 0)]
    order += [(1, 0), (1, 1), (1, 2), (1, 0), (1, 1), (1, 0)]
    for k, (which, part) in enumerate(order):
        aug_ref[0:boxes, k, :] = parts[which][part]
    for k in range(12, 15):
        aug_ref[0:boxes, k, :] = jnp.ones_like(px)
    for k in range(3):
        aug_ref[0:boxes, 15 + k, :] = parts[2][k]


def sweep(entries, begin, end, cells, buffers, opens=True, closes=True, beside=None, inline=0):
    rows_ref, probe_ref = cells
    target_ref, g_ref, high_ref, low_ref, result_ref = buffers
    group = len(entries)
    probes = result_ref.shape[1]

    def distances(number, n):
        leaf, cell, _ = entries[n](number)
        return dot(rows_ref[cell], target_ref[leaf])

    def joined(p, multiply, n):
        both = multiply(p, high_ref[n])
        return both[:probes] + both[probes:] + multiply(p[:probes], low_ref[n])

    def products(number, n):
        leaf, cell, back = entries[n](number)
        result = [(leaf, joined(probe_ref[cell], dot, n))]
        if back is not None:
            result.append((back[0], joined(probe_ref[back[1]], dot_rows, n)))
        return result

    if opens:
        high_ref[group - 1] = jnp.zeros_like(high_ref[group - 1])
        low_ref[group - 1] = jnp.zeros_like(low_ref[group - 1])
        for n in range(group):
            g_ref[n] = distances(begin, n)

    def step(number, carry, meanwhile=lambda: None):
        sums = []
        for n in range(group):
            sums += products(number if n else number - 1, (n - 1) % group)
            high, low = split(kernel_of(g_ref[n]))
            high_ref[n] = high
            low_ref[n] = low
            g_ref[n] = distances(number + 1, n)
            meanwhile()
        for leaf, value in sums:
            result_ref[leaf] += value
        return carry

    lax.fori_loop(begin, end - inline, step, 0)
    if beside is not None:
        pieces = beside()
        next(pieces)
        for number in range(end - inline, end):
            step(jnp.int32(number), 0, lambda: next(pieces, None))
        for _ in pieces:
            pass
    if closes:
        for leaf, value in products(end - 1, group - 1):
            result_ref[leaf] += value


def pair_tables(levels):
    nodes = node_table() / 2.0
    node_x = np.repeat(nodes, ORDER)
    node_y = np.tile(nodes, ORDER)
    shift_x = np.arange(7.0) - 3.0
    shift_y = np.arange(6.0)[:, None] - 2.0 - np.arange(2.0)[None, :]
    delta_x = node_x[None, :] - node_x[:, None] - shift_x[:, None, None]
    delta_y = node_y[None, None, None, :] - node_y[None, :, None, None] - shift_y[:, None, :, None]
    apart = np.maximum(np.abs(shift_x)[:, None, None], np.abs(shift_y)[None])
    result = []
    for level in range(levels):
        dist = 2.0**level * np.sqrt(delta_x[:, None, :, None] ** 2 + delta_y[None] ** 2)
        scaled = ROOT_THREE * dist / LENGTH_SCALE
        short = scaled * RATIO
        value = AMPLITUDE * (1.0 + scaled) * np.exp(-scaled)
        value = value + SHORT_AMPLITUDE * (1.0 + short) * np.exp(-short)
        value = np.where(apart[:, :, None, :, None] > 1.5, value, 0.0)
        result.append(value.reshape(42 * NODES, 2 * NODES))
    return two_parts(np.stack(result))


def two_parts(value):
    high = value.astype(np.float32).astype(jnp.bfloat16)
    low = (value - high.astype(np.float64)).astype(np.float32).astype(jnp.bfloat16)
    return np.stack([high, low])


def split_dot_const(a, high, low):
    a_high, a_low = split(a)
    rows = a.shape[0]
    both = dot(jnp.concatenate([a_high, a_low], axis=0), high)
    return both[:rows] + both[rows:] + dot(a_high, low)


def dot_rows(a, b):
    return lax.dot_general(a, b, (((1,), (1,)), ((), ())), preferred_element_type=jnp.float32)


def chebyshev(t):
    terms = [None, t, 2.0 * t * t - 1.0]
    while len(terms) < ORDER:
        terms.append(2.0 * t * terms[-1] - terms[-2])
    values = []
    for m in range(ORDER):
        value = float(SERIES[0, m]) + float(SERIES[1, m]) * t
        for n in range(2, ORDER):
            value = value + float(SERIES[n, m]) * terms[n]
        values.append(value)
    return values


def product_kernel(sizes, depth, extra, count_ref, table_ref, down_ref, up_ref, node_ref, offsets_ref, probes_ref,
                out_ref, *refs):
    size_x, size_y = sizes
    rims, refs = refs[:depth], refs[depth:]
    locals_ref, refs = refs[:depth], refs[depth:]
    padded, refs = refs[:extra], refs[extra:]
    window_ref, local_ref, basis_ref, partial_ref, refs = *refs[:4], refs[4:]
    own_ref, grid_ref, pair_ref, refs = refs[0], refs[1], refs[2], refs[3:]
    aug_ref, rows_ref, target_ref, probe_ref, g_ref, high_ref, low_ref, refs = *refs[:7], refs[7:]
    send_sem, recv_sem, line_send, line_recv, own_sem, pair_sem = refs
    windows = (window_ref, *rims)
    side = probes_ref.shape[1]
    probes = probes_ref.shape[0]
    slots = probes_ref.shape[3]
    ix = lax.axis_index("gx")
    iy = lax.axis_index("gy")
    steps = [(dx, dy) for dx in (-1, 0, 1) for dy in (-1, 0, 1) if (dx, dy) != (0, 0)]

    pair_copies = [
        pltpu.make_async_copy(table_ref.at[:, level], pair_ref.at[:, level], pair_sem.at[level])
        for level in range(depth + extra)
    ]
    for copy in pair_copies:
        copy.start()

    def inside(dx, dy):
        x = ix + dx
        y = iy + dy
        return (x >= 0) & (x < size_x) & (y >= 0) & (y < size_y)

    for window in windows:
        window[...] = jnp.zeros_like(window)

    barrier = pltpu.get_barrier_semaphore()

    def greet(x, y):
        pl.semaphore_signal(barrier, inc=1, device_id=(x, y), device_id_type=pl.DeviceIdType.MESH)

    for k in range(1, size_x):
        greet(lax.rem(ix + k, size_x), iy)
    for k in range(1, size_y):
        greet(ix, lax.rem(iy + k, size_y))
    for dx, dy in steps:
        if dx and dy:
            pl.when(inside(dx, dy))(lambda dx=dx, dy=dy: greet(ix + dx, iy + dy))

    lane = lax.broadcasted_iota(jnp.int32, (1, slots), 1)
    for i in range(side):
        for j in range(side):
            count = count_ref[i, j]
            window_ref[i + 1, j + 1, 0:probes, :] = jnp.where(lane < count, probes_ref[:, i, j, :], 0.0)
            window_ref[i + 1, j + 1, probes : probes + 2, :] = offsets_ref[:, i, j, :]
            window_ref[i + 1, j + 1, probes + 2 : ROWS, :] = jnp.full(
                (ROWS - probes - 2, slots), count.astype(jnp.float32)
            )

    def pieces(step, inner, width):
        if step > 0:
            return pl.ds(inner, width), pl.ds(0, width)
        if step < 0:
            return pl.ds(width, width), pl.ds(width + inner, width)
        return pl.ds(width, inner), pl.ds(width, inner)

    def halo_copy(n, which):
        dx, dy = steps[n]
        window = windows[which]
        wide_x, wide_y = (1, 1) if which == 0 else (2, 1)
        from_x, to_x = pieces(dx, window.shape[0] - 2 * wide_x, wide_x)
        from_y, to_y = pieces(dy, window.shape[1] - 2 * wide_y, wide_y)
        return pltpu.make_async_remote_copy(
            src_ref=window.at[from_x, from_y],
            dst_ref=window.at[to_x, to_y],
            send_sem=send_sem.at[which, n],
            recv_sem=recv_sem.at[which, n],
            device_id=(ix + dx, iy + dy),
            device_id_type=pl.DeviceIdType.MESH,
        )

    def send_halo(which):
        for n in range(len(steps)):
            pl.when(inside(*steps[n]))(lambda n=n: halo_copy(n, which).start())

    def receive_halo(which):
        for n in range(len(steps)):
            dx, dy = steps[n]
            pl.when(inside(-dx, -dy))(lambda n=n: halo_copy(n, which).wait_recv())


    for i in range(side):
        for axis in range(2):
            values = chebyshev(2.0 * offsets_ref[axis, i] - 1.0)
            for m in range(ORDER):
                basis_ref[axis, i * side : (i + 1) * side, m, :] = values[m]
    for i in range(side):
        for j in range(0, side, 2):
            pair = []
            for y in (j, j + 1):
                base_x = basis_ref[0, i * side + y]
                base_y = basis_ref[1, i * side + y]
                weights = jnp.concatenate([base_x[m : m + 1] * base_y for m in range(ORDER)], axis=0)
                w_high, w_low = split(weights)
                m_high, m_low = split(window_ref[i + 1, y + 1, 0:probes, :])
                both = dot_rows(jnp.concatenate([m_high, m_low], axis=0), w_high)
                pair.append(both[:probes] + both[probes:] + dot_rows(m_high, w_low))
            rims[0][2 + i, 1 + j // 2] = jnp.concatenate(pair, axis=1)

    for level in range(1, depth + 1):
        boxes = side >> level
        rim_ref = rims[level - 1]
        children = jnp.concatenate(
            [
                jnp.concatenate([rim_ref[2 + 2 * x, 1 + y], rim_ref[3 + 2 * x, 1 + y]], axis=1)
                for x in range(boxes)
                for y in range(boxes)
            ],
            axis=0,
        )
        merged = split_dot_const(children, up_ref[0], up_ref[1])
        if level == depth:
            own_ref[...] = merged[:, 0:NODES]
        else:
            low_lanes = lax.broadcasted_iota(jnp.int32, (1, 2 * NODES), 1) < NODES
            for x in range(boxes):
                for y in range(0, boxes, 2):
                    first = (x * boxes + y) * probes
                    rims[level][2 + x, 1 + y // 2] = jnp.where(
                        low_lanes, merged[first : first + probes], merged[first + probes : first + 2 * probes]
                    )

    wide = side + 2
    middle = wide / 2.0

    def place(cells, base, step):
        row = lax.broadcasted_iota(jnp.int32, (cells, 1), 0).astype(jnp.float32)
        return base + step * row - middle

    def prepare(cells):
        for n, (x, y) in enumerate(cells):
            cell = x * wide + y
            rows_ref[cell] = jnp.transpose(aug_ref[n]).astype(jnp.bfloat16)
            p_high, p_low = split(window_ref[x, y, 0:probes, :] * (FACTOR / LOG2_E))
            probe_ref[cell] = jnp.concatenate([p_high, p_low], axis=0)

    for i in range(side):
        px = (offsets_ref[0, i] + (i + 1.0 - middle)) * SCALE
        py = (offsets_ref[1, i] + place(side, 1.0, 1.0)) * SCALE
        store_sources(aug_ref, px, py)
        prepare([(i + 1, j + 1) for j in range(side)])
        store_targets(aug_ref, px, py)
        for j in range(side):
            target_ref[i * side + j] = aug_ref[j].astype(jnp.bfloat16)
    partial_ref[...] = jnp.zeros_like(partial_ref)

    dummy = wide * wide
    rows_ref[dummy] = jnp.zeros_like(rows_ref[dummy])
    probe_ref[dummy] = jnp.zeros_like(probe_ref[dummy])

    def entry(segments, both_ways, stride, first):
        total = sum(length for length, _, _ in segments)

        def at(step):
            number = step * stride + first
            valid = (step >= 0) & (number < total)
            i = j = x = y = jnp.int32(0)
            start = 0
            for length, spot, (da, db) in segments:
                spot_i, spot_j = spot(jnp.maximum(number - start, 0))
                here = number >= start
                i = jnp.where(here, spot_i, i)
                j = jnp.where(here, spot_j, j)
                x = jnp.where(here, spot_i + da, x)
                y = jnp.where(here, spot_j + db, y)
                start += length
            leaf = jnp.where(valid, i * side + j, 0)
            cell = jnp.where(valid, (x + 1) * wide + y + 1, dummy)
            if not both_ways:
                return leaf, cell, None
            other = jnp.where(valid, x * side + y, 0)
            own = jnp.where(valid, (i + 1) * wide + j + 1, dummy)
            return leaf, cell, (other, own)

        return at, total

    def inner_spot(da, db):
        columns = side - abs(db)
        return lambda k: (lax.div(k, columns) + max(-da, 0), lax.rem(k, columns) + max(-db, 0))

    def outer_spot(da, db):
        edge_i = side - 1 if da > 0 else 0
        edge_j = side - 1 if db > 0 else 0
        if da == 0:
            return lambda k: (k, edge_j)
        if db == 0:
            return lambda k: (edge_i, k)
        rest = lambda k: k - side + (0 if edge_i else 1)
        return lambda k: (jnp.where(k < side, edge_i, rest(k)), jnp.where(k < side, k, edge_j))

    def length(da, db):
        return (side - abs(da)) * (side - abs(db))

    alone = [(length(0, 0), inner_spot(0, 0), (0, 0))]
    mutual = [(length(*step), inner_spot(*step), step) for step in AROUND[:4]]
    outer = [(side * side - length(*step), outer_spot(*step), step) for step in AROUND]
    entries = [entry(mutual, True, 3, n)[0] for n in range(3)] + [entry(alone, False, 1, 0)[0]]
    mutual_steps = -(-entry(mutual, True, 1, 0)[1] // 3)
    cells = rows_ref, probe_ref
    buffers = target_ref, g_ref, high_ref, low_ref, partial_ref
    sweep(entries, 0, FIRST_STEPS, cells, buffers, closes=False)

    sides_x = jnp.minimum(ix, 1) + jnp.minimum(size_x - 1 - ix, 1)
    sides_y = jnp.minimum(iy, 1) + jnp.minimum(size_y - 1 - iy, 1)
    pl.semaphore_wait(barrier, size_x + size_y - 2 + sides_x * sides_y)

    own_copy = pltpu.make_async_copy(own_ref, grid_ref.at[ix, iy], own_sem)
    own_copy.start()

    def line_copy(slot, source, target, x, y):
        return pltpu.make_async_remote_copy(
            src_ref=source,
            dst_ref=target,
            send_sem=line_send.at[slot],
            recv_sem=line_recv.at[slot],
            device_id=(x, y),
            device_id_type=pl.DeviceIdType.MESH,
        )

    along_x = [
        line_copy(k - 1, own_ref, grid_ref.at[ix, iy], lax.rem(ix + k, size_x), iy)
        for k in range(1, size_x)
    ]
    for copy in along_x:
        copy.start()
    send_halo(0)
    for which in range(depth, 0, -1):
        send_halo(which)

    sweep(entries, FIRST_STEPS, SECOND_STEPS, cells, buffers, opens=False, closes=False)
    for copy in along_x:
        copy.wait_recv()
    own_copy.wait()
    along_y = [
        line_copy(size_x - 1 + k - 1, grid_ref.at[:, iy], grid_ref.at[:, iy], ix, lax.rem(iy + k, size_y))
        for k in range(1, size_y)
    ]
    for copy in along_y:
        copy.start()
    sweep(entries, SECOND_STEPS, mutual_steps, cells, buffers, opens=False)

    receive_halo(0)
    for x in (0, wide - 1):
        px = (window_ref[x, :, probes, :] + (x - middle)) * SCALE
        py = (window_ref[x, :, probes + 1, :] + place(wide, 0.0, 1.0)) * SCALE
        store_sources(aug_ref, px, py)
        prepare([(x, y) for y in range(wide)])
    for y in (0, wide - 1):
        px = (window_ref[1 : side + 1, y, probes, :] + place(side, 1.0, 1.0)) * SCALE
        py = (window_ref[1 : side + 1, y, probes + 1, :] + (y - middle)) * SCALE
        store_sources(aug_ref, px, py)
        prepare([(x, y) for x in range(1, side + 1)])
    def lists():
        for copy in pair_copies:
            copy.wait()
        for level in range(depth):
            receive_halo(level + 1)
        for copy in along_y:
            copy.wait_recv()
        yield
        block = 6 * NODES
        length = 6 * block
        sums = {}
        for level in range(depth):
            rim_ref = rims[level]
            half = (rim_ref.shape[0] - 4) // 2
            sources = jnp.concatenate(
                [
                    jnp.concatenate([rim_ref[2 * px + x, py + y] for x in range(6) for y in range(3)], axis=1)
                    for px in range(half)
                    for py in range(half)
                ],
                axis=0,
            )
            cut = 2 * block if level == 0 else length
            for first in range(0, length, cut):
                matrix = [
                    jnp.concatenate(
                        [
                            pair_ref[part, level, block + first : block + first + cut],
                            pair_ref[part, level, first : first + cut],
                        ],
                        axis=1,
                    )
                    for part in range(2)
                ]
                value = split_dot_const(sources[:, first : first + cut], *matrix)
                sums[level] = sums[level] + value if first else value
                yield

        for level in range(extra):
            padded[level][...] = jnp.zeros_like(padded[level])
        padded[0][2 : 2 + size_x, 2 : 2 + size_y] = grid_ref[...]

        def merged_boxes(grid, count_x, count_y):
            children = jnp.concatenate(
                [
                    jnp.concatenate(
                        [grid[2 + 2 * x + c // 2, 2 + 2 * y + c % 2] for c in range(4)], axis=1
                    )
                    for x in range(count_x)
                    for y in range(count_y)
                ],
                axis=0,
            )
            return split_dot_const(children, up_ref[0], up_ref[1])[:, 0:NODES]

        for level in range(1, extra):
            count_x = size_x >> level
            count_y = size_y >> level
            boxes = merged_boxes(padded[level - 1], count_x, count_y)
            for n in range(count_x * count_y):
                padded[level][2 + n // count_y, 2 + n % count_y] = boxes[n * probes : (n + 1) * probes]
        yield

        local = None
        if max(size_x, size_y) > 2 * 2**extra:
            count_x = size_x >> extra
            count_y = size_y >> extra
            boxes = merged_boxes(padded[extra - 1], count_x, count_y)
            box_side = 2.0 ** (depth + extra)
            local = jnp.zeros((probes, NODES), jnp.float32)
            for n in range(count_x * count_y):
                shift_x = (n // count_y - (ix >> extra)).astype(jnp.float32)
                shift_y = (n % count_y - (iy >> extra)).astype(jnp.float32)
                delta_x = (node_ref[0] - node_ref[1] - shift_x) * (box_side * UNIT)
                delta_y = (node_ref[2] - node_ref[3] - shift_y) * (box_side * UNIT)
                matrix = FACTOR * matern(delta_x * delta_x + delta_y * delta_y)
                apart = jnp.maximum(jnp.abs(shift_x), jnp.abs(shift_y)) >= 2.0
                local = local + split_dot(boxes[n * probes : (n + 1) * probes], jnp.where(apart, matrix, 0.0))

        for level in range(extra - 1, -1, -1):
            first_x = (ix >> (level + 1)) * 2
            first_y = (iy >> (level + 1)) * 2
            child_x = (ix >> level) % 2
            child_y = (iy >> level) % 2
            sources = jnp.concatenate(
                [padded[level][first_x + x, first_y + y] for x in range(6) for y in range(6)], axis=1
            )
            rows = pl.ds(pl.multiple_of((1 - child_x) * block, block), length)
            value = split_dot_const(
                sources, pair_ref[0, depth + level, rows], pair_ref[1, depth + level, rows]
            )
            own = jnp.where(child_y > 0, value[:, NODES:], value[:, :NODES])
            if local is not None:
                spread = split_dot_const(local, down_ref[0], down_ref[1])
                near_y = [
                    jnp.where(child_y > 0, spread[:, (2 * c + 1) * NODES : (2 * c + 2) * NODES],
                              spread[:, 2 * c * NODES : (2 * c + 1) * NODES])
                    for c in range(2)
                ]
                own = own + jnp.where(child_x > 0, near_y[1], near_y[0])
            local = own
            yield

        above = local
        for level in range(depth - 1, -1, -1):
            half = side >> (level + 1)
            value = sums[level] + split_dot_const(above, down_ref[0], down_ref[1])
            target = local_ref if level == 0 else locals_ref[level]
            for box in range(half * half):
                for child in range(4):
                    target[2 * (box // half) + child // 2, 2 * (box % half) + child % 2] = value[
                        box * probes : (box + 1) * probes, child * NODES : (child + 1) * NODES
                    ]
            if level > 0:
                above = jnp.concatenate(
                    [target[x, y] for x in range(2 * half) for y in range(2 * half)], axis=0
                )
            yield

    rest = [(side * side - mutual_steps, lambda k: inner_spot(0, 0)(k + mutual_steps), (0, 0))]
    rest = outer + (rest if mutual_steps < side * side else [])
    entries = [entry(rest, False, GROUP, n) for n in range(GROUP)]
    outer_steps = -(-entries[0][1] // GROUP)
    inline = min(INLINE_STEPS, outer_steps)
    sweep([at for at, _ in entries], 0, outer_steps, cells, buffers, beside=lists, inline=inline)

    for leaf in range(side * side):
        i = leaf // side
        j = leaf % side
        base_x = basis_ref[0, leaf]
        base_y = basis_ref[1, leaf]
        weights = jnp.concatenate([base_x[m : m + 1] * base_y for m in range(ORDER)], axis=0)
        value = split_dot(local_ref[i, j], weights) + partial_ref[leaf]
        value = value + NUGGET * window_ref[i + 1, j + 1, 0:probes, :]
        out_ref[:, i, j, :] = jnp.where(lane < count_ref[i, j], value, 0.0)
    for which in range(depth + 1):
        for n in range(len(steps)):
            pl.when(inside(*steps[n]))(lambda which=which, n=n: halo_copy(n, which).wait_send())
    for copy in along_x + along_y:
        copy.wait_send()


def per_device(offsets, probes, counts):
    count_p, side, _, slots = probes.shape
    depth = side.bit_length() - 1
    extra = 2
    size_x = lax.axis_size("gx")
    size_y = lax.axis_size("gy")
    wide = side + 2
    maps = child_maps().astype(np.float64)
    up = maps.reshape(4 * NODES, NODES)
    down = np.transpose(maps, (2, 0, 1)).reshape(NODES, 4 * NODES)
    nodes = node_table() / 2.0
    node_x = np.broadcast_to(np.repeat(nodes, ORDER), (NODES, NODES))
    node_y = np.broadcast_to(np.tile(nodes, ORDER), (NODES, NODES))
    smem = pl.BlockSpec(memory_space=pltpu.SMEM)
    vmem = pl.BlockSpec(memory_space=pltpu.VMEM)

    def shape(*dims):
        return jax.ShapeDtypeStruct(dims, jnp.float32)

    def scratch(*dims):
        return pltpu.VMEM(dims, jnp.float32)

    return pl.pallas_call(
        functools.partial(product_kernel, (size_x, size_y), depth, extra),
        out_shape=shape(count_p, side, side, slots),
        in_specs=[smem, pl.BlockSpec(memory_space=pl.ANY)] + [vmem] * 5,
        out_specs=vmem,
        scratch_shapes=[
            scratch((side >> k) + 4, ((side >> k) + 4) // 2, count_p, 2 * NODES) for k in range(depth)
        ]
        + [scratch(side >> k, side >> k, count_p, NODES) for k in range(depth)]
        + [scratch((size_x >> k) + 4, (size_y >> k) + 4, count_p, NODES) for k in range(extra)]
        + [
            scratch(wide, wide, ROWS, slots),
            scratch(side, side, count_p, NODES),
            scratch(2, side * side, ORDER, slots),
            scratch(side * side, count_p, slots),
            scratch(count_p, NODES),
            scratch(size_x, size_y, count_p, NODES),
            pltpu.VMEM((2, depth + extra, 42 * NODES, 2 * NODES), jnp.bfloat16),
            scratch(wide, AUG, slots),
            pltpu.VMEM((wide * wide + 1, slots, AUG), jnp.bfloat16),
            pltpu.VMEM((side * side, AUG, slots), jnp.bfloat16),
            pltpu.VMEM((wide * wide + 1, 2 * count_p, slots), jnp.bfloat16),
            scratch(4, slots, slots),
            pltpu.VMEM((4, slots, slots), jnp.bfloat16),
            pltpu.VMEM((4, slots, slots), jnp.bfloat16),
            pltpu.SemaphoreType.DMA((depth + 1, 8)),
            pltpu.SemaphoreType.DMA((depth + 1, 8)),
            pltpu.SemaphoreType.DMA((size_x + size_y - 2,)),
            pltpu.SemaphoreType.DMA((size_x + size_y - 2,)),
            pltpu.SemaphoreType.DMA,
            pltpu.SemaphoreType.DMA((depth + extra,)),
        ],
        compiler_params=pltpu.CompilerParams(collective_id=0, has_side_effects=True),
        name="product",
    )(
        counts,
        jnp.asarray(pair_tables(depth + extra)),
        jnp.asarray(two_parts(down)),
        jnp.asarray(two_parts(np.concatenate([up, up], axis=1))),
        jnp.asarray(np.stack([node_x, node_x.T, node_y, node_y.T]), jnp.float32),
        offsets,
        probes,
    )


def solution(mesh):
    placed = (P(None, "gx", "gy", None), P(None, "gx", "gy", None), P("gx", "gy"))
    return jax.shard_map(
        per_device, mesh=mesh, in_specs=placed, out_specs=P(None, "gx", "gy", None), check_vma=False
    )
```

```python
import functools
import math

import jax
import jax.numpy as jnp
import numpy as np
from jax import lax
from jax.experimental import pallas as pl
from jax.experimental.pallas import tpu as pltpu
from jax.sharding import PartitionSpec as P

ORDER = 8
NODES = ORDER * ORDER
ROOT_THREE = 1.7320508075688772
LENGTH_SCALE = 6.0
AMPLITUDE = 1.0 / 96.0
SHORT_AMPLITUDE = 1.0 / 16.0
NUGGET = 0.5
RATIO = 12
UNIT = ROOT_THREE * RATIO / LENGTH_SCALE
FACTOR = AMPLITUDE / RATIO
LOG2_E = 1.4426950408889634
SHORT_SHIFT = math.log2(SHORT_AMPLITUDE / FACTOR)
HIGH = lax.Precision.HIGH
HIGHEST = lax.Precision.HIGHEST
ROWS = 24
AROUND = ((0, 1), (1, 0), (1, 1), (1, -1), (0, -1), (-1, 0), (-1, -1), (-1, 1))
FIRST_STEPS = 4
SECOND_STEPS = 12
GROUP = 4
INLINE_STEPS = 4
UPWARD_STEPS = 4
RING_STEPS = 1
SCALE = UNIT * LOG2_E
AUG = 32


def node_table():
    slots = np.arange(ORDER)
    return np.cos((2.0 * slots + 1.0) * (np.pi / (2.0 * ORDER)))


def series_at_nodes():
    powers = np.arange(ORDER)
    slots = np.arange(ORDER)
    table = np.cos(powers[:, None] * (2.0 * slots[None, :] + 1.0) * (np.pi / (2.0 * ORDER)))
    table = table * (2.0 / ORDER)
    table[0] = 1.0 / ORDER
    return table


SERIES = series_at_nodes()


def interpolation(coords):
    angles = np.arccos(np.clip(coords, -1.0, 1.0))
    series = np.cos(angles[:, None] * np.arange(ORDER))
    return series @ series_at_nodes()


def child_maps():
    nodes = node_table()
    result = []
    for child_x in range(2):
        for child_y in range(2):
            weight_x = interpolation((nodes - 1.0) / 2.0 + child_x)
            weight_y = interpolation((nodes - 1.0) / 2.0 + child_y)
            result.append(
                (weight_x[:, None, :, None] * weight_y[None, :, None, :]).reshape(NODES, NODES)
            )
    return np.stack(result).astype(np.float32)


def matern(dist_sq):
    safe = jnp.maximum(dist_sq, 1e-30)
    scaled = safe * lax.rsqrt(safe)
    decay = jnp.exp2(scaled * (-LOG2_E / RATIO))
    short = jnp.exp2(scaled * -LOG2_E + SHORT_SHIFT)
    return decay * (scaled + RATIO) + short * (scaled + 1.0)


def split(value):
    high = value.astype(jnp.bfloat16)
    return high, (value - high.astype(jnp.float32)).astype(jnp.bfloat16)


def dot(a, b):
    return jnp.dot(a, b, preferred_element_type=jnp.float32)


def split_dot(a, b):
    a_high, a_low = split(a)
    b_high, b_low = split(b)
    return dot(a_high, b_high) + dot(a_high, b_low) + dot(a_low, b_high)


def kernel_of(dist_sq):
    safe = jnp.maximum(dist_sq, 1e-30)
    scaled = safe * lax.rsqrt(safe)
    decay = jnp.exp2(scaled * (-1.0 / RATIO))
    short = jnp.exp2(SHORT_SHIFT - scaled)
    return decay * (scaled + RATIO * LOG2_E) + short * (scaled + LOG2_E)


def three(value):
    first = value.astype(jnp.bfloat16)
    rest = value - first.astype(jnp.float32)
    second = rest.astype(jnp.bfloat16)
    third = (rest - second.astype(jnp.float32)).astype(jnp.bfloat16)
    return [part.astype(jnp.float32) for part in (first, second, third)]


def store_sources(aug_ref, px, py):
    boxes = px.shape[0]
    parts = three(px), three(py), three(px * px + py * py)
    order = [(0, 0), (0, 0), (0, 0), (0, 1), (0, 1), (0, 2)]
    order += [(1, 0), (1, 0), (1, 0), (1, 1), (1, 1), (1, 2), (2, 0), (2, 1), (2, 2)]
    for k, (which, part) in enumerate(order):
        aug_ref[0:boxes, k, :] = parts[which][part]
    for k in range(15, 18):
        aug_ref[0:boxes, k, :] = jnp.ones_like(px)
    for k in range(18, AUG):
        aug_ref[0:boxes, k, :] = jnp.zeros_like(px)


def store_targets(aug_ref, px, py):
    boxes = px.shape[0]
    parts = three(-2.0 * px), three(-2.0 * py), three(px * px + py * py)
    order = [(0, 0), (0, 1), (0, 2), (0, 0), (0, 1), (0, 0)]
    order += [(1, 0), (1, 1), (1, 2), (1, 0), (1, 1), (1, 0)]
    for k, (which, part) in enumerate(order):
        aug_ref[0:boxes, k, :] = parts[which][part]
    for k in range(12, 15):
        aug_ref[0:boxes, k, :] = jnp.ones_like(px)
    for k in range(3):
        aug_ref[0:boxes, 15 + k, :] = parts[2][k]


def sweep(entries, begin, end, cells, buffers, opens=True, closes=True, beside=None, inline=0):
    rows_ref, probe_ref = cells
    target_ref, g_ref, high_ref, low_ref, result_ref = buffers
    group = len(entries)
    probes = result_ref.shape[1]

    def distances(number, n):
        leaf, cell, _ = entries[n](number)
        return dot(rows_ref[cell], target_ref[leaf])

    def joined(p, multiply, n):
        both = multiply(p, high_ref[n])
        return both[:probes] + both[probes:] + multiply(p[:probes], low_ref[n])

    def products(number, n):
        leaf, cell, back = entries[n](number)
        result = [(leaf, joined(probe_ref[cell], dot, n))]
        if back is not None:
            result.append((back[0], joined(probe_ref[back[1]], dot_rows, n)))
        return result

    if opens:
        high_ref[group - 1] = jnp.zeros_like(high_ref[group - 1])
        low_ref[group - 1] = jnp.zeros_like(low_ref[group - 1])
        for n in range(group):
            g_ref[n] = distances(begin, n)

    def step(number, carry, meanwhile=lambda: None):
        sums = []
        for n in range(group):
            sums += products(number if n else number - 1, (n - 1) % group)
            high, low = split(kernel_of(g_ref[n]))
            high_ref[n] = high
            low_ref[n] = low
            g_ref[n] = distances(number + 1, n)
            meanwhile()
        for leaf, value in sums:
            result_ref[leaf] += value
        return carry

    lax.fori_loop(begin, end - inline, step, 0)
    if beside is not None:
        pieces = beside()
        next(pieces)
        for number in range(end - inline, end):
            step(jnp.int32(number), 0, lambda: next(pieces, None))
        for _ in pieces:
            pass
    if closes:
        for leaf, value in products(end - 1, group - 1):
            result_ref[leaf] += value


def pair_tables(levels):
    nodes = node_table() / 2.0
    node_x = np.repeat(nodes, ORDER)
    node_y = np.tile(nodes, ORDER)
    shift_x = np.arange(7.0) - 3.0
    shift_y = np.arange(6.0)[:, None] - 2.0 - np.arange(2.0)[None, :]
    delta_x = node_x[None, :] - node_x[:, None] - shift_x[:, None, None]
    delta_y = node_y[None, None, None, :] - node_y[None, :, None, None] - shift_y[:, None, :, None]
    apart = np.maximum(np.abs(shift_x)[:, None, None], np.abs(shift_y)[None])
    result = []
    for level in range(levels):
        dist = 2.0**level * np.sqrt(delta_x[:, None, :, None] ** 2 + delta_y[None] ** 2)
        scaled = ROOT_THREE * dist / LENGTH_SCALE
        short = scaled * RATIO
        value = AMPLITUDE * (1.0 + scaled) * np.exp(-scaled)
        value = value + SHORT_AMPLITUDE * (1.0 + short) * np.exp(-short)
        value = np.where(apart[:, :, None, :, None] > 1.5, value, 0.0)
        result.append(value.reshape(42 * NODES, 2 * NODES))
    return two_parts(np.stack(result))


def two_parts(value):
    high = value.astype(np.float32).astype(jnp.bfloat16)
    low = (value - high.astype(np.float64)).astype(np.float32).astype(jnp.bfloat16)
    return np.stack([high, low])


def split_dot_const(a, high, low):
    a_high, a_low = split(a)
    rows = a.shape[0]
    both = dot(jnp.concatenate([a_high, a_low], axis=0), high)
    return both[:rows] + both[rows:] + dot(a_high, low)


def dot_rows(a, b):
    return lax.dot_general(a, b, (((1,), (1,)), ((), ())), preferred_element_type=jnp.float32)


def chebyshev(t):
    terms = [None, t, 2.0 * t * t - 1.0]
    while len(terms) < ORDER:
        terms.append(2.0 * t * terms[-1] - terms[-2])
    values = []
    for m in range(ORDER):
        value = float(SERIES[0, m]) + float(SERIES[1, m]) * t
        for n in range(2, ORDER):
            value = value + float(SERIES[n, m]) * terms[n]
        values.append(value)
    return values


def product_kernel(sizes, depth, extra, count_ref, table_ref, down_ref, up_ref, node_ref, offsets_ref, probes_ref,
                out_ref, *refs):
    size_x, size_y = sizes
    rims, refs = refs[:depth], refs[depth:]
    locals_ref, refs = refs[:depth], refs[depth:]
    padded, refs = refs[:extra], refs[extra:]
    window_ref, local_ref, basis_ref, partial_ref, refs = *refs[:4], refs[4:]
    own_ref, grid_ref, pair_ref, refs = refs[0], refs[1], refs[2], refs[3:]
    aug_ref, rows_ref, target_ref, probe_ref, g_ref, high_ref, low_ref, refs = *refs[:7], refs[7:]
    send_sem, recv_sem, line_send, line_recv, own_sem, pair_sem = refs
    windows = (window_ref, *rims)
    side = probes_ref.shape[1]
    probes = probes_ref.shape[0]
    slots = probes_ref.shape[3]
    ix = lax.axis_index("gx")
    iy = lax.axis_index("gy")
    steps = [(dx, dy) for dx in (-1, 0, 1) for dy in (-1, 0, 1) if (dx, dy) != (0, 0)]

    pair_copies = [
        pltpu.make_async_copy(table_ref.at[:, level], pair_ref.at[:, level], pair_sem.at[level])
        for level in range(depth + extra)
    ]
    for copy in pair_copies:
        copy.start()

    def inside(dx, dy):
        x = ix + dx
        y = iy + dy
        return (x >= 0) & (x < size_x) & (y >= 0) & (y < size_y)

    for window in windows:
        window[...] = jnp.zeros_like(window)

    barrier = pltpu.get_barrier_semaphore()

    def greet(x, y):
        pl.semaphore_signal(barrier, inc=1, device_id=(x, y), device_id_type=pl.DeviceIdType.MESH)

    for k in range(1, size_x):
        greet(lax.rem(ix + k, size_x), iy)
    for k in range(1, size_y):
        greet(ix, lax.rem(iy + k, size_y))
    for dx, dy in steps:
        if dx and dy:
            pl.when(inside(dx, dy))(lambda dx=dx, dy=dy: greet(ix + dx, iy + dy))

    lane = lax.broadcasted_iota(jnp.int32, (1, slots), 1)
    for i in range(side):
        for j in range(side):
            count = count_ref[i, j]
            window_ref[i + 1, j + 1, 0:probes, :] = jnp.where(lane < count, probes_ref[:, i, j, :], 0.0)
            window_ref[i + 1, j + 1, probes : probes + 2, :] = offsets_ref[:, i, j, :]
            window_ref[i + 1, j + 1, probes + 2 : ROWS, :] = jnp.full(
                (ROWS - probes - 2, slots), count.astype(jnp.float32)
            )

    def pieces(step, inner, width):
        if step > 0:
            return pl.ds(inner, width), pl.ds(0, width)
        if step < 0:
            return pl.ds(width, width), pl.ds(width + inner, width)
        return pl.ds(width, inner), pl.ds(width, inner)

    def halo_copy(n, which):
        dx, dy = steps[n]
        window = windows[which]
        wide_x, wide_y = (1, 1) if which == 0 else (2, 1)
        from_x, to_x = pieces(dx, window.shape[0] - 2 * wide_x, wide_x)
        from_y, to_y = pieces(dy, window.shape[1] - 2 * wide_y, wide_y)
        return pltpu.make_async_remote_copy(
            src_ref=window.at[from_x, from_y],
            dst_ref=window.at[to_x, to_y],
            send_sem=send_sem.at[which, n],
            recv_sem=recv_sem.at[which, n],
            device_id=(ix + dx, iy + dy),
            device_id_type=pl.DeviceIdType.MESH,
        )

    def send_halo(which):
        for n in range(len(steps)):
            pl.when(inside(*steps[n]))(lambda n=n: halo_copy(n, which).start())

    def receive_halo(which):
        for n in range(len(steps)):
            dx, dy = steps[n]
            pl.when(inside(-dx, -dy))(lambda n=n: halo_copy(n, which).wait_recv())


    wide = side + 2
    middle = wide / 2.0

    def place(cells, base, step):
        row = lax.broadcasted_iota(jnp.int32, (cells, 1), 0).astype(jnp.float32)
        return base + step * row - middle

    def prepare(cells):
        for n, (x, y) in enumerate(cells):
            cell = x * wide + y
            rows_ref[cell] = jnp.transpose(aug_ref[n]).astype(jnp.bfloat16)
            p_high, p_low = split(window_ref[x, y, 0:probes, :] * (FACTOR / LOG2_E))
            probe_ref[cell] = jnp.concatenate([p_high, p_low], axis=0)

    for i in range(side):
        px = (offsets_ref[0, i] + (i + 1.0 - middle)) * SCALE
        py = (offsets_ref[1, i] + place(side, 1.0, 1.0)) * SCALE
        store_sources(aug_ref, px, py)
        prepare([(i + 1, j + 1) for j in range(side)])
        store_targets(aug_ref, px, py)
        for j in range(side):
            target_ref[i * side + j] = aug_ref[j].astype(jnp.bfloat16)
    partial_ref[...] = jnp.zeros_like(partial_ref)

    dummy = wide * wide
    rows_ref[dummy] = jnp.zeros_like(rows_ref[dummy])
    probe_ref[dummy] = jnp.zeros_like(probe_ref[dummy])

    def entry(segments, both_ways, stride, first):
        total = sum(length for length, _, _ in segments)

        def at(step):
            number = step * stride + first
            valid = (step >= 0) & (number < total)
            i = j = x = y = jnp.int32(0)
            start = 0
            for length, spot, (da, db) in segments:
                spot_i, spot_j = spot(jnp.maximum(number - start, 0))
                here = number >= start
                i = jnp.where(here, spot_i, i)
                j = jnp.where(here, spot_j, j)
                x = jnp.where(here, spot_i + da, x)
                y = jnp.where(here, spot_j + db, y)
                start += length
            leaf = jnp.where(valid, i * side + j, 0)
            cell = jnp.where(valid, (x + 1) * wide + y + 1, dummy)
            if not both_ways:
                return leaf, cell, None
            other = jnp.where(valid, x * side + y, 0)
            own = jnp.where(valid, (i + 1) * wide + j + 1, dummy)
            return leaf, cell, (other, own)

        return at, total

    def inner_spot(da, db):
        columns = side - abs(db)
        return lambda k: (lax.div(k, columns) + max(-da, 0), lax.rem(k, columns) + max(-db, 0))

    def outer_spot(da, db):
        edge_i = side - 1 if da > 0 else 0
        edge_j = side - 1 if db > 0 else 0
        if da == 0:
            return lambda k: (k, edge_j)
        if db == 0:
            return lambda k: (edge_i, k)
        rest = lambda k: k - side + (0 if edge_i else 1)
        return lambda k: (jnp.where(k < side, edge_i, rest(k)), jnp.where(k < side, k, edge_j))

    def length(da, db):
        return (side - abs(da)) * (side - abs(db))

    alone = [(length(0, 0), inner_spot(0, 0), (0, 0))]
    mutual = [(length(*step), inner_spot(*step), step) for step in AROUND[:4]]
    outer = [(side * side - length(*step), outer_spot(*step), step) for step in AROUND]
    entries = [entry(mutual, True, 3, n)[0] for n in range(3)] + [entry(alone, False, 1, 0)[0]]
    mutual_steps = -(-entry(mutual, True, 1, 0)[1] // 3)
    cells = rows_ref, probe_ref
    buffers = target_ref, g_ref, high_ref, low_ref, partial_ref
    def upward():
        yield
        for i in range(side):
            for axis in range(2):
                values = chebyshev(2.0 * offsets_ref[axis, i] - 1.0)
                for m in range(ORDER):
                    basis_ref[axis, i * side : (i + 1) * side, m, :] = values[m]
        for i in range(side):
            for j in range(0, side, 2):
                pair = []
                for y in (j, j + 1):
                    base_x = basis_ref[0, i * side + y]
                    base_y = basis_ref[1, i * side + y]
                    weights = jnp.concatenate([base_x[m : m + 1] * base_y for m in range(ORDER)], axis=0)
                    w_high, w_low = split(weights)
                    m_high, m_low = split(window_ref[i + 1, y + 1, 0:probes, :])
                    both = dot_rows(jnp.concatenate([m_high, m_low], axis=0), w_high)
                    pair.append(both[:probes] + both[probes:] + dot_rows(m_high, w_low))
                rims[0][2 + i, 1 + j // 2] = jnp.concatenate(pair, axis=1)
                yield
        for level in range(1, depth + 1):
            boxes = side >> level
            rim_ref = rims[level - 1]
            children = jnp.concatenate(
                [
                    jnp.concatenate([rim_ref[2 + 2 * x, 1 + y], rim_ref[3 + 2 * x, 1 + y]], axis=1)
                    for x in range(boxes)
                    for y in range(boxes)
                ],
                axis=0,
            )
            merged = split_dot_const(children, up_ref[0], up_ref[1])
            if level == depth:
                own_ref[...] = merged[:, 0:NODES]
            else:
                low_lanes = lax.broadcasted_iota(jnp.int32, (1, 2 * NODES), 1) < NODES
                for x in range(boxes):
                    for y in range(0, boxes, 2):
                        first = (x * boxes + y) * probes
                        rims[level][2 + x, 1 + y // 2] = jnp.where(
                            low_lanes, merged[first : first + probes], merged[first + probes : first + 2 * probes]
                        )
            yield

    sweep(entries, 0, FIRST_STEPS, cells, buffers, closes=False, beside=upward, inline=UPWARD_STEPS)

    sides_x = jnp.minimum(ix, 1) + jnp.minimum(size_x - 1 - ix, 1)
    sides_y = jnp.minimum(iy, 1) + jnp.minimum(size_y - 1 - iy, 1)
    pl.semaphore_wait(barrier, size_x + size_y - 2 + sides_x * sides_y)

    own_copy = pltpu.make_async_copy(own_ref, grid_ref.at[ix, iy], own_sem)
    own_copy.start()

    def line_copy(slot, source, target, x, y):
        return pltpu.make_async_remote_copy(
            src_ref=source,
            dst_ref=target,
            send_sem=line_send.at[slot],
            recv_sem=line_recv.at[slot],
            device_id=(x, y),
            device_id_type=pl.DeviceIdType.MESH,
        )

    along_x = [
        line_copy(k - 1, own_ref, grid_ref.at[ix, iy], lax.rem(ix + k, size_x), iy)
        for k in range(1, size_x)
    ]
    for copy in along_x:
        copy.start()
    send_halo(0)
    for which in range(depth, 0, -1):
        send_halo(which)

    sweep(entries, FIRST_STEPS, SECOND_STEPS, cells, buffers, opens=False, closes=False)
    for copy in along_x:
        copy.wait_recv()
    own_copy.wait()
    along_y = [
        line_copy(size_x - 1 + k - 1, grid_ref.at[:, iy], grid_ref.at[:, iy], ix, lax.rem(iy + k, size_y))
        for k in range(1, size_y)
    ]
    for copy in along_y:
        copy.start()
    def ring():
        receive_halo(0)
        yield
        for x in (0, wide - 1):
            px = (window_ref[x, :, probes, :] + (x - middle)) * SCALE
            py = (window_ref[x, :, probes + 1, :] + place(wide, 0.0, 1.0)) * SCALE
            store_sources(aug_ref, px, py)
            prepare([(x, y) for y in range(wide)])
            yield
        for y in (0, wide - 1):
            px = (window_ref[1 : side + 1, y, probes, :] + place(side, 1.0, 1.0)) * SCALE
            py = (window_ref[1 : side + 1, y, probes + 1, :] + (y - middle)) * SCALE
            store_sources(aug_ref, px, py)
            prepare([(x, y) for x in range(1, side + 1)])
            yield

    sweep(entries, SECOND_STEPS, mutual_steps, cells, buffers, opens=False, beside=ring, inline=RING_STEPS)

    def lists():
        for copy in pair_copies:
            copy.wait()
        for level in range(depth):
            receive_halo(level + 1)
        for copy in along_y:
            copy.wait_recv()
        yield
        block = 6 * NODES
        length = 6 * block
        sums = {}
        for level in range(depth):
            rim_ref = rims[level]
            half = (rim_ref.shape[0] - 4) // 2
            sources = jnp.concatenate(
                [
                    jnp.concatenate([rim_ref[2 * px + x, py + y] for x in range(6) for y in range(3)], axis=1)
                    for px in range(half)
                    for py in range(half)
                ],
                axis=0,
            )
            cut = 2 * block if level == 0 else length
            for first in range(0, length, cut):
                matrix = [
                    jnp.concatenate(
                        [
                            pair_ref[part, level, block + first : block + first + cut],
                            pair_ref[part, level, first : first + cut],
                        ],
                        axis=1,
                    )
                    for part in range(2)
                ]
                value = split_dot_const(sources[:, first : first + cut], *matrix)
                sums[level] = sums[level] + value if first else value
                yield

        for level in range(extra):
            padded[level][...] = jnp.zeros_like(padded[level])
        padded[0][2 : 2 + size_x, 2 : 2 + size_y] = grid_ref[...]

        def merged_boxes(grid, count_x, count_y):
            children = jnp.concatenate(
                [
                    jnp.concatenate(
                        [grid[2 + 2 * x + c // 2, 2 + 2 * y + c % 2] for c in range(4)], axis=1
                    )
                    for x in range(count_x)
                    for y in range(count_y)
                ],
                axis=0,
            )
            return split_dot_const(children, up_ref[0], up_ref[1])[:, 0:NODES]

        for level in range(1, extra):
            count_x = size_x >> level
            count_y = size_y >> level
            boxes = merged_boxes(padded[level - 1], count_x, count_y)
            for n in range(count_x * count_y):
                padded[level][2 + n // count_y, 2 + n % count_y] = boxes[n * probes : (n + 1) * probes]
        yield

        local = None
        if max(size_x, size_y) > 2 * 2**extra:
            count_x = size_x >> extra
            count_y = size_y >> extra
            boxes = merged_boxes(padded[extra - 1], count_x, count_y)
            box_side = 2.0 ** (depth + extra)
            local = jnp.zeros((probes, NODES), jnp.float32)
            for n in range(count_x * count_y):
                shift_x = (n // count_y - (ix >> extra)).astype(jnp.float32)
                shift_y = (n % count_y - (iy >> extra)).astype(jnp.float32)
                delta_x = (node_ref[0] - node_ref[1] - shift_x) * (box_side * UNIT)
                delta_y = (node_ref[2] - node_ref[3] - shift_y) * (box_side * UNIT)
                matrix = FACTOR * matern(delta_x * delta_x + delta_y * delta_y)
                apart = jnp.maximum(jnp.abs(shift_x), jnp.abs(shift_y)) >= 2.0
                local = local + split_dot(boxes[n * probes : (n + 1) * probes], jnp.where(apart, matrix, 0.0))

        for level in range(extra - 1, -1, -1):
            first_x = (ix >> (level + 1)) * 2
            first_y = (iy >> (level + 1)) * 2
            child_x = (ix >> level) % 2
            child_y = (iy >> level) % 2
            sources = jnp.concatenate(
                [padded[level][first_x + x, first_y + y] for x in range(6) for y in range(6)], axis=1
            )
            rows = pl.ds(pl.multiple_of((1 - child_x) * block, block), length)
            value = split_dot_const(
                sources, pair_ref[0, depth + level, rows], pair_ref[1, depth + level, rows]
            )
            own = jnp.where(child_y > 0, value[:, NODES:], value[:, :NODES])
            if local is not None:
                spread = split_dot_const(local, down_ref[0], down_ref[1])
                near_y = [
                    jnp.where(child_y > 0, spread[:, (2 * c + 1) * NODES : (2 * c + 2) * NODES],
                              spread[:, 2 * c * NODES : (2 * c + 1) * NODES])
                    for c in range(2)
                ]
                own = own + jnp.where(child_x > 0, near_y[1], near_y[0])
            local = own
            yield

        above = local
        for level in range(depth - 1, -1, -1):
            half = side >> (level + 1)
            value = sums[level] + split_dot_const(above, down_ref[0], down_ref[1])
            target = local_ref if level == 0 else locals_ref[level]
            for box in range(half * half):
                for child in range(4):
                    target[2 * (box // half) + child // 2, 2 * (box % half) + child % 2] = value[
                        box * probes : (box + 1) * probes, child * NODES : (child + 1) * NODES
                    ]
            if level > 0:
                above = jnp.concatenate(
                    [target[x, y] for x in range(2 * half) for y in range(2 * half)], axis=0
                )
            yield

    rest = [(side * side - mutual_steps, lambda k: inner_spot(0, 0)(k + mutual_steps), (0, 0))]
    rest = outer + (rest if mutual_steps < side * side else [])
    entries = [entry(rest, False, GROUP, n) for n in range(GROUP)]
    outer_steps = -(-entries[0][1] // GROUP)
    inline = min(INLINE_STEPS, outer_steps)
    sweep([at for at, _ in entries], 0, outer_steps, cells, buffers, beside=lists, inline=inline)

    for leaf in range(side * side):
        i = leaf // side
        j = leaf % side
        base_x = basis_ref[0, leaf]
        base_y = basis_ref[1, leaf]
        weights = jnp.concatenate([base_x[m : m + 1] * base_y for m in range(ORDER)], axis=0)
        value = split_dot(local_ref[i, j], weights) + partial_ref[leaf]
        value = value + NUGGET * window_ref[i + 1, j + 1, 0:probes, :]
        out_ref[:, i, j, :] = jnp.where(lane < count_ref[i, j], value, 0.0)
    for which in range(depth + 1):
        for n in range(len(steps)):
            pl.when(inside(*steps[n]))(lambda which=which, n=n: halo_copy(n, which).wait_send())
    for copy in along_x + along_y:
        copy.wait_send()


def per_device(offsets, probes, counts):
    count_p, side, _, slots = probes.shape
    depth = side.bit_length() - 1
    extra = 2
    size_x = lax.axis_size("gx")
    size_y = lax.axis_size("gy")
    wide = side + 2
    maps = child_maps().astype(np.float64)
    up = maps.reshape(4 * NODES, NODES)
    down = np.transpose(maps, (2, 0, 1)).reshape(NODES, 4 * NODES)
    nodes = node_table() / 2.0
    node_x = np.broadcast_to(np.repeat(nodes, ORDER), (NODES, NODES))
    node_y = np.broadcast_to(np.tile(nodes, ORDER), (NODES, NODES))
    smem = pl.BlockSpec(memory_space=pltpu.SMEM)
    vmem = pl.BlockSpec(memory_space=pltpu.VMEM)

    def shape(*dims):
        return jax.ShapeDtypeStruct(dims, jnp.float32)

    def scratch(*dims):
        return pltpu.VMEM(dims, jnp.float32)

    return pl.pallas_call(
        functools.partial(product_kernel, (size_x, size_y), depth, extra),
        out_shape=shape(count_p, side, side, slots),
        in_specs=[smem, pl.BlockSpec(memory_space=pl.ANY)] + [vmem] * 5,
        out_specs=vmem,
        scratch_shapes=[
            scratch((side >> k) + 4, ((side >> k) + 4) // 2, count_p, 2 * NODES) for k in range(depth)
        ]
        + [scratch(side >> k, side >> k, count_p, NODES) for k in range(depth)]
        + [scratch((size_x >> k) + 4, (size_y >> k) + 4, count_p, NODES) for k in range(extra)]
        + [
            scratch(wide, wide, ROWS, slots),
            scratch(side, side, count_p, NODES),
            scratch(2, side * side, ORDER, slots),
            scratch(side * side, count_p, slots),
            scratch(count_p, NODES),
            scratch(size_x, size_y, count_p, NODES),
            pltpu.VMEM((2, depth + extra, 42 * NODES, 2 * NODES), jnp.bfloat16),
            scratch(wide, AUG, slots),
            pltpu.VMEM((wide * wide + 1, slots, AUG), jnp.bfloat16),
            pltpu.VMEM((side * side, AUG, slots), jnp.bfloat16),
            pltpu.VMEM((wide * wide + 1, 2 * count_p, slots), jnp.bfloat16),
            scratch(4, slots, slots),
            pltpu.VMEM((4, slots, slots), jnp.bfloat16),
            pltpu.VMEM((4, slots, slots), jnp.bfloat16),
            pltpu.SemaphoreType.DMA((depth + 1, 8)),
            pltpu.SemaphoreType.DMA((depth + 1, 8)),
            pltpu.SemaphoreType.DMA((size_x + size_y - 2,)),
            pltpu.SemaphoreType.DMA((size_x + size_y - 2,)),
            pltpu.SemaphoreType.DMA,
            pltpu.SemaphoreType.DMA((depth + extra,)),
        ],
        compiler_params=pltpu.CompilerParams(
            collective_id=0, has_side_effects=True, vmem_limit_bytes=48 * 2**20
        ),
        name="product",
    )(
        counts,
        jnp.asarray(pair_tables(depth + extra)),
        jnp.asarray(two_parts(down)),
        jnp.asarray(two_parts(np.concatenate([up, up], axis=1))),
        jnp.asarray(np.stack([node_x, node_x.T, node_y, node_y.T]), jnp.float32),
        offsets,
        probes,
    )


def solution(mesh):
    placed = (P(None, "gx", "gy", None), P(None, "gx", "gy", None), P("gx", "gy"))
    return jax.shard_map(
        per_device, mesh=mesh, in_specs=placed, out_specs=P(None, "gx", "gy", None), check_vma=False
    )
```
